32 devices in a mesh: row: 8 (over y, x, core), col: 4 (over z).
Axes of the slice: x: 2, y: 2, z: 4, core: 2. Of those that a mesh axis runs over, the one named last changes fastest.
Arguments:
- diag_blocks: float32 [16, 512, 512], P('row', None, 'col'), as said below
- near_blocks: float32 [16, 4, 512, 512], P('row', None, None, 'col'), may hold values from -0.1 to 0.1, as said below
- cluster_bases: float32 [16, 512, 512], P('row', 'col'), as said below
- near_ids: int32 [16, 4], P('row'), may hold values from 0 to 15, as said below
- near_count: int32 [16], P('row'), may hold values from 1 to 4
- parent_bases: float32 [8, 512, 512], P('row'), as said below
Outputs:
- leaf_diag: float32 [16, 256, 256], P('row', None, 'col')
- leaf_near: float32 [16, 4, 256, 256], P('row', None, None, 'col')
- parent_diag: float32 [8, 256, 256], P('row', None, 'col')
The draws below stay inside these ranges and needn't reach their ends.
Inputs may be any that keep to these rules, and one draw needn't show every extreme that they name: `near_ids`: slot 0 of cluster i names its sibling: i + 2 when i // 2 is even, else i - 2. The other slots may name any cluster. For sibling clusters a and b = a + 2 (a // 2 even), near_blocks[b, 0] is the transpose of near_blocks[a, 0]. `diag_blocks`: Symmetric. `cluster_bases`: the identity plus a small full-rank perturbation. `parent_bases`: the identity plus a small full-rank perturbation.
All inputs are finite; a program needn't handle non-finite values.
Results may differ from the reference program's by a relative error of at most 0.0003.
Values sent between devices are 32-bit elements; how exact they have to be, the bound alone decides.
No kernel may reach another device: no remote copies, remote signals or barrier semaphores. Data moves between devices by JAX's collectives and lax.ppermute only.
A program may use at most 128 MiB of HBM per device.

```python
import math
import jax
import jax.numpy as jnp
from jax import lax

B = 512
K = 256
NEAR = 4
C_DEV = 2
CLUSTERS = 16
PARENTS = 8
N_ROW = 8


def rough_square(key, count, size):
    return jax.random.normal(key, (count, size, size), jnp.float32)


def draw_diag_blocks(key, part):
    rough = rough_square(jax.random.fold_in(key, 11), CLUSTERS, B)
    symmetric = (rough + jnp.swapaxes(rough, 1, 2)) / math.sqrt(2.0 * B)
    matrix = 3.0 * jnp.eye(B, dtype=jnp.float32)[None] + 0.7 * symmetric
    return matrix


def draw_near_blocks(key, part):
    spread = 0.5 / math.sqrt(B)
    shape = (CLUSTERS, NEAR, B, B)
    values = jnp.clip(spread * jax.random.normal(jax.random.fold_in(key, 51), shape, jnp.float32), -0.1, 0.1)
    indices = jnp.arange(CLUSTERS, dtype=jnp.int32)
    second = indices // C_DEV % 2 == 1
    partner = jnp.where(second, indices - C_DEV, indices)
    mirrored = jnp.swapaxes(values[partner, 0], 1, 2)
    slot_zero = jnp.where(second[:, None, None], mirrored, values[:, 0])
    return values.at[:, 0].set(slot_zero)


def draw_cluster_bases(key, part):
    rough = rough_square(jax.random.fold_in(key, 21), CLUSTERS, B)
    return jnp.eye(B, dtype=jnp.float32)[None] + 0.35 * rough / math.sqrt(B)


def draw_parent_bases(key, part):
    rough = rough_square(jax.random.fold_in(key, 31), PARENTS, 2 * K)
    return jnp.eye(2 * K, dtype=jnp.float32)[None] + 0.35 * rough / math.sqrt(2 * K)


def draw_near_ids(key, part):
    indices = jnp.arange(CLUSTERS, dtype=jnp.int32)
    sibling = jnp.where(indices // C_DEV % 2 == 0, indices + C_DEV, indices - C_DEV)
    others = jax.random.randint(jax.random.fold_in(key, 41), (CLUSTERS, NEAR - 1), 0, CLUSTERS, jnp.int32)
    return jnp.concatenate([sibling[:, None], others], axis=1)


def plant(result, stream_key, smallest, top_value):
    index_at = [jax.random.randint(jax.random.fold_in(stream_key, axis), (), 0, length) for axis, length in enumerate(result.shape)]
    longest = result.shape.index(max(result.shape))
    next_to = index_at[:longest] + [(index_at[longest] + 1) % result.shape[longest]] + index_at[longest + 1:]
    return result.at[tuple(index_at)].set(smallest).at[tuple(next_to)].set(top_value)


def setup_inputs(seed: int = 0) -> dict:
    arg_keys = jax.random.split(jax.random.key(seed), 7)
    diag_blocks = draw_diag_blocks(jax.random.fold_in(arg_keys[6], 71), 0)
    near_blocks = draw_near_blocks(jax.random.fold_in(arg_keys[6], 71), 0)
    cluster_bases = draw_cluster_bases(jax.random.fold_in(arg_keys[6], 71), 0)
    near_ids = draw_near_ids(jax.random.fold_in(arg_keys[6], 71), 0)
    near_count = plant(jax.random.randint(arg_keys[4], (CLUSTERS,), 1, NEAR + 1), jax.random.fold_in(arg_keys[4], 1), 1, NEAR).astype(jnp.int32)
    parent_bases = draw_parent_bases(jax.random.fold_in(arg_keys[6], 71), 0)
    return {"diag_blocks": diag_blocks, "near_blocks": near_blocks, "cluster_bases": cluster_bases, "near_ids": near_ids, "near_count": near_count, "parent_bases": parent_bases}


highest = lax.Precision.HIGHEST

def eliminate(dense, redundant):
    factor = jnp.linalg.cholesky(dense[:redundant, :redundant])
    solved = jax.scipy.linalg.cho_solve((factor, True), dense[:redundant, redundant:])
    schur = dense[redundant:, redundant:] - jnp.dot(dense[redundant:, :redundant], solved, precision=highest)
    return (solved, schur)

def reference(diag_blocks, near_blocks, cluster_bases, near_ids, near_count, parent_bases):
    redundant = B - K
    skeleton_bases = cluster_bases[:, :, redundant:]

    def per_cluster(items):
        block, nears, basis, neighbours, live_count = items
        product = jnp.dot(block, basis, precision=highest)
        dense = jnp.einsum('ji,jk->ik', basis, product, precision=highest)
        solved, schur = eliminate(dense, redundant)
        chosen = skeleton_bases[neighbours]
        right = jnp.einsum('nij,njk->nik', nears, chosen, precision=highest)
        moved = jnp.einsum('ji,njk->nik', basis, right, precision=highest)
        coupled = moved[:, redundant:, :] - jnp.einsum('ri,nrk->nik', solved, moved[:, :redundant, :], precision=highest)
        live = (jnp.arange(NEAR) < live_count).astype(jnp.float32)
        return (schur, coupled * live[:, None, None])
    leaf_diag, leaf_near = lax.map(per_cluster, (diag_blocks, near_blocks, cluster_bases, near_ids, near_count))
    halves = N_ROW // 2

    def split_pairs(stack):
        grouped = stack.reshape((halves, 2, C_DEV) + stack.shape[1:])
        return (grouped[:, 0].reshape((PARENTS,) + stack.shape[1:]), grouped[:, 1].reshape((PARENTS,) + stack.shape[1:]))
    diag_first, diag_second = split_pairs(leaf_diag)
    near_first, near_second = split_pairs(leaf_near[:, 0])
    upper = jnp.concatenate([diag_first, near_first], axis=2)
    lower = jnp.concatenate([near_second, diag_second], axis=2)
    merged = jnp.concatenate([upper, lower], axis=1)

    def per_parent(items):
        merged_one, basis = items
        product = jnp.dot(merged_one, basis, precision=highest)
        dense = jnp.einsum('ji,jk->ik', basis, product, precision=highest)
        return eliminate(dense, K)[1]
    parent_diag = lax.map(per_parent, (merged, parent_bases))
    return (leaf_diag, leaf_near, parent_diag)
```

```python
import jax
import jax.numpy as jnp
from jax import lax
from jax.experimental import pallas as pl
from jax.experimental.pallas import tpu as pltpu
from jax.sharding import PartitionSpec as P

B = 512
K = 256
NEAR = 4
PANEL = 8


highest = lax.Precision.HIGHEST


def partner(shard, axis, apart):
    return lax.ppermute(shard, axis, [(i, i ^ 1 << apart) for i in range(lax.axis_size(axis))])


def dot(a, b, left=1, right=0):
    dims = (((left,), (right,)), ((), ()))
    return lax.dot_general(a, b, dims, precision=highest, preferred_element_type=jnp.float32)


def sweep(block):
    size = len(block)
    e = [[block[min(i, j)][max(i, j)] for j in range(size)] for i in range(size)]
    for k in range(size):
        inv = 1.0 / e[k][k]
        t = [e[k][j] * inv for j in range(size)]
        for i in range(size):
            for j in range(i, size):
                if i != k and j != k:
                    e[i][j] = e[i][j] - e[i][k] * t[j]
                    e[j][i] = e[i][j]
        for j in range(size):
            if j != k:
                e[k][j] = e[j][k] = t[j]
        e[k][k] = -inv
    return e


def panel_step(a, lane, sub):
    n = a.shape[0]
    cols = [jnp.broadcast_to(a[:, s : s + 1], (n, n)) for s in range(PANEL)]
    block = [[jnp.broadcast_to(cols[j][i : i + 1], (PANEL, n)) if i <= j else None for j in range(PANEL)] for i in range(PANEL)]
    negated = sweep(block)
    result = jnp.where(lane < PANEL, jnp.where(lane == sub, 1.0, 0.0), a)
    rows = [jnp.broadcast_to(result[t : t + 1], (PANEL, n)) for t in range(PANEL)]
    for s in range(PANEL):
        terms = [negated[s][t] * rows[t] for t in range(PANEL)]
        while len(terms) > 1:
            terms = [terms[i] + terms[i + 1] for i in range(0, len(terms), 2)]
        spread = jnp.concatenate([terms[0]] * (n // PANEL), axis=0)
        result = result + jnp.where(sub == s, cols[s] - 1.0, cols[s]) * spread
    return result


def pivot_steps(a, lane, sub):
    n = a.shape[0]
    for s in range(PANEL):
        col = jnp.broadcast_to(a[:, s : s + 1], (n, n))
        row = jnp.where(lane[:1] == s, 1.0, a[s : s + 1, :]) * (1.0 / col[s : s + 1, :])
        cleared = jnp.where(lane == s, jnp.where(sub == s, 1.0, 0.0), a)
        a = cleared - jnp.where(sub == s, col - 1.0, col) * row
    return a


def inverse(blocks):
    n = blocks[0].shape[0]
    lane = lax.broadcasted_iota(jnp.int32, (n, n), 1)
    sub = lax.broadcasted_iota(jnp.int32, (n, n), 0)
    step = panel_step if len(blocks) == 1 else pivot_steps

    def body(_, mats):
        mats = [step(a, lane, sub) for a in mats]
        return tuple(
            pltpu.roll(jnp.concatenate([a[PANEL:], a[:PANEL]], axis=0), n - PANEL, 1) for a in mats
        )

    return lax.fori_loop(0, n // PANEL, body, tuple(blocks))


def eliminate_kernel(dense_ref, solved_ref, schur_ref):
    count, size, _ = dense_ref.shape
    half = size // 4
    full = 2 * half
    every = range(count)
    corner = [dense_ref[b, :full, :full] for b in every]
    corner = [(c + c.T) * 0.5 for c in corner]
    cross = [c[:half, half:] for c in corner]
    first = inverse([c[:half, :half] for c in corner])
    link = [dot(first[b], cross[b]) for b in every]
    second = inverse([corner[b][half:, half:] - dot(cross[b], link[b], 0, 0) for b in every])
    for b in every:
        top = dense_ref[b, :half, full:]
        low = dot(second[b], dense_ref[b, half:full, full:] - dot(link[b], top, 0, 0))
        up = dot(first[b], top) - dot(link[b], low)
        solved_ref[b, :half, :] = up
        solved_ref[b, half:, :] = low
        schur_ref[b] = (
            dense_ref[b, full:, full:]
            - dot(dense_ref[b, full:, :half], up)
            - dot(dense_ref[b, full:, half:full], low)
        )


def eliminate(dense):
    count, size, _ = dense.shape
    out = jax.ShapeDtypeStruct((count, size // 2, size // 2), jnp.float32)
    return pl.pallas_call(eliminate_kernel, out_shape=(out, out))(dense)


def per_device(diag_blocks, near_blocks, cluster_bases, near_ids, near_count, parent_bases):
    clusters = diag_blocks.shape[0]
    redundant = B - K
    column = lax.axis_index("col")
    quarter = K // lax.axis_size("col")
    own_rows = cluster_bases.shape[1]
    full_bases = lax.all_gather(cluster_bases, "col", axis=1, tiled=True)
    partial_value = jnp.einsum("cij,cjk->cik", diag_blocks, cluster_bases, precision=highest)
    summed = lax.psum(partial_value, "col")
    dense = jnp.einsum("cji,cjk->cik", full_bases, summed, precision=highest)
    solved, schur = eliminate(dense)
    leaf_diag = lax.dynamic_slice_in_dim(schur, column * quarter, quarter, 2)
    flat_ids = near_ids.reshape(-1)
    shards = lax.all_gather(cluster_bases[:, :, redundant:], "row", axis=0, tiled=True)
    number = shards.shape[0]
    one_hot = (flat_ids[:, None] == jnp.arange(number, dtype=jnp.int32)[None, :]).astype(
        jnp.float32
    )
    picked = jnp.dot(one_hot, shards.reshape(number, -1), precision=highest)
    picked = picked.reshape(clusters, NEAR, own_rows, K)
    terms = jnp.einsum("cnij,cnjk->cnik", near_blocks, picked, precision=highest)
    right_part = lax.psum_scatter(terms, "col", scatter_dimension=3, tiled=True)
    moved = jnp.einsum("cji,cnjk->cnik", full_bases, right_part, precision=highest)
    coupled = moved[:, :, redundant:, :] - jnp.einsum(
        "cri,cnrk->cnik", solved, moved[:, :, :redundant, :], precision=highest
    )
    live = (jnp.arange(NEAR, dtype=jnp.int32)[None, :] < near_count[:, None]).astype(jnp.float32)
    leaf_near = coupled * live[:, :, None, None]
    halfway = clusters // 2
    parity = lax.axis_index("row") % 2
    stacked = jnp.stack([leaf_diag, leaf_near[:, 0]])
    kept = lax.dynamic_slice_in_dim(stacked, parity * halfway, halfway, 1)
    outgoing = lax.dynamic_slice_in_dim(stacked, (1 - parity) * halfway, halfway, 1)
    arrived = partner(outgoing, "row", 0)
    first_child = jnp.where(parity == 0, kept, arrived)
    second_child = jnp.where(parity == 0, arrived, kept)
    left_columns = jnp.concatenate([first_child[0], second_child[1]], axis=1)
    right_columns = jnp.concatenate([first_child[1], second_child[0]], axis=1)
    merged = jnp.concatenate([left_columns, right_columns], axis=2)
    rows_first = lax.dynamic_slice_in_dim(parent_bases, column * quarter, quarter, 1)
    rows_second = lax.dynamic_slice_in_dim(parent_bases, K + column * quarter, quarter, 1)
    chosen_rows = jnp.concatenate([rows_first, rows_second], axis=1)
    lifted = jnp.einsum("hji,hjk->hik", parent_bases, merged, precision=highest)
    parent_part = jnp.einsum("hij,hjk->hik", lifted, chosen_rows, precision=highest)
    parent_dense = lax.psum(parent_part, "col")
    parent_schur = eliminate(parent_dense)[1]
    parent_diag = lax.dynamic_slice_in_dim(parent_schur, column * quarter, quarter, 2)
    return (leaf_diag, leaf_near, parent_diag)


def solution(mesh):
    return jax.shard_map(
        per_device,
        mesh=mesh,
        in_specs=(
            P("row", None, "col"),
            P("row", None, None, "col"),
            P("row", "col", None),
            P("row", None),
            P("row"),
            P("row", None, None),
        ),
        out_specs=(P("row", None, "col"), P("row", None, None, "col"), P("row", None, "col")),
        check_vma=False,
    )
```

```python
import jax
import jax.numpy as jnp
from jax import lax
from jax.experimental import pallas as pl
from jax.experimental.pallas import tpu as pltpu
from jax.sharding import PartitionSpec as P

B = 512
K = 256
PANEL = 8


highest = lax.Precision.HIGHEST


def dot(a, b, left=1, right=0):
    dims = (((left,), (right,)), ((), ()))
    return lax.dot_general(a, b, dims, precision=highest, preferred_element_type=jnp.float32)


def sweep(block):
    size = len(block)
    e = [[block[min(i, j)][max(i, j)] for j in range(size)] for i in range(size)]
    for k in range(size):
        inv = 1.0 / e[k][k]
        t = [e[k][j] * inv for j in range(size)]
        for i in range(size):
            for j in range(i, size):
                if i != k and j != k:
                    e[i][j] = e[i][j] - e[i][k] * t[j]
                    e[j][i] = e[i][j]
        for j in range(size):
            if j != k:
                e[k][j] = e[j][k] = t[j]
        e[k][k] = -inv
    return e


def panel_step(a, lane, sub):
    n = a.shape[0]
    cols = [jnp.broadcast_to(a[:, s : s + 1], (n, n)) for s in range(PANEL)]
    block = [[jnp.broadcast_to(cols[j][i : i + 1], (PANEL, n)) if i <= j else None for j in range(PANEL)] for i in range(PANEL)]
    negated = sweep(block)
    result = jnp.where(lane < PANEL, jnp.where(lane == sub, 1.0, 0.0), a)
    rows = [jnp.broadcast_to(result[t : t + 1], (PANEL, n)) for t in range(PANEL)]
    for s in range(PANEL):
        terms = [negated[s][t] * rows[t] for t in range(PANEL)]
        while len(terms) > 1:
            terms = [terms[i] + terms[i + 1] for i in range(0, len(terms), 2)]
        spread = jnp.concatenate([terms[0]] * (n // PANEL), axis=0)
        result = result + jnp.where(sub == s, cols[s] - 1.0, cols[s]) * spread
    return result


def inverse(a):
    n = a.shape[0]
    lane = lax.broadcasted_iota(jnp.int32, (n, n), 1)
    sub = lax.broadcasted_iota(jnp.int32, (n, n), 0)

    def body(_, mat):
        mat = panel_step(mat, lane, sub)
        return pltpu.roll(jnp.concatenate([mat[PANEL:], mat[:PANEL]], axis=0), n - PANEL, 1)

    return lax.fori_loop(0, n // PANEL, body, a)


def solve(corner, right):
    half = corner.shape[0] // 2
    cross = corner[:half, half:]
    first = inverse(corner[:half, :half])
    link = dot(first, cross)
    second = inverse(corner[half:, half:] - dot(cross, link, 0, 0))
    low = dot(second, right[half:] - dot(link, right[:half], 0, 0))
    up = dot(first, right[:half]) - dot(link, low)
    return jnp.concatenate([up, low], axis=0)


def leaf_kernel(place, a_own, a_near, a_far2, a_far3, u0, u1, u2, u3, w_ref, schur_ref):
    z = place[0]
    rows = u0.shape[0]
    skeleton = w_ref.shape[1]
    redundant = u0.shape[1] - skeleton

    def block(ref, index):
        return ref[pl.ds(pl.multiple_of(index * rows, rows), rows), :]

    near = [jnp.concatenate([block(a_own, z ^ m), block(a_near, z ^ m)], axis=1) for m in range(4)]
    corner = jnp.concatenate(near[:2], axis=0)
    edge = jnp.concatenate(near[2:], axis=0)
    inner = z % 2
    far = [jnp.concatenate([block(a_far2, i), block(a_far3, i)], axis=1) for i in (inner, 1 - inner)]
    far = jnp.concatenate(far, axis=0)
    u_near = jnp.concatenate([u0[...], u1[...]], axis=0)
    u_far = jnp.concatenate([u2[...], u3[...]], axis=0)
    y_near = dot(corner, u_near) + dot(edge, u_far, 0, 0)
    y_far = dot(edge, u_near) + dot(far, u_far)
    upper = dot(u_near[:, :redundant], y_near, 0, 0) + dot(u_far[:, :redundant], y_far, 0, 0)
    lower = dot(u_near[:, redundant:], y_near[:, redundant:], 0, 0) + dot(
        u_far[:, redundant:], y_far[:, redundant:], 0, 0
    )
    rr, rs = upper[:, :redundant], upper[:, redundant:]
    solved = solve((rr + rr.T) * 0.5, rs)
    schur_ref[...] = lower - dot(rs, solved, 0, 0)
    for m, u in enumerate((u0, u1, u2, u3)):
        part = u[:, redundant:] - dot(u[:, :redundant], solved)
        w_ref[pl.ds(pl.multiple_of((z ^ m) * rows, rows), rows), :] = part


def near_kernel(live, w_ref, *refs):
    slots = refs[0].shape[0]
    blocks, bases = refs[:4], refs[4:8]
    flipped_ref = refs[8]
    w = w_ref[...]
    for k in range(slots):
        right = dot(blocks[0][k], bases[0][k])
        for j in range(1, 4):
            right = right + dot(blocks[j][k], bases[j][k])
        flipped_ref[k] = jnp.where(live[k] > 0, dot(right, w, 0, 0), 0.0)
        if len(refs) > 9:
            refs[9][k] = dot(w, right, 0, 0)


def parent_kernel(second_own, own, arrived, v_ref, flipped_ref):
    size = own.shape[1]
    swap = second_own[0] > 0
    v_top, v_low = v_ref[:size, :], v_ref[size:, :]

    def pick(a, b, index):
        return jnp.where(swap, b[index], a[index])

    top = dot(pick(own, arrived, 0), v_top) + dot(pick(own, arrived, 1), v_low)
    low = dot(pick(arrived, own, 1), v_top) + dot(pick(arrived, own, 0), v_low)
    dense = dot(v_top, top, 0, 0) + dot(v_low, low, 0, 0)
    rr = dense[:size, :size]
    solved = solve((rr + rr.T) * 0.5, dense[:size, size:])
    flipped_ref[...] = (dense[size:, size:] - dot(dense[size:, :size], solved)).T


def call(kernel, outs, scalar, *arrays):
    vmem = pl.BlockSpec(memory_space=pltpu.VMEM)
    specs = [pl.BlockSpec(memory_space=pltpu.SMEM)] + [vmem] * len(arrays)
    shapes = [jax.ShapeDtypeStruct(shape, jnp.float32) for shape in outs]
    return pl.pallas_call(kernel, out_shape=shapes, in_specs=specs, out_specs=[vmem] * len(outs))(
        scalar, *arrays
    )


def pick(array, index):
    return lax.dynamic_index_in_dim(array, index, 0, keepdims=False)


def after(values, ready):
    return lax.optimization_barrier((values, ready))[0]


def per_device(diag_blocks, near_blocks, cluster_bases, near_ids, near_count, parent_bases):
    clusters, rows, size = cluster_bases.shape
    slots = near_blocks.shape[1]
    skeleton = K
    n_row, n_col = lax.axis_size("row"), lax.axis_size("col")
    assert n_col == 2 * clusters == 4 and n_row & (n_row - 1) == 0
    quarter = skeleton // n_col
    row, column = lax.axis_index("row"), lax.axis_index("col")
    kind = row % 2
    mine, other = column // 2, 1 - column // 2
    owner = column % 2 == kind
    both = ("row", "col")
    owned = [(r, z) for r in range(n_row) for z in range(n_col) if z % 2 == r % 2]

    def to_owner(x, j):
        return lax.ppermute(x, both, [(r * n_col + (z ^ j), r * n_col + z) for r, z in owned])

    def from_owner(x, j):
        return lax.ppermute(x, both, [(r * n_col + z, r * n_col + (z ^ j)) for r, z in owned])

    def across(x, bit):
        return lax.ppermute(x, "row", [(r, r ^ bit) for r in range(n_row)])

    def gather(x, y, cut=lambda a: a):
        return [to_owner(x, 1), to_owner(cut(y), 2), to_owner(cut(y), 3)]

    u_own, u_other = pick(cluster_bases, mine), pick(cluster_bases, other)
    a_own, a_other = pick(diag_blocks, mine), pick(diag_blocks, other)
    a_half = lax.dynamic_slice_in_dim(a_other, mine * 2 * rows, 2 * rows, 0)
    u_got = gather(u_own, u_other)
    a_got = [to_owner(a_own, 1), to_owner(a_half, 2), to_owner(a_half, 3)]

    shard = cluster_bases[:, :, size - skeleton :]
    sibling = across(shard, 1)
    table = shard
    bits = [1 << t for t in range(1, n_row.bit_length() - 1)] + [1]
    for bit in bits:
        table = jnp.concatenate([table, across(table, bit)], axis=0)
    apart = (near_ids // clusters) ^ row
    where = sum(((apart // bit) % 2) << t for t, bit in enumerate(bits)) * clusters + near_ids % clusters

    def named(which):
        spots = pick(where, which)
        return jnp.stack([pick(table, spots[k]) for k in range(1, slots)])

    first = (u_got, a_got)
    n_own, n_other = pick(near_blocks, mine), pick(near_blocks, other)
    n0, n0_other = after((n_own[:1], n_other[:1]), first)
    s0, s0_other = after((pick(sibling, mine)[None], pick(sibling, other)[None]), first)
    s0_got, n0_got = gather(s0, s0_other), gather(n0, n0_other)
    n1, n1_other = after((n_own[1:2], n_other[1:2]), first)
    n1_got = gather(n1, n1_other)

    place = column[None].astype(jnp.int32)
    w, schur = call(
        leaf_kernel,
        [(size, skeleton), (skeleton, skeleton)],
        place,
        *(a_own, *a_got),
        *(u_own, *u_got),
    )
    s1, s1_other, n2, n2_other = after((named(mine), named(other), n_own[2:], n_other[2:]), w)
    s1_got, n2_got = gather(s1, s1_other), gather(n2, n2_other)

    live = (jnp.arange(slots, dtype=jnp.int32) < pick(near_count, mine)).astype(jnp.int32)
    near0_flipped, near0 = call(
        near_kernel,
        [(1, skeleton, skeleton)] * 2,
        live[:1],
        w,
        n0,
        *n0_got,
        s0,
        *s0_got,
    )

    heads = [(r, (n_col - 1) * (r % 2)) for r in range(n_row)]
    pair = jnp.stack([schur, near0[0]])
    arrived = lax.ppermute(pair, both, [((r ^ 1) * n_col + (z ^ 1), r * n_col + z) for r, z in heads])
    (parent_flipped,) = call(
        parent_kernel,
        [(skeleton, skeleton)],
        kind[None].astype(jnp.int32),
        pair,
        arrived,
        parent_bases[0],
    )

    def rows_of(x, c):
        return lax.dynamic_slice_in_dim(x, c * quarter, quarter, x.ndim - 2)

    def spread(x):
        got = [from_owner(rows_of(x, column ^ j), j) for j in range(1, 4)]
        here = jnp.where(owner, rows_of(x, column), got[0])
        there = got[1] + got[2]
        low = jnp.where(mine == 0, here, there)
        high = jnp.where(mine == 0, there, here)
        return jnp.swapaxes(jnp.stack([low, high]), -1, -2)

    early = spread(jnp.concatenate([schur[None], near0_flipped], axis=0))
    near_a = call(
        near_kernel,
        [(1, skeleton, skeleton)],
        live[1:2],
        w,
        n1,
        *n1_got,
        s1[:1],
        *(s[:1] for s in s1_got),
    )[0]
    near_b = call(
        near_kernel,
        [(slots - 2, skeleton, skeleton)],
        live[2:],
        w,
        n2,
        *n2_got,
        s1[1:],
        *(s[1:] for s in s1_got),
    )[0]
    late = spread(jnp.concatenate([near_a, near_b], axis=0))
    leaf_diag = early[:, 0]
    leaf_near = jnp.concatenate([early[:, 1:], late], axis=1)
    head = column == (n_col - 1) * kind
    parts = [
        lax.ppermute(
            rows_of(parent_flipped, column ^ j),
            both,
            [(r * n_col + z, r * n_col + (z ^ j)) for r, z in heads],
        )
        for j in range(1, 4)
    ]
    final = jnp.where(head, rows_of(parent_flipped, column), parts[0] + parts[1] + parts[2])
    return (leaf_diag, leaf_near, final.T[None])


def solution(mesh):
    return jax.shard_map(
        per_device,
        mesh=mesh,
        in_specs=(
            P("row", None, "col"),
            P("row", None, None, "col"),
            P("row", "col", None),
            P("row", None),
            P("row"),
            P("row", None, None),
        ),
        out_specs=(P("row", None, "col"), P("row", None, None, "col"), P("row", None, "col")),
        check_vma=False,
    )
```

```python
import jax
import jax.numpy as jnp
from jax import lax
from jax.experimental import pallas as pl
from jax.experimental.pallas import tpu as pltpu
from jax.sharding import PartitionSpec as P

B = 512
K = 256
PANEL = 8


highest = lax.Precision.HIGHEST


def dot(a, b, left=1, right=0):
    dims = (((left,), (right,)), ((), ()))
    return lax.dot_general(a, b, dims, precision=highest, preferred_element_type=jnp.float32)


def dot3(a, b):
    a_high, b_high = a.astype(jnp.bfloat16), b.astype(jnp.bfloat16)
    a_low = (a - a_high.astype(jnp.float32)).astype(jnp.bfloat16)
    b_low = (b - b_high.astype(jnp.float32)).astype(jnp.bfloat16)

    def product(x, y):
        return jnp.dot(x, y, preferred_element_type=jnp.float32)

    return product(a_high, b_high) + (product(a_high, b_low) + product(a_low, b_high))


def sweep(block):
    size = len(block)
    e = [[block[min(i, j)][max(i, j)] for j in range(size)] for i in range(size)]
    for k in range(size):
        inv = 1.0 / e[k][k]
        t = [e[k][j] * inv for j in range(size)]
        for i in range(size):
            for j in range(i, size):
                if i != k and j != k:
                    e[i][j] = e[i][j] - e[i][k] * t[j]
                    e[j][i] = e[i][j]
        for j in range(size):
            if j != k:
                e[k][j] = e[j][k] = t[j]
        e[k][k] = -inv
    return e


def panel_step(a, lane, sub):
    n = a.shape[0]
    cols = [jnp.broadcast_to(a[:, s : s + 1], (n, n)) for s in range(PANEL)]
    block = [[jnp.broadcast_to(cols[j][i : i + 1], (PANEL, n)) if i <= j else None for j in range(PANEL)] for i in range(PANEL)]
    negated = sweep(block)
    result = jnp.where(lane < PANEL, jnp.where(lane == sub, 1.0, 0.0), a)
    rows = [jnp.broadcast_to(result[t : t + 1], (PANEL, n)) for t in range(PANEL)]
    for s in range(PANEL):
        terms = [negated[s][t] * rows[t] for t in range(PANEL)]
        while len(terms) > 1:
            terms = [terms[i] + terms[i + 1] for i in range(0, len(terms), 2)]
        spread = jnp.concatenate([terms[0]] * (n // PANEL), axis=0)
        result = result + jnp.where(sub == s, cols[s] - 1.0, cols[s]) * spread
    return result


def inverse(a):
    n = a.shape[0]
    lane = lax.broadcasted_iota(jnp.int32, (n, n), 1)
    sub = lax.broadcasted_iota(jnp.int32, (n, n), 0)

    def body(_, mat):
        mat = panel_step(mat, lane, sub)
        return pltpu.roll(jnp.concatenate([mat[PANEL:], mat[:PANEL]], axis=0), n - PANEL, 1)

    return lax.fori_loop(0, n // PANEL, body, a)


def solve(corner, right):
    half = corner.shape[0] // 2
    cross, turned = corner[:half, half:], corner[half:, :half]
    first = inverse(corner[:half, :half])
    link, link_turned = dot(first, cross), dot(turned, first)
    second = inverse(corner[half:, half:] - dot(turned, link))
    low = dot(second, right[half:] - dot(link_turned, right[:half]))
    up = dot(first, right[:half]) - dot(link, low)
    return jnp.concatenate([up, low], axis=0)


def eliminate(dense, redundant):
    rr = dense[:redundant, :redundant]
    solved = solve((rr + rr.T) * 0.5, dense[:redundant, redundant:])
    return solved, dense[redundant:, redundant:] - dot(dense[redundant:, :redundant], solved)


def wide(ref, start, count):
    return jnp.concatenate([ref[start + i] for i in range(count)], axis=1)


def leaf_kernel(place, own, near, far2, far3, w_ref, schur_ref):
    z = place[0]
    inner = z % 2
    edge = own.shape[1]
    redundant = 4 * edge - w_ref.shape[1]
    pairs = [jnp.concatenate([own[z ^ m], near[z ^ m]], axis=1) for m in range(4)]
    corner = jnp.concatenate(pairs[:2], axis=0)
    side = jnp.concatenate(pairs[2:], axis=0)
    far = [jnp.concatenate([far2[i], far3[i]], axis=1) for i in (inner, 1 - inner)]
    far = jnp.concatenate(far, axis=0)
    bases = [wide(own, 4, 4), wide(near, 4, 4), wide(far2, 2, 4), wide(far3, 2, 4)]
    u = jnp.concatenate(bases, axis=0)
    ut = u.T
    ut_near, ut_far = ut[:, : 2 * edge], ut[:, 2 * edge :]
    yt_near = dot(ut_near, corner) + dot(ut_far, side)
    yt_far = dot(ut_near, side, 1, 1) + dot(ut_far, far)
    dense = dot(jnp.concatenate([yt_near, yt_far], axis=1), u)
    solved, schur = eliminate(dense, redundant)
    schur_ref[...] = schur
    wt = ut[redundant:] - dot(solved.T, ut[:redundant])
    for m in range(4):
        w_ref[z ^ m] = wt[:, m * edge : (m + 1) * edge]


def coupling(w_ref, blocks, bases):
    w = jnp.concatenate([w_ref[b] for b in range(4)], axis=1)
    return dot3(w, dot3(jnp.concatenate(blocks, axis=1), jnp.concatenate(bases, axis=0)))


def tall(ref, start):
    return jnp.concatenate([ref[start + i] for i in range(4)], axis=0)


def near_first_kernel(live, w_ref, bases, n0, n1, n2, n3, pair_in, flipped_ref, pair_ref):
    result = coupling(w_ref, [tall(n, 0) for n in (n0, n1, n2, n3)], [bases[j ^ 1] for j in range(4)])
    result = jnp.where(live[0] > 0, result, 0.0)
    pair_ref[0] = pair_in[...]
    pair_ref[1] = result
    flipped_ref[0] = pair_in[...]
    flipped_ref[1] = result.T


def near_rest_kernel(live, w_ref, *refs):
    early, late, flipped_ref = refs[:4], refs[4:8], refs[8]
    ahead = early[0].shape[0] // 4
    total = flipped_ref.shape[0]
    behind = 4 * (total - ahead)
    for k in range(total):
        blocks = [tall(e, 4 * k) if k < ahead else tall(f, 4 * (k - ahead)) for e, f in zip(early, late)]
        bases = [wide(f, behind + 2 * k, 2) for f in late]
        result = coupling(w_ref, blocks, bases)
        flipped_ref[k] = jnp.where(live[k + 1] > 0, result, 0.0).T


def parent_kernel(second_own, own, arrived, vt_ref, v_ref, flipped_ref):
    size = own.shape[1]
    swap = second_own[0] > 0

    def pick(a, b, index):
        return jnp.where(swap, b[index], a[index])

    top = jnp.concatenate([pick(own, arrived, 0), pick(own, arrived, 1)], axis=1)
    low = jnp.concatenate([pick(arrived, own, 1), pick(arrived, own, 0)], axis=1)
    merged = jnp.concatenate([top, low], axis=0)
    dense = dot(dot(vt_ref[...], merged), v_ref[...])
    flipped_ref[0] = eliminate(dense, size)[1].T


def call(kernel, outs, scalar, *arrays):
    vmem = pl.BlockSpec(memory_space=pltpu.VMEM)
    specs = [pl.BlockSpec(memory_space=pltpu.SMEM)] + [vmem] * len(arrays)
    shapes = [jax.ShapeDtypeStruct(shape, jnp.float32) for shape in outs]
    return pl.pallas_call(kernel, out_shape=shapes, in_specs=specs, out_specs=[vmem] * len(outs))(
        scalar, *arrays
    )


def pick(array, index):
    return lax.dynamic_index_in_dim(array, index, 0, keepdims=False)


def after(values, ready):
    return lax.optimization_barrier((values, ready))[0]


def across_lanes(x, edge):
    return [x[:, i : i + edge] for i in range(0, x.shape[1], edge)]


def down_rows(x, edge):
    return [x[i : i + edge] for i in range(0, x.shape[0], edge)]


def per_device(diag_blocks, near_blocks, cluster_bases, near_ids, near_count, parent_bases):
    clusters, edge, size = cluster_bases.shape
    slots = near_blocks.shape[1]
    skeleton = K
    n_row, n_col = lax.axis_size("row"), lax.axis_size("col")
    assert n_col == 2 * clusters == 4 and n_row & (n_row - 1) == 0
    quarter = skeleton // n_col
    row, column = lax.axis_index("row"), lax.axis_index("col")
    kind = row % 2
    mine, other = column // 2, 1 - column // 2
    owner = column % 2 == kind
    both = ("row", "col")
    owned = [(r, z) for r in range(n_row) for z in range(n_col) if z % 2 == r % 2]
    heads = [(r, (n_col - 1) * (r % 2)) for r in range(n_row)]

    def to_owner(x, j):
        return lax.ppermute(x, both, [(r * n_col + (z ^ j), r * n_col + z) for r, z in owned])

    def from_owner(x, j):
        return lax.ppermute(x, both, [(r * n_col + z, r * n_col + (z ^ j)) for r, z in owned])

    def from_sibling(x, places):
        return lax.ppermute(x, both, [((r ^ 1) * n_col + (z ^ 1), r * n_col + z) for r, z in places])

    def across(x, bit):
        return lax.ppermute(x, "row", [(r, r ^ bit) for r in range(n_row)])

    def gather(x, y):
        return [x, to_owner(x, 1), to_owner(y, 2), to_owner(y, 3)]

    a_other = lax.dynamic_slice_in_dim(pick(diag_blocks, other), mine * 2 * edge, 2 * edge, 0)
    u_mine, u_other = pick(cluster_bases, mine), pick(cluster_bases, other)
    full = jnp.stack(down_rows(pick(diag_blocks, mine), edge) + across_lanes(u_mine, edge))
    half = jnp.stack(down_rows(a_other, edge) + across_lanes(u_other, edge))
    leaf = gather(full, half)
    leaf_got = leaf[1:]

    table = after(cluster_bases[:, :, size - skeleton :], (full, half))
    bits = [1 << t for t in range(1, n_row.bit_length() - 1)] + [1]
    for bit in bits[:-1]:
        table = jnp.concatenate([table, across(table, bit)], axis=0)

    n_mine, n_other = pick(near_blocks, mine), pick(near_blocks, other)
    n_mine = n_mine.reshape(slots * 4, edge, edge)
    n_other = n_other.reshape(slots * 4, edge, edge)
    n0 = gather(*after((n_mine[:4], n_other[:4]), leaf_got))
    skeletons = jnp.stack([u_mine[:, size - skeleton :]] + [jnp.concatenate([x[-2], x[-1]], axis=1) for x in leaf_got])
    sibling = from_sibling(skeletons, owned)

    place = column[None].astype(jnp.int32)
    w, schur = call(
        leaf_kernel,
        [(4, skeleton, edge), (skeleton, skeleton)],
        place,
        *leaf,
    )
    n_early = gather(*after((n_mine[4:12], n_other[4:12]), w))

    live = (jnp.arange(slots, dtype=jnp.int32) < pick(near_count, mine)).astype(jnp.int32)
    early, pair = call(
        near_first_kernel,
        [(2, skeleton, skeleton)] * 2,
        live,
        w,
        sibling,
        *n0,
        schur,
    )
    arrived = from_sibling(pair, heads)

    table = after(table, w)
    halves = [table, across(table, bits[-1])]
    apart = (near_ids // clusters) ^ row
    spot = sum(((apart // bit) % 2) << t for t, bit in enumerate(bits[:-1])) * clusters + near_ids % clusters
    turned = apart % 2

    def named(which):
        spots, sides = pick(spot, which), pick(turned, which)
        found = [
            jnp.where(sides[k] > 0, pick(halves[1], spots[k]), pick(halves[0], spots[k]))
            for k in range(1, slots)
        ]
        return [block for x in found for block in across_lanes(x, edge)]

    late_mine, late_other = after((n_mine[12:], n_other[12:]), pair)
    late = gather(
        jnp.stack(list(late_mine) + named(mine)), jnp.stack(list(late_other) + named(other))
    )

    v = parent_bases[0]
    (parent,) = call(
        parent_kernel,
        [(1, skeleton, skeleton)],
        kind[None].astype(jnp.int32),
        pair,
        arrived,
        v.T,
        v,
    )
    (rest,) = call(
        near_rest_kernel,
        [(slots - 1, skeleton, skeleton)],
        live,
        w,
        *n_early,
        *late,
    )

    results = jnp.concatenate([early, rest, parent], axis=0)

    def rows_of(c):
        return lax.dynamic_slice_in_dim(results, c * quarter, quarter, 1)

    got = [rows_of(column)] + [from_owner(rows_of(column ^ j), j) for j in range(1, 4)]
    here = jnp.where(owner, got[0], got[1])
    there = got[2] + got[3]
    low = jnp.where(mine == 0, here, there)
    high = jnp.where(mine == 0, there, here)
    leaf_diag = jnp.stack([low[0], high[0]])
    leaf_near = jnp.stack([low[1 : 1 + slots], high[1 : 1 + slots]])
    final = jnp.where(kind == 0, low[1 + slots], high[1 + slots])
    return (
        jnp.swapaxes(leaf_diag, -1, -2),
        jnp.swapaxes(leaf_near, -1, -2),
        final.T[None],
    )


def solution(mesh):
    return jax.shard_map(
        per_device,
        mesh=mesh,
        in_specs=(
            P("row", None, "col"),
            P("row", None, None, "col"),
            P("row", "col", None),
            P("row", None),
            P("row"),
            P("row", None, None),
        ),
        out_specs=(P("row", None, "col"), P("row", None, None, "col"), P("row", None, "col")),
        check_vma=False,
    )
```

```python
import jax
import jax.numpy as jnp
from jax import lax
from jax.experimental import pallas as pl
from jax.experimental.pallas import tpu as pltpu
from jax.sharding import PartitionSpec as P

B = 512
K = 256
PANEL = 8


highest = lax.Precision.HIGHEST


def dot(a, b, left=1, right=0):
    dims = (((left,), (right,)), ((), ()))
    return lax.dot_general(a, b, dims, precision=highest, preferred_element_type=jnp.float32)


def dot3(a, b):
    a_high, b_high = a.astype(jnp.bfloat16), b.astype(jnp.bfloat16)
    a_low = (a - a_high.astype(jnp.float32)).astype(jnp.bfloat16)
    b_low = (b - b_high.astype(jnp.float32)).astype(jnp.bfloat16)

    def product(x, y):
        return jnp.dot(x, y, preferred_element_type=jnp.float32)

    return product(a_high, b_high) + (product(a_high, b_low) + product(a_low, b_high))


def sweep(block):
    size = len(block)
    e = [[block[min(i, j)][max(i, j)] for j in range(size)] for i in range(size)]
    for k in range(size):
        inv = 1.0 / e[k][k]
        t = [e[k][j] * inv for j in range(size)]
        for i in range(size):
            for j in range(i, size):
                if i != k and j != k:
                    e[i][j] = e[i][j] - e[i][k] * t[j]
                    e[j][i] = e[i][j]
        for j in range(size):
            if j != k:
                e[k][j] = e[j][k] = t[j]
        e[k][k] = -inv
    return e


def panel_step(a, lane, sub):
    n = a.shape[0]
    cols = [jnp.broadcast_to(a[:, s : s + 1], (n, n)) for s in range(PANEL)]
    block = [[jnp.broadcast_to(cols[j][i : i + 1], (PANEL, n)) if i <= j else None for j in range(PANEL)] for i in range(PANEL)]
    negated = sweep(block)
    result = jnp.where(lane < PANEL, jnp.where(lane == sub, 1.0, 0.0), a)
    rows = [jnp.broadcast_to(result[t : t + 1], (PANEL, n)) for t in range(PANEL)]
    for s in range(PANEL):
        terms = [negated[s][t] * rows[t] for t in range(PANEL)]
        while len(terms) > 1:
            terms = [terms[i] + terms[i + 1] for i in range(0, len(terms), 2)]
        spread = jnp.concatenate([terms[0]] * (n // PANEL), axis=0)
        result = result + jnp.where(sub == s, cols[s] - 1.0, cols[s]) * spread
    return result


def inverse(a):
    n = a.shape[0]
    lane = lax.broadcasted_iota(jnp.int32, (n, n), 1)
    sub = lax.broadcasted_iota(jnp.int32, (n, n), 0)

    def body(_, mat):
        mat = panel_step(mat, lane, sub)
        return pltpu.roll(jnp.concatenate([mat[PANEL:], mat[:PANEL]], axis=0), n - PANEL, 1)

    return lax.fori_loop(0, n // PANEL, body, a)


def solve(corner, right):
    half = corner.shape[0] // 2
    cross, turned = corner[:half, half:], corner[half:, :half]
    first = inverse(corner[:half, :half])
    link, link_turned = dot(first, cross), dot(turned, first)
    second = inverse(corner[half:, half:] - dot(turned, link))
    low = dot(second, right[half:] - dot(link_turned, right[:half]))
    up = dot(first, right[:half]) - dot(link, low)
    return jnp.concatenate([up, low], axis=0)


def eliminate(dense, redundant):
    rr = dense[:redundant, :redundant]
    solved = solve((rr + rr.T) * 0.5, dense[:redundant, redundant:])
    return solved, dense[redundant:, redundant:] - dot(dense[redundant:, :redundant], solved)


def wide(ref, start, count):
    return jnp.concatenate([ref[start + i] for i in range(count)], axis=1)


def leaf_kernel(place, own, near, far2, far3, w_ref, schur_ref):
    z = place[1]
    inner = z & 1
    edge = own.shape[1]
    redundant = 4 * edge - w_ref.shape[1]
    pairs = [jnp.concatenate([own[z ^ m], near[z ^ m]], axis=1) for m in range(4)]
    corner = jnp.concatenate(pairs[:2], axis=0)
    side = jnp.concatenate(pairs[2:], axis=0)
    far = [jnp.concatenate([far2[i], far3[i]], axis=1) for i in (inner, 1 - inner)]
    far = jnp.concatenate(far, axis=0)
    bases = [wide(own, 4, 4), wide(near, 4, 4), wide(far2, 2, 4), wide(far3, 2, 4)]
    u = jnp.concatenate(bases, axis=0)
    ut = u.T
    ut_near, ut_far = ut[:, : 2 * edge], ut[:, 2 * edge :]
    yt_near = dot(ut_near, corner) + dot(ut_far, side)
    yt_far = dot(ut_near, side, 1, 1) + dot(ut_far, far)
    dense = dot(jnp.concatenate([yt_near, yt_far], axis=1), u)
    solved, schur = eliminate(dense, redundant)
    schur_ref[...] = schur
    wt = ut[redundant:] - dot(solved.T, ut[:redundant])
    for m in range(4):
        w_ref[z ^ m] = wt[:, m * edge : (m + 1) * edge]


def pack_kernel(place, diag, bases, full, half, shard):
    edge = bases.shape[1]
    mine = place[1] >> 1
    other = 1 - mine
    for i in range(4):
        lanes = slice(i * edge, (i + 1) * edge)
        full[i] = diag[mine, lanes, :]
        full[4 + i] = bases[mine, :, lanes]
        half[2 + i] = bases[other, :, lanes]
    for i in range(2):
        half[i] = diag[other, pl.ds(pl.multiple_of((2 * mine + i) * edge, edge), edge), :]
    for c in range(bases.shape[0]):
        shard[c] = bases[c, :, bases.shape[2] - shard.shape[2] :]


def skeleton_kernel(place, own, near, far2, far3, out):
    for j, ref in enumerate((own, near, far2, far3)):
        out[j] = wide(ref, ref.shape[0] - 2, 2)


def name_kernel(place, ids, low, high, mine_ref, other_ref):
    row, mine = place[0], place[1] >> 1
    clusters, slots = ids.shape
    for which, out in ((mine, mine_ref), (1 - mine, other_ref)):
        for k in range(1, slots):
            name = ids[which, k]
            apart = lax.div(name, clusters) ^ row
            spot = (apart >> 1) * clusters + lax.rem(name, clusters)
            out[k - 1] = jnp.where((apart & 1) > 0, high[spot], low[spot])


def coupling(w_ref, blocks, bases):
    w = jnp.concatenate([w_ref[b] for b in range(4)], axis=1)
    return dot3(w, dot3(jnp.concatenate(blocks, axis=1), jnp.concatenate(bases, axis=0)))


def tall(ref, start):
    return jnp.concatenate([ref[start + i] for i in range(4)], axis=0)


def deal(z, flipped, index, parts):
    quarter = parts[0].shape[1]
    for j, part in enumerate(parts):
        part[index] = flipped[index, pl.ds(pl.multiple_of((z ^ j) * quarter, quarter), quarter), :]


def near_first_kernel(place, count, w_ref, bases, n0, n1, n2, n3, schur, pair, p0, p1, p2, p3, flipped):
    z = place[1]
    result = coupling(w_ref, [tall(n, 0) for n in (n0, n1, n2, n3)], [bases[j ^ 1] for j in range(4)])
    result = jnp.where(count[z >> 1] > 0, result, 0.0)
    pair[0] = schur[...]
    pair[1] = result
    flipped[0] = schur[...]
    flipped[1] = result.T
    for i in range(2):
        deal(z, flipped, i, (p0, p1, p2, p3))


def near_rest_kernel(place, count, w_ref, parent, *refs):
    z = place[1]
    early, late, named, parts, flipped = refs[:4], refs[4:8], refs[8:12], refs[12:16], refs[16]
    ahead = early[0].shape[0] // 4 - 1
    total = named[0].shape[0]
    for k in range(total):
        blocks = [tall(e, 4 * k + 4) if k < ahead else tall(f, 4 * (k - ahead)) for e, f in zip(early, late)]
        result = coupling(w_ref, blocks, [s[k] for s in named])
        flipped[k] = jnp.where(count[z >> 1] > k + 1, result, 0.0).T
        deal(z, flipped, k, parts)
    flipped[total] = parent[...]
    deal(z, flipped, total, parts)


def finish_kernel(place, *refs):
    row, z = place[0], place[1]
    early, late, (diag, near, final) = refs[:4], refs[4:8], refs[8:]
    owner = (z & 1) == (row & 1)
    swap = z >> 1

    def sides(parts, i):
        here = jnp.where(owner, parts[0][i], parts[1][i])
        return here.T, (parts[2][i] + parts[3][i]).T

    def place_both(ref, index, parts, i):
        here, there = sides(parts, i)
        ref[(swap,) + index] = here
        ref[(1 - swap,) + index] = there

    place_both(diag, (), early, 0)
    place_both(near, (0,), early, 1)
    total = late[0].shape[0] - 1
    for k in range(total):
        place_both(near, (k + 1,), late, k)
    here, there = sides(late, total)
    final[0] = jnp.where(swap == (row & 1), here, there)


def parent_kernel(place, own, arrived, vt_ref, v_ref, flipped_ref):
    size = own.shape[1]
    swap = (place[0] & 1) > 0

    def choose(a, b, index):
        return jnp.where(swap, b[index], a[index])

    top = jnp.concatenate([choose(own, arrived, 0), choose(own, arrived, 1)], axis=1)
    low = jnp.concatenate([choose(arrived, own, 1), choose(arrived, own, 0)], axis=1)
    merged = jnp.concatenate([top, low], axis=0)
    dense = dot(dot(vt_ref[...], merged), v_ref[...])
    flipped_ref[...] = eliminate(dense, size)[1].T


def call(kernel, outs, scalars, arrays, us=2, scratch=()):
    vmem = pl.BlockSpec(memory_space=pltpu.VMEM)
    specs = [pl.BlockSpec(memory_space=pltpu.SMEM)] * len(scalars) + [vmem] * len(arrays)
    shapes = [jax.ShapeDtypeStruct(shape, jnp.float32) for shape in outs]
    cost = pl.CostEstimate(flops=us * 10**9, bytes_accessed=us * 10**6, transcendentals=0)
    return pl.pallas_call(
        kernel,
        out_shape=shapes,
        in_specs=specs,
        out_specs=[vmem] * len(outs),
        scratch_shapes=[pltpu.VMEM(shape, jnp.float32) for shape in scratch],
        cost_estimate=cost,
    )(*scalars, *arrays)


def pick(array, index):
    return lax.dynamic_index_in_dim(array, index, 0, keepdims=False)


def after(values, ready):
    return lax.optimization_barrier((values, ready))[0]


def per_device(diag_blocks, near_blocks, cluster_bases, near_ids, near_count, parent_bases):
    clusters, edge, size = cluster_bases.shape
    slots = near_blocks.shape[1]
    skeleton = K
    n_row, n_col = lax.axis_size("row"), lax.axis_size("col")
    assert n_col == 2 * clusters == 4 and n_row & (n_row - 1) == 0
    quarter = skeleton // n_col
    row, column = lax.axis_index("row"), lax.axis_index("col")
    place = jnp.stack([row, column]).astype(jnp.int32)
    mine, other = column // 2, 1 - column // 2
    both = ("row", "col")
    owned = [(r, z) for r in range(n_row) for z in range(n_col) if z % 2 == r % 2]
    heads = [(r, (n_col - 1) * (r % 2)) for r in range(n_row)]

    def to_owner(x, j):
        return lax.ppermute(x, both, [(r * n_col + (z ^ j), r * n_col + z) for r, z in owned])

    def from_owner(x, j):
        return lax.ppermute(x, both, [(r * n_col + z, r * n_col + (z ^ j)) for r, z in owned])

    def from_sibling(x, places):
        return lax.ppermute(x, both, [((r ^ 1) * n_col + (z ^ 1), r * n_col + z) for r, z in places])

    def across(x, bit):
        return lax.ppermute(x, "row", [(r, r ^ bit) for r in range(n_row)])

    def gather(x, y):
        return [x, to_owner(x, 1), to_owner(y, 2), to_owner(y, 3)]

    def scatter(parts):
        return [parts[0]] + [from_owner(parts[j], j) for j in range(1, 4)]

    full, half, table = call(
        pack_kernel,
        [(8, edge, edge), (6, edge, edge), (clusters, edge, skeleton)],
        [place],
        [diag_blocks, cluster_bases],
    )
    leaf = gather(full, half)

    bits = [1 << t for t in range(1, n_row.bit_length() - 1)]
    for bit in bits:
        table = jnp.concatenate([table, across(table, bit)], axis=0)

    near = near_blocks.reshape(clusters, slots * 4, edge, edge)
    n_mine, n_other = pick(near, mine), pick(near, other)
    n_early = gather(*after((n_mine[:8], n_other[:8]), leaf[1:]))
    (skeletons,) = call(skeleton_kernel, [(4, edge, skeleton)], [place], leaf)
    sibling = from_sibling(skeletons, owned)

    w, schur = call(
        leaf_kernel, [(4, skeleton, edge), (skeleton, skeleton)], [place], leaf, 22
    )
    n_late = gather(*after((n_mine[8:], n_other[8:]), w))

    pair, *first = call(
        near_first_kernel,
        [(2, skeleton, skeleton)] + [(2, quarter, skeleton)] * 4,
        [place, near_count],
        [w, sibling, *n_early, schur],
        4,
        [(2, skeleton, skeleton)],
    )
    arrived = from_sibling(pair, heads)

    table = after(table, w)
    s_mine, s_other = call(
        name_kernel,
        [(slots - 1, edge, skeleton)] * 2,
        [place, near_ids],
        [table, across(table, 1)],
    )
    named = gather(*after((s_mine, s_other), pair))
    early = scatter(first)

    v = parent_bases[0]
    (parent,) = call(
        parent_kernel, [(skeleton, skeleton)], [place], [pair, arrived, v.T, v], 22
    )
    rest = call(
        near_rest_kernel,
        [(slots, quarter, skeleton)] * 4,
        [place, near_count],
        [after(w, early[1:]), parent, *n_early, *n_late, *named],
        7,
        [(slots, skeleton, skeleton)],
    )
    late = scatter(rest)
    return tuple(
        call(
            finish_kernel,
            [
                (clusters, skeleton, quarter),
                (clusters, slots, skeleton, quarter),
                (1, skeleton, quarter),
            ],
            [place],
            [*early, *late],
        )
    )


def solution(mesh):
    return jax.shard_map(
        per_device,
        mesh=mesh,
        in_specs=(
            P("row", None, "col"),
            P("row", None, None, "col"),
            P("row", "col", None),
            P("row", None),
            P("row"),
            P("row", None, None),
        ),
        out_specs=(P("row", None, "col"), P("row", None, None, "col"), P("row", None, "col")),
        check_vma=False,
    )
```

```python
import jax
import jax.numpy as jnp
from jax import lax
from jax.experimental import pallas as pl
from jax.experimental.pallas import tpu as pltpu
from jax.sharding import PartitionSpec as P


K = 256
PANEL = 8


highest = lax.Precision.HIGHEST


def dot(a, b, left=1, right=0):
    dims = (((left,), (right,)), ((), ()))
    return lax.dot_general(a, b, dims, precision=highest, preferred_element_type=jnp.float32)


def dot3(a, b):
    a_high, b_high = a.astype(jnp.bfloat16), b.astype(jnp.bfloat16)
    a_low = (a - a_high.astype(jnp.float32)).astype(jnp.bfloat16)
    b_low = (b - b_high.astype(jnp.float32)).astype(jnp.bfloat16)

    def product(x, y):
        return jnp.dot(x, y, preferred_element_type=jnp.float32)

    return product(a_high, b_high) + (product(a_high, b_low) + product(a_low, b_high))


def sweep(block):
    size = len(block)
    e = [[block[min(i, j)][max(i, j)] for j in range(size)] for i in range(size)]
    for k in range(size):
        inv = 1.0 / e[k][k]
        t = [e[k][j] * inv for j in range(size)]
        for i in range(size):
            for j in range(i, size):
                if i != k and j != k:
                    e[i][j] = e[i][j] - e[i][k] * t[j]
                    e[j][i] = e[i][j]
        for j in range(size):
            if j != k:
                e[k][j] = e[j][k] = t[j]
        e[k][k] = -inv
    return e


def panel_step(a, lane, sub):
    n = a.shape[0]
    cols = [jnp.broadcast_to(a[:, s : s + 1], (n, n)) for s in range(PANEL)]
    block = [[jnp.broadcast_to(cols[j][i : i + 1], (PANEL, n)) if i <= j else None for j in range(PANEL)] for i in range(PANEL)]
    negated = sweep(block)
    result = jnp.where(lane < PANEL, jnp.where(lane == sub, 1.0, 0.0), a)
    rows = [jnp.broadcast_to(result[t : t + 1], (PANEL, n)) for t in range(PANEL)]
    for s in range(PANEL):
        terms = [negated[s][t] * rows[t] for t in range(PANEL)]
        while len(terms) > 1:
            terms = [terms[i] + terms[i + 1] for i in range(0, len(terms), 2)]
        spread = jnp.concatenate([terms[0]] * (n // PANEL), axis=0)
        top = jnp.where(sub[:PANEL] == s, cols[s][:PANEL] - 1.0, cols[s][:PANEL])
        result = result + jnp.concatenate([top, cols[s][PANEL:]], axis=0) * spread
    return result


def inverse(a):
    n = a.shape[0]
    lane = lax.broadcasted_iota(jnp.int32, (n, n), 1)
    sub = lax.broadcasted_iota(jnp.int32, (n, n), 0)

    def body(_, mat):
        mat = panel_step(mat, lane, sub)
        return pltpu.roll(jnp.concatenate([mat[PANEL:], mat[:PANEL]], axis=0), n - PANEL, 1)

    return lax.fori_loop(0, n // PANEL, body, a)


def solve(corner, right):
    half = corner.shape[0] // 2
    cross, turned = corner[:half, half:], corner[half:, :half]
    first = inverse(corner[:half, :half])
    link, link_turned = dot(first, cross), dot(turned, first)
    second = inverse(corner[half:, half:] - dot(turned, link))
    low = dot(second, right[half:] - dot(link_turned, right[:half]))
    up = dot(first, right[:half]) - dot(link, low)
    return jnp.concatenate([up, low], axis=0)


def eliminate(dense, redundant):
    rr = dense[:redundant, :redundant]
    solved = solve((rr + rr.T) * 0.5, dense[:redundant, redundant:])
    return solved, dense[redundant:, redundant:] - dot(dense[redundant:, :redundant], solved)


def wide(ref, start, count):
    return jnp.concatenate([ref[start + i] for i in range(count)], axis=1)


def leaf_kernel(place, own, near, far2, far3, w_ref, schur_ref):
    z = place[1]
    inner = z & 1
    edge = own.shape[1]
    redundant = 4 * edge - w_ref.shape[1]
    pairs = [jnp.concatenate([own[z ^ m], near[z ^ m]], axis=1) for m in range(4)]
    corner = jnp.concatenate(pairs[:2], axis=0)
    side = jnp.concatenate(pairs[2:], axis=0)
    far = [jnp.concatenate([far2[i], far3[i]], axis=1) for i in (inner, 1 - inner)]
    far = jnp.concatenate(far, axis=0)
    bases = [wide(own, 4, 4), wide(near, 4, 4), wide(far2, 2, 4), wide(far3, 2, 4)]
    u = jnp.concatenate(bases, axis=0)
    ut = u.T
    ut_near, ut_far = ut[:, : 2 * edge], ut[:, 2 * edge :]
    yt_near = dot(ut_near, corner) + dot(ut_far, side)
    yt_far = dot(ut_near, side, 1, 1) + dot(ut_far, far)
    dense = dot(jnp.concatenate([yt_near, yt_far], axis=1), u)
    solved, schur = eliminate(dense, redundant)
    schur_ref[...] = schur
    wt = ut[redundant:] - dot(solved.T, ut[:redundant])
    for m in range(4):
        w_ref[z ^ m] = wt[:, m * edge : (m + 1) * edge]


def pack_kernel(place, diag, bases, full, half, shard):
    edge = bases.shape[1]
    mine = place[1] >> 1
    other = 1 - mine
    for i in range(4):
        lanes = slice(i * edge, (i + 1) * edge)
        full[i] = diag[mine, lanes, :]
        full[4 + i] = bases[mine, :, lanes]
        half[2 + i] = bases[other, :, lanes]
    for i in range(2):
        half[i] = diag[other, pl.ds(pl.multiple_of((2 * mine + i) * edge, edge), edge), :]
    for c in range(bases.shape[0]):
        shard[c] = bases[c, :, bases.shape[2] - shard.shape[2] :]


def skeleton_kernel(place, own, near, far2, far3, out):
    for j, ref in enumerate((own, near, far2, far3)):
        out[j] = wide(ref, ref.shape[0] - 2, 2)


def name_kernel(place, ids, low, high, mine_ref, other_ref):
    row, mine = place[0], place[1] >> 1
    clusters, slots = ids.shape
    for which, out in ((mine, mine_ref), (1 - mine, other_ref)):
        for k in range(1, slots):
            name = ids[which, k]
            apart = lax.div(name, clusters) ^ row
            spot = (apart >> 1) * clusters + lax.rem(name, clusters)
            out[k - 1] = jnp.where((apart & 1) > 0, high[spot], low[spot])


def coupling(w_ref, blocks, bases):
    w = jnp.concatenate([w_ref[b] for b in range(4)], axis=1)
    return dot3(w, dot3(jnp.concatenate(blocks, axis=1), jnp.concatenate(bases, axis=0)))


def tall(ref, start):
    return jnp.concatenate([ref[start + i] for i in range(4)], axis=0)


def deal(z, flipped, index, parts):
    quarter = parts[0].shape[1]
    for j, part in enumerate(parts):
        part[index] = flipped[index, pl.ds(pl.multiple_of((z ^ j) * quarter, quarter), quarter), :]


def near_first_kernel(place, count, w_ref, bases, n0, n1, n2, n3, schur, pair, flipped):
    result = coupling(w_ref, [tall(n, 0) for n in (n0, n1, n2, n3)], [bases[j ^ 1] for j in range(4)])
    result = jnp.where(count[place[1] >> 1] > 0, result, 0.0)
    pair[0] = schur[...]
    pair[1] = result
    flipped[...] = result.T


def near_rest_kernel(place, count, w_ref, schur, first, parent, *refs):
    z = place[1]
    blocks, named, parts, flipped = refs[:4], refs[4:8], refs[8:12], refs[12]
    total = named[0].shape[0]
    flipped[0] = schur[...]
    flipped[1] = first[...]
    for k in range(total):
        result = coupling(w_ref, [tall(n, 4 * k) for n in blocks], [s[k] for s in named])
        flipped[k + 2] = jnp.where(count[z >> 1] > k + 1, result, 0.0).T
    flipped[total + 2] = parent[...]
    for i in range(total + 3):
        deal(z, flipped, i, parts)


def finish_kernel(place, *refs):
    row, z = place[0], place[1]
    parts, (diag, near, final) = refs[:4], refs[4:]
    owner = (z & 1) == (row & 1)
    swap = z >> 1
    last = parts[0].shape[0] - 1

    def sides(i):
        return jnp.where(owner, parts[0][i], parts[1][i]), parts[2][i] + parts[3][i]

    for i in range(last):
        for side, value in zip((swap, 1 - swap), sides(i)):
            if i == 0:
                diag[side] = value
            else:
                near[side, i - 1] = value
    here, there = sides(last)
    final[0] = jnp.where(swap == (row & 1), here, there)


def parent_kernel(place, own, arrived, vt_ref, v_ref, flipped_ref):
    size = own.shape[1]
    swap = (place[0] & 1) > 0

    def choose(a, b, index):
        return jnp.where(swap, b[index], a[index])

    top = jnp.concatenate([choose(own, arrived, 0), choose(own, arrived, 1)], axis=1)
    low = jnp.concatenate([choose(arrived, own, 1), choose(arrived, own, 0)], axis=1)
    merged = jnp.concatenate([top, low], axis=0)
    dense = dot(dot(vt_ref[...], merged), v_ref[...])
    flipped_ref[...] = eliminate(dense, size)[1].T


def call(kernel, outs, scalars, arrays, us=2, scratch=()):
    vmem = pl.BlockSpec(memory_space=pltpu.VMEM)
    specs = [pl.BlockSpec(memory_space=pltpu.SMEM)] * len(scalars) + [vmem] * len(arrays)
    shapes = [jax.ShapeDtypeStruct(shape, jnp.float32) for shape in outs]
    cost = pl.CostEstimate(flops=us * 10**9, bytes_accessed=us * 10**6, transcendentals=0)
    return pl.pallas_call(
        kernel,
        out_shape=shapes,
        in_specs=specs,
        out_specs=[vmem] * len(outs),
        scratch_shapes=[pltpu.VMEM(shape, jnp.float32) for shape in scratch],
        cost_estimate=cost,
    )(*scalars, *arrays)


def pick(array, index):
    return lax.dynamic_index_in_dim(array, index, 0, keepdims=False)


def after(values, ready):
    return lax.optimization_barrier((values, ready))[0]


def levels(diag_blocks, near_blocks, cluster_bases, near_ids, near_count, parent_bases):
    clusters, edge, _ = cluster_bases.shape
    slots = near_blocks.shape[1]
    skeleton = K
    n_row, n_col = lax.axis_size("row"), lax.axis_size("col")
    assert n_col == 2 * clusters == 4 and n_row & (n_row - 1) == 0
    quarter = skeleton // n_col
    row, column = lax.axis_index("row"), lax.axis_index("col")
    place = jnp.stack([row, column]).astype(jnp.int32)
    mine, other = column // 2, 1 - column // 2
    both = ("row", "col")
    owned = [(r, z) for r in range(n_row) for z in range(n_col) if z % 2 == r % 2]
    heads = [(r, (n_col - 1) * (r % 2)) for r in range(n_row)]

    def to_owner(x, j):
        return lax.ppermute(x, both, [(r * n_col + (z ^ j), r * n_col + z) for r, z in owned])

    def from_owner(x, j):
        return lax.ppermute(x, both, [(r * n_col + z, r * n_col + (z ^ j)) for r, z in owned])

    def from_sibling(x, places):
        return lax.ppermute(x, both, [((r ^ 1) * n_col + (z ^ 1), r * n_col + z) for r, z in places])

    def across(x, bit):
        return lax.ppermute(x, "row", [(r, r ^ bit) for r in range(n_row)])

    def gather(x, y):
        got = [x]
        for j, payload in enumerate((x, y, y), 1):
            got.append(to_owner(payload, j))
        return got

    def scatter(parts):
        return [parts[0]] + [from_owner(parts[j], j) for j in range(1, 4)]

    full, half, table = call(
        pack_kernel,
        [(8, edge, edge), (6, edge, edge), (clusters, edge, skeleton)],
        [place],
        [diag_blocks, cluster_bases],
    )
    leaf = gather(full, half)

    bits = [1 << t for t in range(1, n_row.bit_length() - 1)]
    for bit in bits:
        table = jnp.concatenate([table, across(table, bit)], axis=0)

    near = near_blocks.reshape(clusters, slots * 4, edge, edge)
    n_mine, n_other = pick(near, mine), pick(near, other)
    ready = after((n_mine[:4], n_other[:4], n_mine[4:], n_other[4:]), leaf[1:])
    n_early, n_late = gather(*ready[:2]), gather(*ready[2:])
    (skeletons,) = call(skeleton_kernel, [(4, edge, skeleton)], [place], leaf)
    sibling = from_sibling(skeletons, owned)

    w, schur = call(
        leaf_kernel, [(4, skeleton, edge), (skeleton, skeleton)], [place], leaf, 22
    )

    pair, first = call(
        near_first_kernel,
        [(2, skeleton, skeleton), (skeleton, skeleton)],
        [place, near_count],
        [w, sibling, *n_early, schur],
        4,
    )
    arrived = from_sibling(pair, heads)

    table = after(table, w)
    s_mine, s_other = call(
        name_kernel,
        [(slots - 1, edge, skeleton)] * 2,
        [place, near_ids],
        [table, across(table, 1)],
    )
    named = gather(*after((s_mine, s_other), pair))

    v = parent_bases[0]
    (parent,) = call(
        parent_kernel, [(skeleton, skeleton)], [place], [pair, arrived, v.T, v], 22
    )
    total = slots + 2
    results = call(
        near_rest_kernel,
        [(total, quarter, skeleton)] * 4,
        [place, near_count],
        [w, schur, first, parent, *n_late, *named],
        7,
        [(total, skeleton, skeleton)],
    )
    turned = call(
        finish_kernel,
        [(clusters, quarter, skeleton), (clusters, slots, quarter, skeleton), (1, quarter, skeleton)],
        [place],
        scatter(results),
    )
    return tuple(jnp.swapaxes(x, -1, -2) for x in turned)


def solution(mesh):
    return jax.shard_map(
        levels,
        mesh=mesh,
        in_specs=(
            P("row", None, "col"),
            P("row", None, None, "col"),
            P("row", "col", None),
            P("row", None),
            P("row"),
            P("row", None, None),
        ),
        out_specs=(P("row", None, "col"), P("row", None, None, "col"), P("row", None, "col")),
        check_vma=False,
    )
```

```python
import jax
import jax.numpy as jnp
from jax import lax
from jax.experimental import pallas as pl
from jax.experimental.pallas import tpu as pltpu
from jax.sharding import PartitionSpec as P


K = 256
PANEL = 8


highest = lax.Precision.HIGHEST


def dot(a, b, left=1, right=0):
    dims = (((left,), (right,)), ((), ()))
    return lax.dot_general(a, b, dims, precision=highest, preferred_element_type=jnp.float32)


def dot3(a, b):
    a_high, b_high = a.astype(jnp.bfloat16), b.astype(jnp.bfloat16)
    a_low = (a - a_high.astype(jnp.float32)).astype(jnp.bfloat16)
    b_low = (b - b_high.astype(jnp.float32)).astype(jnp.bfloat16)

    def product(x, y):
        return jnp.dot(x, y, preferred_element_type=jnp.float32)

    return product(a_high, b_high) + (product(a_high, b_low) + product(a_low, b_high))


def sweep(block):
    size = len(block)
    e = [[block[min(i, j)][max(i, j)] for j in range(size)] for i in range(size)]
    for k in range(size):
        inv = 1.0 / e[k][k]
        t = [e[k][j] * inv for j in range(size)]
        for i in range(size):
            for j in range(i, size):
                if i != k and j != k:
                    e[i][j] = e[i][j] - e[i][k] * t[j]
                    e[j][i] = e[i][j]
        for j in range(size):
            if j != k:
                e[k][j] = e[j][k] = t[j]
        e[k][k] = -inv
    return e


def panel_step(a, lane, sub):
    n = a.shape[0]
    cols = [jnp.broadcast_to(a[:, s : s + 1], (n, n)) for s in range(PANEL)]
    block = [[jnp.broadcast_to(cols[j][i : i + 1], (PANEL, n)) if i <= j else None for j in range(PANEL)] for i in range(PANEL)]
    negated = sweep(block)
    result = jnp.where(lane < PANEL, jnp.where(lane == sub, 1.0, 0.0), a)
    rows = [jnp.broadcast_to(result[t : t + 1], (PANEL, n)) for t in range(PANEL)]
    for s in range(PANEL):
        terms = [negated[s][t] * rows[t] for t in range(PANEL)]
        while len(terms) > 1:
            terms = [terms[i] + terms[i + 1] for i in range(0, len(terms), 2)]
        spread = jnp.concatenate([terms[0]] * (n // PANEL), axis=0)
        top = jnp.where(sub[:PANEL] == s, cols[s][:PANEL] - 1.0, cols[s][:PANEL])
        result = result + jnp.concatenate([top, cols[s][PANEL:]], axis=0) * spread
    return result


def inverse(a):
    n = a.shape[0]
    lane = lax.broadcasted_iota(jnp.int32, (n, n), 1)
    sub = lax.broadcasted_iota(jnp.int32, (n, n), 0)

    def body(_, mat):
        mat = panel_step(mat, lane, sub)
        return pltpu.roll(jnp.concatenate([mat[PANEL:], mat[:PANEL]], axis=0), n - PANEL, 1)

    return lax.fori_loop(0, n // PANEL, body, a)


def solve(corner, right):
    half = corner.shape[0] // 2
    cross, turned = corner[:half, half:], corner[half:, :half]
    first = inverse(corner[:half, :half])
    link, link_turned = dot(first, cross), dot(turned, first)
    second = inverse(corner[half:, half:] - dot(turned, link))
    low = dot(second, right[half:] - dot(link_turned, right[:half]))
    up = dot(first, right[:half]) - dot(link, low)
    return jnp.concatenate([up, low], axis=0)


def eliminate(dense, redundant):
    rr = dense[:redundant, :redundant]
    solved = solve((rr + rr.T) * 0.5, dense[:redundant, redundant:])
    return solved, dense[redundant:, redundant:] - dot(dense[redundant:, :redundant], solved)


def wide(ref, start, count):
    return jnp.concatenate([ref[start + i] for i in range(count)], axis=1)


def leaf_kernel(place, own, near, far2, far3, w_ref, schur_ref):
    z = place[1]
    inner = z & 1
    edge = own.shape[1]
    redundant = 4 * edge - w_ref.shape[1]
    pairs = [jnp.concatenate([own[z ^ m], near[z ^ m]], axis=1) for m in range(4)]
    corner = jnp.concatenate(pairs[:2], axis=0)
    side = jnp.concatenate(pairs[2:], axis=0)
    far = [jnp.concatenate([far2[i], far3[i]], axis=1) for i in (inner, 1 - inner)]
    far = jnp.concatenate(far, axis=0)
    bases = [wide(own, 4, 4), wide(near, 4, 4), wide(far2, 2, 4), wide(far3, 2, 4)]
    u = jnp.concatenate(bases, axis=0)
    ut = u.T
    ut_near, ut_far = ut[:, : 2 * edge], ut[:, 2 * edge :]
    yt_near = dot(ut_near, corner) + dot(ut_far, side)
    yt_far = dot(ut_near, side, 1, 1) + dot(ut_far, far)
    dense = dot(jnp.concatenate([yt_near, yt_far], axis=1), u)
    solved, schur = eliminate(dense, redundant)
    schur_ref[...] = schur
    wt = ut[redundant:] - dot(solved.T, ut[:redundant])
    for m in range(4):
        w_ref[z ^ m] = wt[:, m * edge : (m + 1) * edge]


def pack_kernel(place, diag, bases, full, half, shard):
    edge = bases.shape[1]
    mine = place[1] >> 1
    other = 1 - mine
    for i in range(4):
        lanes = slice(i * edge, (i + 1) * edge)
        full[i] = diag[mine, lanes, :]
        full[4 + i] = bases[mine, :, lanes]
        half[2 + i] = bases[other, :, lanes]
    for i in range(2):
        half[i] = diag[other, pl.ds(pl.multiple_of((2 * mine + i) * edge, edge), edge), :]
    for c in range(bases.shape[0]):
        shard[c] = bases[c, :, bases.shape[2] - shard.shape[2] :]


def skeleton_kernel(place, own, near, far2, far3, out):
    for j, ref in enumerate((own, near, far2, far3)):
        out[j] = wide(ref, ref.shape[0] - 2, 2)


def split_kernel(place, near, v, first_mine, first_other, rest_mine, rest_other, turned):
    mine = place[1] >> 1
    count = first_mine.shape[0]
    turned[...] = v[...].T
    for which, first, rest in ((mine, first_mine, rest_mine), (1 - mine, first_other, rest_other)):
        for i in range(near.shape[1]):
            if i < count:
                first[i] = near[which, i]
            else:
                rest[i - count] = near[which, i]


def name_kernel(place, ids, low0, low1, high0, high1, _, __, rest_mine, rest_other, found, sems):
    row, mine = place[0], place[1] >> 1
    clusters, slots = ids.shape
    edge = found.shape[2]
    copies = []
    for side, (which, rest) in enumerate(((mine, rest_mine), (1 - mine, rest_other))):
        for k in range(1, slots):
            name = ids[which, k]
            apart = lax.div(name, clusters) ^ row
            spot = (apart >> 1) * clusters + lax.rem(name, clusters)
            inner = lax.rem(spot, low0.shape[0])
            late = spot >= low0.shape[0]
            low = jnp.where(late, low1[inner], low0[inner])
            base = jnp.where((apart & 1) > 0, jnp.where(late, high1[inner], high0[inner]), low)
            for b in range(2):
                found[side, 2 * (k - 1) + b] = base[:, b * edge : (b + 1) * edge]
        count = found.shape[1]
        copy = pltpu.make_async_copy(
            found.at[side], rest.at[pl.ds(rest.shape[0] - count, count)], sems.at[side]
        )
        copy.start()
        copies.append(copy)
    for copy in copies:
        copy.wait()


def coupling(w_ref, blocks, bases):
    w = jnp.concatenate([w_ref[b] for b in range(4)], axis=1)
    return dot3(w, dot3(jnp.concatenate(blocks, axis=1), jnp.concatenate(bases, axis=0)))


def tall(ref, start):
    return jnp.concatenate([ref[start + i] for i in range(4)], axis=0)


def deal(z, flipped, index, parts):
    quarter = parts[0].shape[1]
    for j, part in enumerate(parts):
        part[index] = flipped[index, pl.ds(pl.multiple_of((z ^ j) * quarter, quarter), quarter), :]


def near_first_kernel(place, count, w_ref, bases, n0, n1, n2, n3, schur, pair, flipped):
    result = coupling(w_ref, [tall(n, 0) for n in (n0, n1, n2, n3)], [bases[j ^ 1] for j in range(4)])
    result = jnp.where(count[place[1] >> 1] > 0, result, 0.0)
    pair[0] = schur[...]
    pair[1] = result
    flipped[...] = result.T


def near_rest_kernel(place, count, w_ref, schur, first, parent, *refs):
    z = place[1]
    blocks, parts, flipped = refs[:4], refs[4:8], refs[8]
    total = blocks[0].shape[0] // 6
    flipped[0] = schur[...]
    flipped[1] = first[...]
    for k in range(total):
        result = coupling(w_ref, [tall(n, 4 * k) for n in blocks], [wide(n, 4 * total + 2 * k, 2) for n in blocks])
        flipped[k + 2] = jnp.where(count[z >> 1] > k + 1, result, 0.0).T
    flipped[total + 2] = parent[...]
    for i in range(total + 3):
        deal(z, flipped, i, parts)


def finish_kernel(place, *refs):
    row, z = place[0], place[1]
    parts, (diag, near, final) = refs[:4], refs[4:]
    owner = (z & 1) == (row & 1)
    swap = z >> 1
    last = parts[0].shape[0] - 1

    def sides(i):
        return jnp.where(owner, parts[0][i], parts[1][i]), parts[2][i] + parts[3][i]

    for i in range(last):
        for side, value in zip((swap, 1 - swap), sides(i)):
            if i == 0:
                diag[side] = value
            else:
                near[side, i - 1] = value
    here, there = sides(last)
    final[0] = jnp.where(swap == (row & 1), here, there)


def parent_kernel(place, own, arrived, vt_ref, v_ref, flipped_ref):
    size = own.shape[1]
    swap = (place[0] & 1) > 0

    def choose(a, b, index):
        return jnp.where(swap, b[index], a[index])

    top = jnp.concatenate([choose(own, arrived, 0), choose(own, arrived, 1)], axis=1)
    low = jnp.concatenate([choose(arrived, own, 1), choose(arrived, own, 0)], axis=1)
    merged = jnp.concatenate([top, low], axis=0)
    dense = dot(dot(vt_ref[...], merged), v_ref[...])
    flipped_ref[...] = eliminate(dense, size)[1].T


def call(kernel, outs, scalars, arrays, us=2, scratch=()):
    vmem = pl.BlockSpec(memory_space=pltpu.VMEM)
    specs = [pl.BlockSpec(memory_space=pltpu.SMEM)] * len(scalars) + [vmem] * len(arrays)
    shapes = [jax.ShapeDtypeStruct(shape, jnp.float32) for shape in outs]
    cost = pl.CostEstimate(flops=us * 10**9, bytes_accessed=us * 10**6, transcendentals=0)
    return pl.pallas_call(
        kernel,
        out_shape=shapes,
        in_specs=specs,
        out_specs=[vmem] * len(outs),
        scratch_shapes=[pltpu.VMEM(shape, jnp.float32) for shape in scratch],
        cost_estimate=cost,
    )(*scalars, *arrays)


def after(values, ready):
    return lax.optimization_barrier((values, ready))[0]


def levels(diag_blocks, near_blocks, cluster_bases, near_ids, near_count, parent_bases):
    clusters, edge, size = cluster_bases.shape
    slots = near_blocks.shape[1]
    skeleton = K
    n_row, n_col = lax.axis_size("row"), lax.axis_size("col")
    assert n_col == 2 * clusters == 4 and n_row & (n_row - 1) == 0
    quarter = skeleton // n_col
    row, column = lax.axis_index("row"), lax.axis_index("col")
    place = jnp.stack([row, column]).astype(jnp.int32)
    both = ("row", "col")
    owned = [(r, z) for r in range(n_row) for z in range(n_col) if z % 2 == r % 2]
    heads = [(r, (n_col - 1) * (r % 2)) for r in range(n_row)]

    def to_owner(x, j):
        return lax.ppermute(x, both, [(r * n_col + (z ^ j), r * n_col + z) for r, z in owned])

    def from_owner(x, j):
        return lax.ppermute(x, both, [(r * n_col + z, r * n_col + (z ^ j)) for r, z in owned])

    def from_sibling(x, places):
        return lax.ppermute(x, both, [((r ^ 1) * n_col + (z ^ 1), r * n_col + z) for r, z in places])

    def across(x, bit):
        return lax.ppermute(x, "row", [(r, r ^ bit) for r in range(n_row)])

    def gather(x, y):
        got = [x]
        for j, payload in enumerate((x, y, y), 1):
            got.append(to_owner(payload, j))
        return got

    def scatter(parts):
        return [parts[0]] + [from_owner(parts[j], j) for j in range(1, 4)]

    full, half, table = call(
        pack_kernel,
        [(8, edge, edge), (6, edge, edge), (clusters, edge, skeleton)],
        [place],
        [diag_blocks, cluster_bases],
    )
    leaf = gather(full, half)

    bits = [1 << t for t in range(1, n_row.bit_length() - 1)]
    pieces = [table]
    for bit in bits:
        pieces = [jnp.concatenate(pieces, axis=0) if len(pieces) > 1 else table]
        pieces.append(across(pieces[0], bit))

    near = near_blocks.reshape(clusters, slots * 4, edge, edge)
    rest_blocks = (slots - 1) * 6
    v = parent_bases[0]
    split = call(
        split_kernel,
        [(4, edge, edge)] * 2 + [(rest_blocks, edge, edge)] * 2 + [(size, size)],
        [place],
        [near, v],
    )
    anywhere = pl.BlockSpec(memory_space=pl.ANY)
    swapped = [across(piece, 1) for piece in pieces]
    scalar, vmem = pl.BlockSpec(memory_space=pltpu.SMEM), pl.BlockSpec(memory_space=pltpu.VMEM)
    rest = pl.pallas_call(
        name_kernel,
        out_shape=[jax.ShapeDtypeStruct((rest_blocks, edge, edge), jnp.float32)] * 2,
        in_specs=[scalar] * 2 + [vmem] * 4 + [anywhere] * 2,
        out_specs=[anywhere] * 2,
        scratch_shapes=[
            pltpu.VMEM((2, (slots - 1) * 2, edge, edge), jnp.float32),
            pltpu.SemaphoreType.DMA((2,)),
        ],
        input_output_aliases={6: 0, 7: 1},
    )(place, near_ids, *pieces, *swapped, split[2], split[3])
    n_early = gather(*after((split[0], split[1]), leaf[1:]))
    n_rest = gather(*after(rest, leaf[1:]))
    (skeletons,) = call(skeleton_kernel, [(4, edge, skeleton)], [place], leaf)
    sibling = from_sibling(skeletons, owned)

    w, schur = call(
        leaf_kernel, [(4, skeleton, edge), (skeleton, skeleton)], [place], leaf, 22
    )

    pair, first = call(
        near_first_kernel,
        [(2, skeleton, skeleton), (skeleton, skeleton)],
        [place, near_count],
        [w, sibling, *n_early, schur],
        4,
    )
    arrived = from_sibling(pair, heads)

    (parent,) = call(
        parent_kernel, [(skeleton, skeleton)], [place], [pair, arrived, split[4], v], 22
    )
    total = slots + 2
    results = call(
        near_rest_kernel,
        [(total, quarter, skeleton)] * 4,
        [place, near_count],
        [w, schur, first, parent, *n_rest],
        7,
        [(total, skeleton, skeleton)],
    )
    turned = call(
        finish_kernel,
        [(clusters, quarter, skeleton), (clusters, slots, quarter, skeleton), (1, quarter, skeleton)],
        [place],
        scatter(results),
    )
    return tuple(jnp.swapaxes(x, -1, -2) for x in turned)


def solution(mesh):
    return jax.shard_map(
        levels,
        mesh=mesh,
        in_specs=(
            P("row", None, "col"),
            P("row", None, None, "col"),
            P("row", "col", None),
            P("row", None),
            P("row"),
            P("row", None, None),
        ),
        out_specs=(P("row", None, "col"), P("row", None, None, "col"), P("row", None, "col")),
        check_vma=False,
    )
```

```python
import jax
import jax.numpy as jnp
from jax import lax
from jax.experimental import pallas as pl
from jax.experimental.pallas import tpu as pltpu
from jax.sharding import PartitionSpec as P


K = 256
PANEL = 8


highest = lax.Precision.HIGHEST


def dot(a, b, left=1, right=0):
    dims = (((left,), (right,)), ((), ()))
    return lax.dot_general(a, b, dims, precision=highest, preferred_element_type=jnp.float32)


def dot3(a, b):
    a_high, b_high = a.astype(jnp.bfloat16), b.astype(jnp.bfloat16)
    a_low = (a - a_high.astype(jnp.float32)).astype(jnp.bfloat16)
    b_low = (b - b_high.astype(jnp.float32)).astype(jnp.bfloat16)

    def product(x, y):
        return jnp.dot(x, y, preferred_element_type=jnp.float32)

    return product(a_high, b_high) + (product(a_high, b_low) + product(a_low, b_high))


def sweep(block):
    size = len(block)
    e = [[block[min(i, j)][max(i, j)] for j in range(size)] for i in range(size)]
    for k in range(size):
        inv = 1.0 / e[k][k]
        t = [e[k][j] * inv for j in range(size)]
        for i in range(size):
            for j in range(i, size):
                if i != k and j != k:
                    e[i][j] = e[i][j] - e[i][k] * t[j]
                    e[j][i] = e[i][j]
        for j in range(size):
            if j != k:
                e[k][j] = e[j][k] = t[j]
        e[k][k] = -inv
    return e


def panel_step(a, lane, sub):
    n = a.shape[0]
    cols = [jnp.broadcast_to(a[:, s : s + 1], (n, n)) for s in range(PANEL)]
    block = [[jnp.broadcast_to(cols[j][i : i + 1], (PANEL, n)) if i <= j else None for j in range(PANEL)] for i in range(PANEL)]
    negated = sweep(block)
    result = jnp.where(lane < PANEL, jnp.where(lane == sub, 1.0, 0.0), a)
    rows = [jnp.broadcast_to(result[t : t + 1], (PANEL, n)) for t in range(PANEL)]
    for s in range(PANEL):
        terms = [negated[s][t] * rows[t] for t in range(PANEL)]
        while len(terms) > 1:
            terms = [terms[i] + terms[i + 1] for i in range(0, len(terms), 2)]
        spread = jnp.concatenate([terms[0]] * (n // PANEL), axis=0)
        top = jnp.where(sub[:PANEL] == s, cols[s][:PANEL] - 1.0, cols[s][:PANEL])
        result = result + jnp.concatenate([top, cols[s][PANEL:]], axis=0) * spread
    return result


def inverse(a):
    n = a.shape[0]
    lane = lax.broadcasted_iota(jnp.int32, (n, n), 1)
    sub = lax.broadcasted_iota(jnp.int32, (n, n), 0)

    def body(_, mat):
        mat = panel_step(mat, lane, sub)
        return pltpu.roll(jnp.concatenate([mat[PANEL:], mat[:PANEL]], axis=0), n - PANEL, 1)

    return lax.fori_loop(0, n // PANEL, body, a)


def solve(corner, right):
    half = corner.shape[0] // 2
    cross, turned = corner[:half, half:], corner[half:, :half]
    first = inverse(corner[:half, :half])
    link, link_turned = dot(first, cross), dot(turned, first)
    second = inverse(corner[half:, half:] - dot(turned, link))
    low = dot(second, right[half:] - dot(link_turned, right[:half]))
    up = dot(first, right[:half]) - dot(link, low)
    return jnp.concatenate([up, low], axis=0)


def eliminate(dense, redundant):
    rr = dense[:redundant, :redundant]
    solved = solve((rr + rr.T) * 0.5, dense[:redundant, redundant:])
    return solved, dense[redundant:, redundant:] - dot(dense[redundant:, :redundant], solved)


def wide(ref, start, count):
    return jnp.concatenate([ref[start + i] for i in range(count)], axis=1)


def leaf_kernel(place, own, near, far2, far3, w_ref, schur_ref):
    z = place[1]
    inner = z & 1
    edge = own.shape[1]
    redundant = 4 * edge - w_ref.shape[1]
    pairs = [jnp.concatenate([own[z ^ m], near[z ^ m]], axis=1) for m in range(4)]
    corner = jnp.concatenate(pairs[:2], axis=0)
    side = jnp.concatenate(pairs[2:], axis=0)
    far = [jnp.concatenate([far2[i], far3[i]], axis=1) for i in (inner, 1 - inner)]
    far = jnp.concatenate(far, axis=0)
    bases = [wide(own, 4, 4), wide(near, 4, 4), wide(far2, 2, 4), wide(far3, 2, 4)]
    u = jnp.concatenate(bases, axis=0)
    ut = u.T
    ut_near, ut_far = ut[:, : 2 * edge], ut[:, 2 * edge :]
    yt_near = dot(ut_near, corner) + dot(ut_far, side)
    yt_far = dot(ut_near, side, 1, 1) + dot(ut_far, far)
    dense = dot(jnp.concatenate([yt_near, yt_far], axis=1), u)
    solved, schur = eliminate(dense, redundant)
    schur_ref[...] = schur
    wt = ut[redundant:] - dot(solved.T, ut[:redundant])
    for m in range(4):
        w_ref[z ^ m] = wt[:, m * edge : (m + 1) * edge]


def pack_kernel(place, diag, bases, full, half, shard):
    edge = bases.shape[1]
    mine = place[1] >> 1
    other = 1 - mine
    for i in range(4):
        lanes = slice(i * edge, (i + 1) * edge)
        full[i] = diag[mine, lanes, :]
        full[4 + i] = bases[mine, :, lanes]
        half[2 + i] = bases[other, :, lanes]
    for i in range(2):
        half[i] = diag[other, pl.ds(pl.multiple_of((2 * mine + i) * edge, edge), edge), :]
    for c in range(bases.shape[0]):
        shard[c] = bases[c, :, bases.shape[2] - shard.shape[2] :]


def skeleton_kernel(place, own, near, far2, far3, out):
    for j, ref in enumerate((own, near, far2, far3)):
        out[j] = wide(ref, ref.shape[0] - 2, 2)


def split_kernel(place, near, v, first_mine, first_other, rest_mine, rest_other, turned):
    mine = place[1] >> 1
    count = first_mine.shape[0]
    turned[...] = v[...].T
    for which, first, rest in ((mine, first_mine, rest_mine), (1 - mine, first_other, rest_other)):
        for i in range(near.shape[1]):
            if i < count:
                first[i] = near[which, i]
            else:
                rest[i - count] = near[which, i]


def name_kernel(place, ids, low0, low1, high0, high1, mine_ref, other_ref):
    row, mine = place[0], place[1] >> 1
    clusters, slots = ids.shape
    for which, out in ((mine, mine_ref), (1 - mine, other_ref)):
        for k in range(1, slots):
            name = ids[which, k]
            apart = lax.div(name, clusters) ^ row
            spot = (apart >> 1) * clusters + lax.rem(name, clusters)
            inner = lax.rem(spot, low0.shape[0])
            late = spot >= low0.shape[0]
            low = jnp.where(late, low1[inner], low0[inner])
            high = jnp.where(late, high1[inner], high0[inner])
            out[k - 1] = jnp.where((apart & 1) > 0, high, low)


def coupling(w_ref, blocks, bases):
    w = jnp.concatenate([w_ref[b] for b in range(4)], axis=1)
    return dot3(w, dot3(jnp.concatenate(blocks, axis=1), jnp.concatenate(bases, axis=0)))


def tall(ref, start):
    return jnp.concatenate([ref[start + i] for i in range(4)], axis=0)


def deal(z, flipped, index, parts):
    quarter = parts[0].shape[1]
    for j, part in enumerate(parts):
        part[index] = flipped[index, pl.ds(pl.multiple_of((z ^ j) * quarter, quarter), quarter), :]


def near_first_kernel(place, count, w_ref, bases, n0, n1, n2, n3, top, low, flipped):
    result = coupling(w_ref, [tall(n, 0) for n in (n0, n1, n2, n3)], [bases[j ^ 1] for j in range(4)])
    result = jnp.where(count[place[1] >> 1] > 0, result, 0.0)
    half = top.shape[0]
    top[...], low[...] = result[:half], result[half:]
    flipped[...] = result.T


def near_rest_kernel(place, count, w_ref, schur, first, parent, *refs):
    z = place[1]
    blocks, named, parts, flipped = refs[:4], refs[4:8], refs[8:12], refs[12]
    total = named[0].shape[0]
    flipped[0] = schur[...]
    flipped[1] = first[...]
    for k in range(total):
        result = coupling(w_ref, [tall(n, 4 * k) for n in blocks], [s[k] for s in named])
        flipped[k + 2] = jnp.where(count[z >> 1] > k + 1, result, 0.0).T
    flipped[total + 2] = parent[...]
    for i in range(total + 3):
        deal(z, flipped, i, parts)


def finish_kernel(place, *refs):
    row, z = place[0], place[1]
    parts, (diag, near, final) = refs[:4], refs[4:]
    owner = (z & 1) == (row & 1)
    swap = z >> 1
    last = parts[0].shape[0] - 1

    def sides(i):
        return jnp.where(owner, parts[0][i], parts[1][i]), parts[2][i] + parts[3][i]

    for i in range(last):
        for side, value in zip((swap, 1 - swap), sides(i)):
            if i == 0:
                diag[side] = value
            else:
                near[side, i - 1] = value
    here, there = sides(last)
    final[0] = jnp.where(swap == (row & 1), here, there)


def parent_kernel(place, diag, near0, near1, diag_got, near0_got, near1_got, vt_ref, v_ref, flipped_ref):
    size = diag.shape[0]
    swap = (place[0] & 1) > 0
    near = jnp.concatenate([near0[...], near1[...]], axis=0)
    near_got = jnp.concatenate([near0_got[...], near1_got[...]], axis=0)

    def order(a, b):
        return jnp.where(swap, b, a), jnp.where(swap, a, b)

    diag_first, diag_second = order(diag[...], diag_got[...])
    near_first, near_second = order(near, near_got)
    top = jnp.concatenate([diag_first, near_first], axis=1)
    low = jnp.concatenate([near_second, diag_second], axis=1)
    merged = jnp.concatenate([top, low], axis=0)
    dense = dot(dot(vt_ref[...], merged), v_ref[...])
    flipped_ref[...] = eliminate(dense, size)[1].T


def call(kernel, outs, scalars, arrays, us=2, scratch=()):
    vmem = pl.BlockSpec(memory_space=pltpu.VMEM)
    specs = [pl.BlockSpec(memory_space=pltpu.SMEM)] * len(scalars) + [vmem] * len(arrays)
    shapes = [jax.ShapeDtypeStruct(shape, jnp.float32) for shape in outs]
    cost = pl.CostEstimate(flops=us * 10**9, bytes_accessed=us * 10**6, transcendentals=0)
    return pl.pallas_call(
        kernel,
        out_shape=shapes,
        in_specs=specs,
        out_specs=[vmem] * len(outs),
        scratch_shapes=[pltpu.VMEM(shape, jnp.float32) for shape in scratch],
        cost_estimate=cost,
    )(*scalars, *arrays)


def after(values, ready):
    return lax.optimization_barrier((values, ready))[0]


def levels(diag_blocks, near_blocks, cluster_bases, near_ids, near_count, parent_bases):
    clusters, edge, size = cluster_bases.shape
    slots = near_blocks.shape[1]
    skeleton = K
    n_row, n_col = lax.axis_size("row"), lax.axis_size("col")
    assert n_col == 2 * clusters == 4 and n_row & (n_row - 1) == 0
    quarter = skeleton // n_col
    row, column = lax.axis_index("row"), lax.axis_index("col")
    place = jnp.stack([row, column]).astype(jnp.int32)
    both = ("row", "col")
    owned = [(r, z) for r in range(n_row) for z in range(n_col) if z % 2 == r % 2]
    heads = [(r, (n_col - 1) * (r % 2)) for r in range(n_row)]

    def to_owner(x, j):
        return lax.ppermute(x, both, [(r * n_col + (z ^ j), r * n_col + z) for r, z in owned])

    def from_owner(x, j):
        return lax.ppermute(x, both, [(r * n_col + z, r * n_col + (z ^ j)) for r, z in owned])

    def from_sibling(x, places):
        return lax.ppermute(x, both, [((r ^ 1) * n_col + (z ^ 1), r * n_col + z) for r, z in places])

    def across(x, bit):
        return lax.ppermute(x, "row", [(r, r ^ bit) for r in range(n_row)])

    def gather(x, y):
        got = [x]
        for j, payload in enumerate((x, y, y), 1):
            got.append(to_owner(payload, j))
        return got

    def scatter(parts):
        return [parts[0]] + [from_owner(parts[j], j) for j in range(1, 4)]

    full, half, table = call(
        pack_kernel,
        [(8, edge, edge), (6, edge, edge), (clusters, edge, skeleton)],
        [place],
        [diag_blocks, cluster_bases],
    )
    leaf = gather(full, half)

    bits = [1 << t for t in range(1, n_row.bit_length() - 1)]
    pieces = [table]
    for bit in bits:
        pieces = [jnp.concatenate(pieces, axis=0) if len(pieces) > 1 else table]
        pieces.append(across(pieces[0], bit))

    near = near_blocks.reshape(clusters, slots * 4, edge, edge)
    rest_blocks = (slots - 1) * 4
    v = parent_bases[0]
    split = call(
        split_kernel,
        [(4, edge, edge)] * 2 + [(rest_blocks, edge, edge)] * 2 + [(size, size)],
        [place],
        [near, v],
    )
    swapped = []
    for piece in pieces:
        swapped.append(across(piece, 1))
    n_early = gather(*after((split[0], split[1]), leaf[1:]))
    n_rest = gather(*after((split[2], split[3]), leaf[1:]))
    (skeletons,) = call(skeleton_kernel, [(4, edge, skeleton)], [place], leaf)
    sibling = from_sibling(skeletons, owned)

    w, schur = call(
        leaf_kernel, [(4, skeleton, edge), (skeleton, skeleton)], [place], leaf, 22
    )

    diag_got = from_sibling(schur, heads)
    top, low, first = call(
        near_first_kernel,
        [(skeleton // 2, skeleton)] * 2 + [(skeleton, skeleton)],
        [place, near_count],
        [w, sibling, *n_early],
        4,
    )
    top_got = from_sibling(top, heads)
    low_got = from_sibling(low, heads)
    chosen = call(name_kernel, [(slots - 1, edge, skeleton)] * 2, [place, near_ids], [*after(pieces, first), *swapped])
    named = gather(*chosen)
    (parent,) = call(
        parent_kernel,
        [(skeleton, skeleton)],
        [place],
        [schur, top, low, diag_got, top_got, low_got, split[4], v],
        22,
    )
    total = slots + 2
    results = call(
        near_rest_kernel,
        [(total, quarter, skeleton)] * 4,
        [place, near_count],
        [w, schur, first, parent, *n_rest, *named],
        7,
        [(total, skeleton, skeleton)],
    )
    turned = call(
        finish_kernel,
        [(clusters, quarter, skeleton), (clusters, slots, quarter, skeleton), (1, quarter, skeleton)],
        [place],
        scatter(results),
    )
    return tuple(jnp.swapaxes(x, -1, -2) for x in turned)


def solution(mesh):
    return jax.shard_map(
        levels,
        mesh=mesh,
        in_specs=(
            P("row", None, "col"),
            P("row", None, None, "col"),
            P("row", "col", None),
            P("row", None),
            P("row"),
            P("row", None, None),
        ),
        out_specs=(P("row", None, "col"), P("row", None, None, "col"), P("row", None, "col")),
        check_vma=False,
    )
```

```python
import jax
import jax.numpy as jnp
from jax import lax
from jax.experimental import pallas as pl
from jax.experimental.pallas import tpu as pltpu
from jax.sharding import PartitionSpec as P


K = 256
PANEL = 8


highest = lax.Precision.HIGHEST


def dot(a, b, left=1, right=0):
    dims = (((left,), (right,)), ((), ()))
    return lax.dot_general(a, b, dims, precision=highest, preferred_element_type=jnp.float32)


def dot3(a, b):
    a_high, b_high = a.astype(jnp.bfloat16), b.astype(jnp.bfloat16)
    a_low = (a - a_high.astype(jnp.float32)).astype(jnp.bfloat16)
    b_low = (b - b_high.astype(jnp.float32)).astype(jnp.bfloat16)

    def product(x, y):
        return jnp.dot(x, y, preferred_element_type=jnp.float32)

    return product(a_high, b_high) + (product(a_high, b_low) + product(a_low, b_high))


def sweep(block):
    size = len(block)
    e = [[block[min(i, j)][max(i, j)] for j in range(size)] for i in range(size)]
    for k in range(size):
        inv = 1.0 / e[k][k]
        t = [e[k][j] * inv for j in range(size)]
        for i in range(size):
            for j in range(i, size):
                if i != k and j != k:
                    e[i][j] = e[i][j] - e[i][k] * t[j]
                    e[j][i] = e[i][j]
        for j in range(size):
            if j != k:
                e[k][j] = e[j][k] = t[j]
        e[k][k] = -inv
    return e


def panel_step(a, lane, sub):
    n = a.shape[0]
    cols = [jnp.broadcast_to(a[:, s : s + 1], (n, n)) for s in range(PANEL)]
    block = [[jnp.broadcast_to(cols[j][i : i + 1], (PANEL, n)) if i <= j else None for j in range(PANEL)] for i in range(PANEL)]
    negated = sweep(block)
    result = jnp.where(lane < PANEL, jnp.where(lane == sub, 1.0, 0.0), a)
    rows = [jnp.broadcast_to(result[t : t + 1], (PANEL, n)) for t in range(PANEL)]
    for s in range(PANEL):
        terms = [negated[s][t] * rows[t] for t in range(PANEL)]
        while len(terms) > 1:
            terms = [terms[i] + terms[i + 1] for i in range(0, len(terms), 2)]
        spread = jnp.concatenate([terms[0]] * (n // PANEL), axis=0)
        top = jnp.where(sub[:PANEL] == s, cols[s][:PANEL] - 1.0, cols[s][:PANEL])
        result = result + jnp.concatenate([top, cols[s][PANEL:]], axis=0) * spread
    return result


def inverse(a):
    n = a.shape[0]
    lane = lax.broadcasted_iota(jnp.int32, (n, n), 1)
    sub = lax.broadcasted_iota(jnp.int32, (n, n), 0)

    def body(_, mat):
        mat = panel_step(mat, lane, sub)
        return pltpu.roll(jnp.concatenate([mat[PANEL:], mat[:PANEL]], axis=0), n - PANEL, 1)

    return lax.fori_loop(0, n // PANEL, body, a)


def solve(corner, right):
    half = corner.shape[0] // 2
    cross, turned = corner[:half, half:], corner[half:, :half]
    first = inverse(corner[:half, :half])
    link, link_turned = dot(first, cross), dot(turned, first)
    second = inverse(corner[half:, half:] - dot(turned, link))
    low = dot(second, right[half:] - dot(link_turned, right[:half]))
    up = dot(first, right[:half]) - dot(link, low)
    return jnp.concatenate([up, low], axis=0)


def eliminate(dense, redundant):
    rr = dense[:redundant, :redundant]
    solved = solve((rr + rr.T) * 0.5, dense[:redundant, redundant:])
    return solved, dense[redundant:, redundant:] - dot(dense[redundant:, :redundant], solved)


def wide(ref, start, count):
    return jnp.concatenate([ref[start + i] for i in range(count)], axis=1)


def leaf_kernel(place, own, near, far2, far3, w_ref, schur_ref):
    z = place[1]
    inner = z & 1
    edge = own.shape[1]
    redundant = 4 * edge - w_ref.shape[1]
    pairs = [jnp.concatenate([own[z ^ m], near[z ^ m]], axis=1) for m in range(4)]
    corner = jnp.concatenate(pairs[:2], axis=0)
    side = jnp.concatenate(pairs[2:], axis=0)
    far = [jnp.concatenate([far2[i], far3[i]], axis=1) for i in (inner, 1 - inner)]
    far = jnp.concatenate(far, axis=0)
    bases = [wide(own, 4, 4), wide(near, 4, 4), wide(far2, 2, 4), wide(far3, 2, 4)]
    u = jnp.concatenate(bases, axis=0)
    ut = u.T
    left = jnp.concatenate([corner, side], axis=0)
    right = jnp.concatenate([side.T, far], axis=0)
    dense = dot3(dot3(ut, jnp.concatenate([left, right], axis=1)), u)
    solved, schur = eliminate(dense, redundant)
    schur_ref[...] = schur
    wt = ut[redundant:] - dot(solved.T, ut[:redundant])
    for m in range(4):
        w_ref[z ^ m] = wt[:, m * edge : (m + 1) * edge]


def pack_kernel(place, diag, bases, full, half, shard):
    edge = bases.shape[1]
    mine = place[1] >> 1
    other = 1 - mine
    for i in range(4):
        lanes = slice(i * edge, (i + 1) * edge)
        full[i] = diag[mine, lanes, :]
        full[4 + i] = bases[mine, :, lanes]
        half[2 + i] = bases[other, :, lanes]
    for i in range(2):
        half[i] = diag[other, pl.ds(pl.multiple_of((2 * mine + i) * edge, edge), edge), :]
    for c in range(bases.shape[0]):
        shard[c] = bases[c, :, bases.shape[2] - shard.shape[2] :]


def skeleton_kernel(place, own, near, far2, far3, out):
    for j, ref in enumerate((own, near, far2, far3)):
        out[j] = wide(ref, ref.shape[0] - 2, 2)


def split_kernel(place, near, v, first_mine, first_other, rest_mine, rest_other, turned):
    mine = place[1] >> 1
    count = first_mine.shape[0]
    turned[...] = v[...].T
    for which, first, rest in ((mine, first_mine, rest_mine), (1 - mine, first_other, rest_other)):
        for i in range(near.shape[1]):
            if i < count:
                first[i] = near[which, i]
            else:
                rest[i - count] = near[which, i]


def name_kernel(place, ids, low0, low1, high0, high1, mine_ref, other_ref):
    row, mine = place[0], place[1] >> 1
    clusters, slots = ids.shape
    for which, out in ((mine, mine_ref), (1 - mine, other_ref)):
        for k in range(1, slots):
            name = ids[which, k]
            apart = lax.div(name, clusters) ^ row
            spot = (apart >> 1) * clusters + lax.rem(name, clusters)
            inner = lax.rem(spot, low0.shape[0])
            late = spot >= low0.shape[0]
            low = jnp.where(late, low1[inner], low0[inner])
            high = jnp.where(late, high1[inner], high0[inner])
            out[k - 1] = jnp.where((apart & 1) > 0, high, low)


def coupling(w_ref, blocks, bases):
    w = jnp.concatenate([w_ref[b] for b in range(4)], axis=1)
    return dot3(w, dot3(jnp.concatenate(blocks, axis=1), jnp.concatenate(bases, axis=0)))


def tall(ref, start):
    return jnp.concatenate([ref[start + i] for i in range(4)], axis=0)


def deal(z, flipped, index, parts):
    quarter = parts[0].shape[1]
    for j, part in enumerate(parts):
        part[index] = flipped[index, pl.ds(pl.multiple_of((z ^ j) * quarter, quarter), quarter), :]


def near_first_kernel(place, count, w_ref, bases, n0, n1, n2, n3, top, low, flipped):
    result = coupling(w_ref, [tall(n, 0) for n in (n0, n1, n2, n3)], [bases[j ^ 1] for j in range(4)])
    result = jnp.where(count[place[1] >> 1] > 0, result, 0.0)
    half = top.shape[0]
    top[...], low[...] = result[:half], result[half:]
    flipped[...] = result.T


def near_rest_kernel(place, count, w_ref, schur, first, parent, *refs):
    z = place[1]
    blocks, named, parts, flipped = refs[:4], refs[4:8], refs[8:12], refs[12]
    total = named[0].shape[0]
    flipped[0] = schur[...]
    flipped[1] = first[...]
    for k in range(total):
        result = coupling(w_ref, [tall(n, 4 * k) for n in blocks], [s[k] for s in named])
        flipped[k + 2] = jnp.where(count[z >> 1] > k + 1, result, 0.0).T
    flipped[total + 2] = parent[...]
    for i in range(total + 3):
        deal(z, flipped, i, parts)


def finish_kernel(place, *refs):
    row, z = place[0], place[1]
    parts, (diag, near, final) = refs[:4], refs[4:]
    owner = (z & 1) == (row & 1)
    swap = z >> 1
    last = parts[0].shape[0] - 1

    def sides(i):
        return jnp.where(owner, parts[0][i], parts[1][i]), parts[2][i] + parts[3][i]

    for i in range(last):
        for side, value in zip((swap, 1 - swap), sides(i)):
            if i == 0:
                diag[side] = value
            else:
                near[side, i - 1] = value
    here, there = sides(last)
    final[0] = jnp.where(swap == (row & 1), here, there)


def parent_kernel(place, diag, near0, near1, diag_got, near0_got, near1_got, vt_ref, v_ref, flipped_ref):
    size = diag.shape[0]
    swap = (place[0] & 1) > 0
    near = jnp.concatenate([near0[...], near1[...]], axis=0)
    near_got = jnp.concatenate([near0_got[...], near1_got[...]], axis=0)

    def order(a, b):
        return jnp.where(swap, b, a), jnp.where(swap, a, b)

    diag_first, diag_second = order(diag[...], diag_got[...])
    near_first, near_second = order(near, near_got)
    top = jnp.concatenate([diag_first, near_first], axis=1)
    low = jnp.concatenate([near_second, diag_second], axis=1)
    merged = jnp.concatenate([top, low], axis=0)
    dense = dot3(dot3(vt_ref[...], merged), v_ref[...])
    flipped_ref[...] = eliminate(dense, size)[1].T


def call(kernel, outs, scalars, arrays, us=2, scratch=()):
    vmem = pl.BlockSpec(memory_space=pltpu.VMEM)
    specs = [pl.BlockSpec(memory_space=pltpu.SMEM)] * len(scalars) + [vmem] * len(arrays)
    shapes = [jax.ShapeDtypeStruct(shape, jnp.float32) for shape in outs]
    cost = pl.CostEstimate(flops=us * 10**9, bytes_accessed=us * 10**6, transcendentals=0)
    return pl.pallas_call(
        kernel,
        out_shape=shapes,
        in_specs=specs,
        out_specs=[vmem] * len(outs),
        scratch_shapes=[pltpu.VMEM(shape, jnp.float32) for shape in scratch],
        cost_estimate=cost,
    )(*scalars, *arrays)


def after(values, ready):
    return lax.optimization_barrier((values, ready))[0]


def levels(diag_blocks, near_blocks, cluster_bases, near_ids, near_count, parent_bases):
    clusters, edge, size = cluster_bases.shape
    slots = near_blocks.shape[1]
    skeleton = K
    n_row, n_col = lax.axis_size("row"), lax.axis_size("col")
    assert n_col == 2 * clusters == 4 and n_row & (n_row - 1) == 0
    quarter = skeleton // n_col
    row, column = lax.axis_index("row"), lax.axis_index("col")
    place = jnp.stack([row, column]).astype(jnp.int32)
    both = ("row", "col")
    owned = [(r, z) for r in range(n_row) for z in range(n_col) if z % 2 == r % 2]
    heads = [(r, (n_col - 1) * (r % 2)) for r in range(n_row)]

    def to_owner(x, j):
        return lax.ppermute(x, both, [(r * n_col + (z ^ j), r * n_col + z) for r, z in owned])

    def from_owner(x, j):
        return lax.ppermute(x, both, [(r * n_col + z, r * n_col + (z ^ j)) for r, z in owned])

    def from_sibling(x, places):
        return lax.ppermute(x, both, [((r ^ 1) * n_col + (z ^ 1), r * n_col + z) for r, z in places])

    def across(x, bit):
        return lax.ppermute(x, "row", [(r, r ^ bit) for r in range(n_row)])

    def gather(x, y):
        got = [x]
        for j, payload in enumerate((x, y, y), 1):
            got.append(to_owner(payload, j))
        return got

    def scatter(parts):
        return [parts[0]] + [from_owner(parts[j], j) for j in range(1, 4)]

    full, half, table = call(
        pack_kernel,
        [(8, edge, edge), (6, edge, edge), (clusters, edge, skeleton)],
        [place],
        [diag_blocks, cluster_bases],
    )
    leaf = gather(full, half)

    bits = [1 << t for t in range(1, n_row.bit_length() - 1)]
    pieces = [table]
    for bit in bits:
        pieces = [jnp.concatenate(pieces, axis=0) if len(pieces) > 1 else table]
        pieces.append(across(pieces[0], bit))

    near = near_blocks.reshape(clusters, slots * 4, edge, edge)
    rest_blocks = (slots - 1) * 4
    v = parent_bases[0]
    split = call(
        split_kernel,
        [(4, edge, edge)] * 2 + [(rest_blocks, edge, edge)] * 2 + [(size, size)],
        [place],
        [near, v],
    )
    swapped = []
    for piece in pieces:
        swapped.append(across(piece, 1))
    n_early = gather(*after((split[0], split[1]), leaf[1:]))
    n_rest = gather(*after((split[2], split[3]), leaf[1:]))
    (skeletons,) = call(skeleton_kernel, [(4, edge, skeleton)], [place], leaf)
    sibling = from_sibling(skeletons, owned)

    w, schur = call(
        leaf_kernel, [(4, skeleton, edge), (skeleton, skeleton)], [place], leaf, 22
    )

    diag_got = from_sibling(schur, heads)
    top, low, first = call(
        near_first_kernel,
        [(skeleton // 2, skeleton)] * 2 + [(skeleton, skeleton)],
        [place, near_count],
        [w, sibling, *n_early],
        4,
    )
    top_got = from_sibling(top, heads)
    low_got = from_sibling(low, heads)
    chosen = call(name_kernel, [(slots - 1, edge, skeleton)] * 2, [place, near_ids], [*after(pieces, first), *swapped])
    named = gather(*chosen)
    (parent,) = call(
        parent_kernel,
        [(skeleton, skeleton)],
        [place],
        [schur, top, low, diag_got, top_got, low_got, split[4], v],
        22,
    )
    total = slots + 2
    results = call(
        near_rest_kernel,
        [(total, quarter, skeleton)] * 4,
        [place, near_count],
        [w, schur, first, parent, *n_rest, *named],
        7,
        [(total, skeleton, skeleton)],
    )
    turned = call(
        finish_kernel,
        [(clusters, quarter, skeleton), (clusters, slots, quarter, skeleton), (1, quarter, skeleton)],
        [place],
        scatter(results),
    )
    return tuple(jnp.swapaxes(x, -1, -2) for x in turned)


def solution(mesh):
    return jax.shard_map(
        levels,
        mesh=mesh,
        in_specs=(
            P("row", None, "col"),
            P("row", None, None, "col"),
            P("row", "col", None),
            P("row", None),
            P("row"),
            P("row", None, None),
        ),
        out_specs=(P("row", None, "col"), P("row", None, None, "col"), P("row", None, "col")),
        check_vma=False,
    )
```

```python
import jax
import jax.numpy as jnp
from jax import lax
from jax.experimental import pallas as pl
from jax.experimental.pallas import tpu as pltpu
from jax.sharding import PartitionSpec as P


K = 256
PANEL = 8


highest = lax.Precision.HIGHEST


def dot(a, b, left=1, right=0):
    dims = (((left,), (right,)), ((), ()))
    return lax.dot_general(a, b, dims, precision=highest, preferred_element_type=jnp.float32)


def dot3(a, b):
    a_high, b_high = a.astype(jnp.bfloat16), b.astype(jnp.bfloat16)
    a_low = (a - a_high.astype(jnp.float32)).astype(jnp.bfloat16)
    b_low = (b - b_high.astype(jnp.float32)).astype(jnp.bfloat16)

    def product(x, y):
        return jnp.dot(x, y, preferred_element_type=jnp.float32)

    return product(a_high, b_high) + (product(a_high, b_low) + product(a_low, b_high))


def sweep(block):
    size = len(block)
    e = [[block[min(i, j)][max(i, j)] for j in range(size)] for i in range(size)]
    for k in range(size):
        inv = 1.0 / e[k][k]
        t = [e[k][j] * inv for j in range(size)]
        for i in range(size):
            for j in range(i, size):
                if i != k and j != k:
                    e[i][j] = e[i][j] - e[i][k] * t[j]
                    e[j][i] = e[i][j]
        for j in range(size):
            if j != k:
                e[k][j] = e[j][k] = t[j]
        e[k][k] = -inv
    return e


def panel_step(a, lane, sub):
    n = a.shape[0]
    cols = [jnp.broadcast_to(a[:, s : s + 1], (n, n)) for s in range(PANEL)]
    block = [[jnp.broadcast_to(cols[j][i : i + 1], (PANEL, n)) if i <= j else None for j in range(PANEL)] for i in range(PANEL)]
    negated = sweep(block)
    result = jnp.where(lane < PANEL, jnp.where(lane == sub, 1.0, 0.0), a)
    rows = [jnp.broadcast_to(result[t : t + 1], (PANEL, n)) for t in range(PANEL)]
    for s in range(PANEL):
        terms = [negated[s][t] * rows[t] for t in range(PANEL)]
        while len(terms) > 1:
            terms = [terms[i] + terms[i + 1] for i in range(0, len(terms), 2)]
        spread = jnp.concatenate([terms[0]] * (n // PANEL), axis=0)
        top = jnp.where(sub[:PANEL] == s, cols[s][:PANEL] - 1.0, cols[s][:PANEL])
        result = result + jnp.concatenate([top, cols[s][PANEL:]], axis=0) * spread
    return result


def inverse(a):
    n = a.shape[0]
    lane = lax.broadcasted_iota(jnp.int32, (n, n), 1)
    sub = lax.broadcasted_iota(jnp.int32, (n, n), 0)

    def body(_, mat):
        mat = panel_step(mat, lane, sub)
        return pltpu.roll(jnp.concatenate([mat[PANEL:], mat[:PANEL]], axis=0), n - PANEL, 1)

    return lax.fori_loop(0, n // PANEL, body, a)


def solve(corner, right):
    half = corner.shape[0] // 2
    cross, turned = corner[:half, half:], corner[half:, :half]
    first = inverse(corner[:half, :half])
    link, link_turned = dot(first, cross), dot(turned, first)
    second = inverse(corner[half:, half:] - dot(turned, link))
    low = dot(second, right[half:] - dot(link_turned, right[:half]))
    up = dot(first, right[:half]) - dot(link, low)
    return jnp.concatenate([up, low], axis=0)


def eliminate(dense, redundant):
    rr = dense[:redundant, :redundant]
    solved = solve((rr + rr.T) * 0.5, dense[:redundant, redundant:])
    return solved, dense[redundant:, redundant:] - dot(dense[redundant:, :redundant], solved)


def wide(ref, start, count):
    return jnp.concatenate([ref[start + i] for i in range(count)], axis=1)


def leaf_kernel(place, own, near, far2, far3, w_ref, schur_ref):
    z = place[1]
    inner = z & 1
    edge = own.shape[1]
    redundant = 4 * edge - w_ref.shape[1]
    pairs = [jnp.concatenate([own[z ^ m], near[z ^ m]], axis=1) for m in range(4)]
    corner = jnp.concatenate(pairs[:2], axis=0)
    side = jnp.concatenate(pairs[2:], axis=0)
    far = [jnp.concatenate([far2[i], far3[i]], axis=1) for i in (inner, 1 - inner)]
    far = jnp.concatenate(far, axis=0)
    bases = [wide(own, 4, 4), wide(near, 4, 4), wide(far2, 2, 4), wide(far3, 2, 4)]
    u = jnp.concatenate(bases, axis=0)
    ut = u.T
    left = jnp.concatenate([corner, side], axis=0)
    right = jnp.concatenate([side.T, far], axis=0)
    dense = dot3(dot3(ut, jnp.concatenate([left, right], axis=1)), u)
    solved, schur = eliminate(dense, redundant)
    schur_ref[...] = schur
    wt = ut[redundant:] - dot(solved.T, ut[:redundant])
    for m in range(4):
        w_ref[z ^ m] = wt[:, m * edge : (m + 1) * edge]


def pack_kernel(place, diag, bases, full, half, shard):
    edge = bases.shape[1]
    mine = place[1] >> 1
    other = 1 - mine
    for i in range(4):
        lanes = slice(i * edge, (i + 1) * edge)
        full[i] = diag[mine, lanes, :]
        full[4 + i] = bases[mine, :, lanes]
        half[2 + i] = bases[other, :, lanes]
    for i in range(2):
        half[i] = diag[other, pl.ds(pl.multiple_of((2 * mine + i) * edge, edge), edge), :]
    for c in range(bases.shape[0]):
        shard[c] = bases[c, :, bases.shape[2] - shard.shape[2] :]


def skeleton_kernel(place, own, near, far2, far3, out):
    for j, ref in enumerate((own, near, far2, far3)):
        out[j] = wide(ref, ref.shape[0] - 2, 2)


def split_kernel(place, near, v, first_mine, first_other, rest_mine, rest_other, turned):
    mine = place[1] >> 1
    count = first_mine.shape[0]
    turned[...] = v[...].T
    for which, first, rest in ((mine, first_mine, rest_mine), (1 - mine, first_other, rest_other)):
        for i in range(near.shape[1]):
            if i < count:
                first[i] = near[which, i]
            else:
                rest[i - count] = near[which, i]


def name_kernel(place, ids, low0, low1, high0, high1, mine_ref, other_ref):
    row, mine = place[0], place[1] >> 1
    clusters, slots = ids.shape
    for which, out in ((mine, mine_ref), (1 - mine, other_ref)):
        for k in range(1, slots):
            name = ids[which, k]
            apart = lax.div(name, clusters) ^ row
            spot = (apart >> 1) * clusters + lax.rem(name, clusters)
            inner = lax.rem(spot, low0.shape[0])
            late = spot >= low0.shape[0]
            low = jnp.where(late, low1[inner], low0[inner])
            high = jnp.where(late, high1[inner], high0[inner])
            out[k - 1] = jnp.where((apart & 1) > 0, high, low)


def coupling(w_ref, blocks, bases):
    w = jnp.concatenate([w_ref[b] for b in range(4)], axis=1)
    return dot3(w, dot3(jnp.concatenate(blocks, axis=1), jnp.concatenate(bases, axis=0)))


def tall(ref, start):
    return jnp.concatenate([ref[start + i] for i in range(4)], axis=0)


def deal(z, flipped, index, parts):
    quarter = parts[0].shape[1]
    for j, part in enumerate(parts):
        part[index] = flipped[index, pl.ds(pl.multiple_of((z ^ j) * quarter, quarter), quarter), :]


def near_first_kernel(place, count, w_ref, bases, n0, n1, n2, n3, schur, top, low, flipped, pair):
    result = coupling(w_ref, [tall(n, 0) for n in (n0, n1, n2, n3)], [bases[j ^ 1] for j in range(4)])
    result = jnp.where(count[place[1] >> 1] > 0, result, 0.0)
    half = top.shape[0]
    top[...], low[...] = result[:half], result[half:]
    pair[0], pair[1] = schur[...], result
    flipped[...] = result.T


def near_rest_kernel(place, count, w_ref, schur, first, *refs):
    row, z = place[0], place[1]
    blocks, named, parts, flipped = refs[:4], refs[4:8], refs[8:12], refs[12]
    total = named[0].shape[0]

    @pl.when((z & 1) == (row & 1))
    def _():
        flipped[0] = schur[...]
        flipped[1] = first[...]
        for k in range(total):
            result = coupling(w_ref, [tall(n, 4 * k) for n in blocks], [s[k] for s in named])
            flipped[k + 2] = jnp.where(count[z >> 1] > k + 1, result, 0.0).T
        for i in range(total + 2):
            deal(z, flipped, i, parts)


def finish_kernel(place, *refs):
    row, z = place[0], place[1]
    parts, crown, (diag, near, final) = refs[:4], refs[4:8], refs[8:]
    owner = (z & 1) == (row & 1)
    swap = z >> 1
    for i in range(parts[0].shape[0]):
        here = jnp.where(owner, parts[0][i], parts[1][i])
        there = parts[2][i] + parts[3][i]
        for side, value in ((swap, here), (1 - swap, there)):
            if i == 0:
                diag[side] = value
            else:
                near[side, i - 1] = value
    arrived = crown[1][0] + (crown[2][0] + crown[3][0])
    final[0] = jnp.where(z == 1 + (row & 1), crown[0][0], arrived)


def parent_kernel(place, diag, near0, near1, pair, vt_ref, v_ref, p0, p1, p2, p3, flipped):
    row, z = place[0], place[1]
    size = diag.shape[0]

    @pl.when(z == 1 + (row & 1))
    def _():
        swap = (row & 1) > 0
        near = jnp.concatenate([near0[...], near1[...]], axis=0)

        def order(a, b):
            return jnp.where(swap, b, a), jnp.where(swap, a, b)

        diag_first, diag_second = order(diag[...], pair[0])
        near_first, near_second = order(near, pair[1])
        top = jnp.concatenate([diag_first, near_first], axis=1)
        low = jnp.concatenate([near_second, diag_second], axis=1)
        merged = jnp.concatenate([top, low], axis=0)
        dense = dot3(dot3(vt_ref[...], merged), v_ref[...])
        flipped[0] = eliminate(dense, size)[1].T
        deal(z, flipped, 0, (p0, p1, p2, p3))


def call(kernel, outs, scalars, arrays, us=2, scratch=()):
    vmem = pl.BlockSpec(memory_space=pltpu.VMEM)
    specs = [pl.BlockSpec(memory_space=pltpu.SMEM)] * len(scalars) + [vmem] * len(arrays)
    shapes = [jax.ShapeDtypeStruct(shape, jnp.float32) for shape in outs]
    cost = pl.CostEstimate(flops=us * 10**9, bytes_accessed=us * 10**6, transcendentals=0)
    return pl.pallas_call(
        kernel,
        out_shape=shapes,
        in_specs=specs,
        out_specs=[vmem] * len(outs),
        scratch_shapes=[pltpu.VMEM(shape, jnp.float32) for shape in scratch],
        cost_estimate=cost,
    )(*scalars, *arrays)


def after(values, ready):
    return lax.optimization_barrier((values, ready))[0]


def levels(diag_blocks, near_blocks, cluster_bases, near_ids, near_count, parent_bases):
    clusters, edge, size = cluster_bases.shape
    slots = near_blocks.shape[1]
    skeleton = K
    n_row, n_col = lax.axis_size("row"), lax.axis_size("col")
    assert n_col == 2 * clusters == 4 and n_row & (n_row - 1) == 0
    quarter = skeleton // n_col
    row, column = lax.axis_index("row"), lax.axis_index("col")
    place = jnp.stack([row, column]).astype(jnp.int32)
    both = ("row", "col")
    owned = [(r, z) for r in range(n_row) for z in range(n_col) if z % 2 == r % 2]
    heads = [(r, 1 + r % 2) for r in range(n_row)]

    def to_owner(x, j):
        return lax.ppermute(x, both, [(r * n_col + (z ^ j), r * n_col + z) for r, z in owned])

    def from_owner(x, j):
        return lax.ppermute(x, both, [(r * n_col + z, r * n_col + (z ^ j)) for r, z in owned])

    def from_sibling(x):
        return lax.ppermute(x, both, [((r ^ 1) * n_col + (z ^ 1), r * n_col + z) for r, z in owned])

    def from_neighbour(x):
        return lax.ppermute(x, both, [(r * n_col + (z ^ 1), r * n_col + z) for r, z in heads])

    def from_chip(x):
        return lax.ppermute(x, both, [((r ^ 1) * n_col + z, r * n_col + z) for r, z in heads])

    def from_head(x, j):
        return lax.ppermute(x, both, [(r * n_col + z, r * n_col + (z ^ j)) for r, z in heads])

    def across(x, bit):
        return lax.ppermute(x, "row", [(r, r ^ bit) for r in range(n_row)])

    def gather(x, y):
        got = [x]
        for j, payload in enumerate((x, y, y), 1):
            got.append(to_owner(payload, j))
        return got

    def scatter(parts, send):
        got = [parts[0]]
        for j in range(1, 4):
            got.append(send(parts[j], j))
        return got

    full, half, table = call(
        pack_kernel,
        [(8, edge, edge), (6, edge, edge), (clusters, edge, skeleton)],
        [place],
        [diag_blocks, cluster_bases],
    )
    leaf = gather(full, half)

    bits = [1 << t for t in range(1, n_row.bit_length() - 1)]
    pieces = [table]
    for bit in bits:
        pieces = [jnp.concatenate(pieces, axis=0) if len(pieces) > 1 else table]
        pieces.append(across(pieces[0], bit))

    near = near_blocks.reshape(clusters, slots * 4, edge, edge)
    rest_blocks = (slots - 1) * 4
    v = parent_bases[0]
    split = call(
        split_kernel,
        [(4, edge, edge)] * 2 + [(rest_blocks, edge, edge)] * 2 + [(size, size)],
        [place],
        [near, v],
    )
    swapped = []
    for piece in pieces:
        swapped.append(across(piece, 1))
    n_early = gather(*after((split[0], split[1]), leaf[1:]))
    n_rest = gather(*after((split[2], split[3]), leaf[1:]))
    (skeletons,) = call(skeleton_kernel, [(4, edge, skeleton)], [place], leaf)
    sibling = from_sibling(skeletons)

    w, schur = call(
        leaf_kernel, [(4, skeleton, edge), (skeleton, skeleton)], [place], leaf, 22
    )

    diag_got = from_neighbour(schur)
    top, low, first, pair = call(
        near_first_kernel,
        [(skeleton // 2, skeleton)] * 2 + [(skeleton, skeleton), (2, skeleton, skeleton)],
        [place, near_count],
        [w, sibling, *n_early, schur],
        4,
    )
    top_got = from_neighbour(top)
    low_got = from_neighbour(low)
    pair_got = from_chip(pair)
    chosen = call(
        name_kernel,
        [(slots - 1, edge, skeleton)] * 2,
        [place, near_ids],
        [*after(pieces, first), *swapped],
    )
    named = gather(*chosen)
    crown = call(
        parent_kernel,
        [(1, quarter, skeleton)] * 4,
        [place],
        [diag_got, top_got, low_got, pair_got, split[4], v],
        20,
        [(1, skeleton, skeleton)],
    )
    total = slots + 1
    results = call(
        near_rest_kernel,
        [(total, quarter, skeleton)] * 4,
        [place, near_count],
        [w, schur, first, *n_rest, *named],
        7,
        [(total, skeleton, skeleton)],
    )
    turned = call(
        finish_kernel,
        [(clusters, quarter, skeleton), (clusters, slots, quarter, skeleton), (1, quarter, skeleton)],
        [place],
        scatter(results, from_owner) + scatter(crown, from_head),
    )
    return tuple(jnp.swapaxes(x, -1, -2) for x in turned)


def solution(mesh):
    return jax.shard_map(
        levels,
        mesh=mesh,
        in_specs=(
            P("row", None, "col"),
            P("row", None, None, "col"),
            P("row", "col", None),
            P("row", None),
            P("row"),
            P("row", None, None),
        ),
        out_specs=(P("row", None, "col"), P("row", None, None, "col"), P("row", None, "col")),
        check_vma=False,
    )
```

```python
import jax
import jax.numpy as jnp
from jax import lax
from jax.experimental import pallas as pl
from jax.experimental.pallas import tpu as pltpu
from jax.sharding import PartitionSpec as P


K = 256
PANEL = 8


highest = lax.Precision.HIGHEST


def dot(a, b, left=1, right=0):
    dims = (((left,), (right,)), ((), ()))
    return lax.dot_general(a, b, dims, precision=highest, preferred_element_type=jnp.float32)


def dot3(a, b):
    a_high, b_high = a.astype(jnp.bfloat16), b.astype(jnp.bfloat16)
    a_low = (a - a_high.astype(jnp.float32)).astype(jnp.bfloat16)
    b_low = (b - b_high.astype(jnp.float32)).astype(jnp.bfloat16)

    def product(x, y):
        return jnp.dot(x, y, preferred_element_type=jnp.float32)

    return product(a_high, b_high) + (product(a_high, b_low) + product(a_low, b_high))


def sweep(block):
    size = len(block)
    e = [[block[min(i, j)][max(i, j)] for j in range(size)] for i in range(size)]
    for k in range(size):
        inv = 1.0 / e[k][k]
        t = [e[k][j] * inv for j in range(size)]
        for i in range(size):
            for j in range(i, size):
                if i != k and j != k:
                    e[i][j] = e[i][j] - e[i][k] * t[j]
                    e[j][i] = e[i][j]
        for j in range(size):
            if j != k:
                e[k][j] = e[j][k] = t[j]
        e[k][k] = -inv
    return e


def panel_step(a, lane, sub):
    n = a.shape[0]
    cols = [jnp.broadcast_to(a[:, s : s + 1], (n, n)) for s in range(PANEL)]
    block = [[jnp.broadcast_to(cols[j][i : i + 1], (PANEL, n)) if i <= j else None for j in range(PANEL)] for i in range(PANEL)]
    negated = sweep(block)
    result = jnp.where(lane < PANEL, jnp.where(lane == sub, 1.0, 0.0), a)
    rows = [jnp.broadcast_to(result[t : t + 1], (PANEL, n)) for t in range(PANEL)]
    for s in range(PANEL):
        terms = [negated[s][t] * rows[t] for t in range(PANEL)]
        while len(terms) > 1:
            terms = [terms[i] + terms[i + 1] for i in range(0, len(terms), 2)]
        spread = jnp.concatenate([terms[0]] * (n // PANEL), axis=0)
        top = jnp.where(sub[:PANEL] == s, cols[s][:PANEL] - 1.0, cols[s][:PANEL])
        result = result + jnp.concatenate([top, cols[s][PANEL:]], axis=0) * spread
    return result


def inverse(a):
    n = a.shape[0]
    lane = lax.broadcasted_iota(jnp.int32, (n, n), 1)
    sub = lax.broadcasted_iota(jnp.int32, (n, n), 0)

    def body(_, mat):
        mat = panel_step(mat, lane, sub)
        return pltpu.roll(jnp.concatenate([mat[PANEL:], mat[:PANEL]], axis=0), n - PANEL, 1)

    return lax.fori_loop(0, n // PANEL, body, a)


def solve(corner, right):
    half = corner.shape[0] // 2
    cross, turned = corner[:half, half:], corner[half:, :half]
    first = inverse(corner[:half, :half])
    link, link_turned = dot(first, cross), dot(turned, first)
    second = inverse(corner[half:, half:] - dot(turned, link))
    low = dot(second, right[half:] - dot(link_turned, right[:half]))
    up = dot(first, right[:half]) - dot(link, low)
    return jnp.concatenate([up, low], axis=0)


def eliminate(dense, redundant):
    rr = dense[:redundant, :redundant]
    solved = solve((rr + rr.T) * 0.5, dense[:redundant, redundant:])
    return solved, dense[redundant:, redundant:] - dot(dense[redundant:, :redundant], solved)


def wide(ref, start, count):
    return jnp.concatenate([ref[start + i] for i in range(count)], axis=1)


def leaf_kernel(place, own, near, far2, far3, w_ref, schur_ref):
    z = place[1]
    inner = z & 1
    edge = own.shape[1]
    redundant = 4 * edge - w_ref.shape[1]
    pairs = [jnp.concatenate([own[z ^ m], near[z ^ m]], axis=1) for m in range(4)]
    corner = jnp.concatenate(pairs[:2], axis=0)
    side = jnp.concatenate(pairs[2:], axis=0)
    far = [jnp.concatenate([far2[i], far3[i]], axis=1) for i in (inner, 1 - inner)]
    far = jnp.concatenate(far, axis=0)
    bases = [wide(own, 4, 4), wide(near, 4, 4), wide(far2, 2, 4), wide(far3, 2, 4)]
    u = jnp.concatenate(bases, axis=0)
    ut = u.T
    left = jnp.concatenate([corner, side], axis=0)
    right = jnp.concatenate([side.T, far], axis=0)
    dense = dot3(dot3(ut, jnp.concatenate([left, right], axis=1)), u)
    solved, schur = eliminate(dense, redundant)
    schur_ref[...] = schur
    wt = ut[redundant:] - dot(solved.T, ut[:redundant])
    for m in range(4):
        w_ref[z ^ m] = wt[:, m * edge : (m + 1) * edge]


def pack_kernel(place, diag, bases, full, half, shard):
    edge = bases.shape[1]
    mine = place[1] >> 1
    other = 1 - mine
    for i in range(4):
        lanes = slice(i * edge, (i + 1) * edge)
        full[i] = diag[mine, lanes, :]
        full[4 + i] = bases[mine, :, lanes]
        half[2 + i] = bases[other, :, lanes]
    for i in range(2):
        half[i] = diag[other, pl.ds(pl.multiple_of((2 * mine + i) * edge, edge), edge), :]
    for c in range(bases.shape[0]):
        shard[c] = bases[c, :, bases.shape[2] - shard.shape[2] :]


def skeleton_kernel(place, own, near, far2, far3, out):
    for j, ref in enumerate((own, near, far2, far3)):
        out[j] = wide(ref, ref.shape[0] - 2, 2)


def split_kernel(place, near, v, first_mine, first_other, rest_mine, rest_other, turned):
    mine = place[1] >> 1
    count = first_mine.shape[0]
    turned[...] = v[...].T
    for which, first, rest in ((mine, first_mine, rest_mine), (1 - mine, first_other, rest_other)):
        for i in range(near.shape[1]):
            if i < count:
                first[i] = near[which, i]
            else:
                rest[i - count] = near[which, i]


def name_kernel(place, ids, low0, low1, high0, high1, mine_ref, other_ref):
    row, mine = place[0], place[1] >> 1
    clusters, slots = ids.shape
    for which, out in ((mine, mine_ref), (1 - mine, other_ref)):
        for k in range(1, slots):
            name = ids[which, k]
            apart = lax.div(name, clusters) ^ row
            spot = (apart >> 1) * clusters + lax.rem(name, clusters)
            inner = lax.rem(spot, low0.shape[0])
            late = spot >= low0.shape[0]
            low = jnp.where(late, low1[inner], low0[inner])
            high = jnp.where(late, high1[inner], high0[inner])
            out[k - 1] = jnp.where((apart & 1) > 0, high, low)


def coupling(w_ref, blocks, bases):
    w = jnp.concatenate([w_ref[b] for b in range(4)], axis=1)
    return dot3(w, dot3(jnp.concatenate(blocks, axis=1), jnp.concatenate(bases, axis=0)))


def tall(ref, start):
    return jnp.concatenate([ref[start + i] for i in range(4)], axis=0)


def deal(z, flipped, index, parts):
    quarter = parts[0].shape[1]
    for j, part in enumerate(parts):
        part[index] = flipped[index, pl.ds(pl.multiple_of((z ^ j) * quarter, quarter), quarter), :]


def near_first_kernel(place, count, w_ref, bases, n0, n1, n2, n3, schur, top, low, flipped, pair):
    result = coupling(w_ref, [tall(n, 0) for n in (n0, n1, n2, n3)], [bases[j ^ 1] for j in range(4)])
    result = jnp.where(count[place[1] >> 1] > 0, result, 0.0)
    half = top.shape[0]
    top[...], low[...] = result[:half], result[half:]
    pair[0], pair[1] = schur[...], result
    flipped[...] = result.T


def near_rest_kernel(place, count, w_ref, schur, first, *refs):
    row, z = place[0], place[1]
    blocks, named, parts = refs[:4], refs[4:8], refs[8:12]
    flipped, block_buffer, base_buffer, sems = refs[12:]
    total = named[0].shape[0]

    @pl.when((z & 1) == (row & 1))
    def _():
        copies = []
        for k in range(total):
            for j in range(4):
                tile = pl.ds(4 * k, 4)
                copies.append(
                    pltpu.make_async_copy(blocks[j].at[tile], block_buffer.at[j, tile], sems.at[k, j, 0])
                )
                copies.append(
                    pltpu.make_async_copy(named[j].at[k], base_buffer.at[j, k], sems.at[k, j, 1])
                )
        for copy in copies:
            copy.start()
        flipped[0] = schur[...]
        flipped[1] = first[...]
        for i in range(2):
            deal(z, flipped, i, parts)
        for k in range(total):
            for copy in copies[8 * k : 8 * k + 8]:
                copy.wait()
            result = coupling(
                w_ref,
                [tall(block_buffer.at[j], 4 * k) for j in range(4)],
                [base_buffer[j, k] for j in range(4)],
            )
            flipped[k + 2] = jnp.where(count[z >> 1] > k + 1, result, 0.0).T
            deal(z, flipped, k + 2, parts)


def finish_kernel(place, *refs):
    row, z = place[0], place[1]
    parts, crown, (diag, near, final) = refs[:4], refs[4:8], refs[8:]
    owner = (z & 1) == (row & 1)
    swap = z >> 1
    for i in range(parts[0].shape[0]):
        here = jnp.where(owner, parts[0][i], parts[1][i])
        there = parts[2][i] + parts[3][i]
        for side, value in ((swap, here), (1 - swap, there)):
            if i == 0:
                diag[side] = value
            else:
                near[side, i - 1] = value
    arrived = crown[1][0] + (crown[2][0] + crown[3][0])
    final[0] = jnp.where(z == 1 + (row & 1), crown[0][0], arrived)


def parent_kernel(place, diag, near0, near1, pair, vt_ref, v_ref, p0, p1, p2, p3, flipped):
    row, z = place[0], place[1]
    size = diag.shape[0]

    @pl.when(z == 1 + (row & 1))
    def _():
        swap = (row & 1) > 0
        near = jnp.concatenate([near0[...], near1[...]], axis=0)

        def order(a, b):
            return jnp.where(swap, b, a), jnp.where(swap, a, b)

        diag_first, diag_second = order(diag[...], pair[0])
        near_first, near_second = order(near, pair[1])
        top = jnp.concatenate([diag_first, near_first], axis=1)
        low = jnp.concatenate([near_second, diag_second], axis=1)
        merged = jnp.concatenate([top, low], axis=0)
        dense = dot3(dot3(vt_ref[...], merged), v_ref[...])
        flipped[0] = eliminate(dense, size)[1].T
        deal(z, flipped, 0, (p0, p1, p2, p3))


def call(kernel, outs, scalars, arrays, us=2, scratch=(), left=0):
    vmem = pl.BlockSpec(memory_space=pltpu.VMEM)
    specs = [pl.BlockSpec(memory_space=pltpu.SMEM)] * len(scalars) + [vmem] * (len(arrays) - left)
    specs += [pl.BlockSpec(memory_space=pl.ANY)] * left
    shapes = [jax.ShapeDtypeStruct(shape, jnp.float32) for shape in outs]
    cost = pl.CostEstimate(flops=us * 10**9, bytes_accessed=us * 10**6, transcendentals=0)
    return pl.pallas_call(
        kernel,
        out_shape=shapes,
        in_specs=specs,
        out_specs=[vmem] * len(outs),
        scratch_shapes=[pltpu.VMEM(x, jnp.float32) if isinstance(x, tuple) else x for x in scratch],
        cost_estimate=cost,
    )(*scalars, *arrays)


def after(values, ready):
    return lax.optimization_barrier((values, ready))[0]


def levels(diag_blocks, near_blocks, cluster_bases, near_ids, near_count, parent_bases):
    clusters, edge, size = cluster_bases.shape
    slots = near_blocks.shape[1]
    skeleton = K
    n_row, n_col = lax.axis_size("row"), lax.axis_size("col")
    assert n_col == 2 * clusters == 4 and n_row & (n_row - 1) == 0
    quarter = skeleton // n_col
    row, column = lax.axis_index("row"), lax.axis_index("col")
    place = jnp.stack([row, column]).astype(jnp.int32)
    both = ("row", "col")
    owned = [(r, z) for r in range(n_row) for z in range(n_col) if z % 2 == r % 2]
    heads = [(r, 1 + r % 2) for r in range(n_row)]

    def to_owner(x, j):
        return lax.ppermute(x, both, [(r * n_col + (z ^ j), r * n_col + z) for r, z in owned])

    def from_owner(x, j):
        return lax.ppermute(x, both, [(r * n_col + z, r * n_col + (z ^ j)) for r, z in owned])

    def from_sibling(x):
        return lax.ppermute(x, both, [((r ^ 1) * n_col + (z ^ 1), r * n_col + z) for r, z in owned])

    def from_neighbour(x):
        return lax.ppermute(x, both, [(r * n_col + (z ^ 1), r * n_col + z) for r, z in heads])

    def from_chip(x):
        return lax.ppermute(x, both, [((r ^ 1) * n_col + z, r * n_col + z) for r, z in heads])

    def from_head(x, j):
        return lax.ppermute(x, both, [(r * n_col + z, r * n_col + (z ^ j)) for r, z in heads])

    def across(x, bit):
        return lax.ppermute(x, "row", [(r, r ^ bit) for r in range(n_row)])

    def gather(x, y):
        got = [x]
        for j, payload in enumerate((x, y, y), 1):
            got.append(to_owner(payload, j))
        return got

    def scatter(parts, send):
        got = [parts[0]]
        for j in range(1, 4):
            got.append(send(parts[j], j))
        return got

    full, half, table = call(
        pack_kernel,
        [(8, edge, edge), (6, edge, edge), (clusters, edge, skeleton)],
        [place],
        [diag_blocks, cluster_bases],
    )
    leaf = gather(full, half)

    bits = [1 << t for t in range(1, n_row.bit_length() - 1)]
    pieces = [table]
    for bit in bits:
        pieces = [jnp.concatenate(pieces, axis=0) if len(pieces) > 1 else table]
        pieces.append(across(pieces[0], bit))

    near = near_blocks.reshape(clusters, slots * 4, edge, edge)
    rest_blocks = (slots - 1) * 4
    v = parent_bases[0]
    split = call(
        split_kernel,
        [(4, edge, edge)] * 2 + [(rest_blocks, edge, edge)] * 2 + [(size, size)],
        [place],
        [near, v],
    )
    swapped = []
    for piece in pieces:
        swapped.append(across(piece, 1))
    n_early = gather(*after((split[0], split[1]), leaf[1:]))
    n_rest = gather(*after((split[2], split[3]), leaf[1:]))
    (skeletons,) = call(skeleton_kernel, [(4, edge, skeleton)], [place], leaf)
    sibling = from_sibling(skeletons)

    w, schur = call(
        leaf_kernel, [(4, skeleton, edge), (skeleton, skeleton)], [place], leaf, 22
    )

    diag_got = from_neighbour(schur)
    top, low, first, pair = call(
        near_first_kernel,
        [(skeleton // 2, skeleton)] * 2 + [(skeleton, skeleton), (2, skeleton, skeleton)],
        [place, near_count],
        [w, sibling, *n_early, schur],
        4,
    )
    top_got = from_neighbour(top)
    low_got = from_neighbour(low)
    pair_got = from_chip(pair)
    chosen = call(
        name_kernel,
        [(slots - 1, edge, skeleton)] * 2,
        [place, near_ids],
        [*after(pieces, first), *swapped],
    )
    named = gather(*chosen)
    crown = call(
        parent_kernel,
        [(1, quarter, skeleton)] * 4,
        [place],
        [diag_got, top_got, low_got, pair_got, split[4], v],
        20,
        [(1, skeleton, skeleton)],
    )
    total = slots + 1
    results = call(
        near_rest_kernel,
        [(total, quarter, skeleton)] * 4,
        [place, near_count],
        [w, schur, first, *n_rest, *named],
        7,
        [
            (total, skeleton, skeleton),
            (4, rest_blocks, edge, edge),
            (4, slots - 1, edge, skeleton),
            pltpu.SemaphoreType.DMA((slots - 1, 4, 2)),
        ],
        8,
    )
    turned = call(
        finish_kernel,
        [(clusters, quarter, skeleton), (clusters, slots, quarter, skeleton), (1, quarter, skeleton)],
        [place],
        scatter(results, from_owner) + scatter(crown, from_head),
    )
    return tuple(jnp.swapaxes(x, -1, -2) for x in turned)


def solution(mesh):
    return jax.shard_map(
        levels,
        mesh=mesh,
        in_specs=(
            P("row", None, "col"),
            P("row", None, None, "col"),
            P("row", "col", None),
            P("row", None),
            P("row"),
            P("row", None, None),
        ),
        out_specs=(P("row", None, "col"), P("row", None, None, "col"), P("row", None, "col")),
        check_vma=False,
    )
```

```python
import jax
import jax.numpy as jnp
from jax import lax
from jax.experimental import pallas as pl
from jax.experimental.pallas import tpu as pltpu
from jax.sharding import PartitionSpec as P


K = 256
PANEL = 8


highest = lax.Precision.HIGHEST


def dot(a, b, left=1, right=0):
    dims = (((left,), (right,)), ((), ()))
    return lax.dot_general(a, b, dims, precision=highest, preferred_element_type=jnp.float32)


def dot3(a, b):
    a_high, b_high = a.astype(jnp.bfloat16), b.astype(jnp.bfloat16)
    a_low = (a - a_high.astype(jnp.float32)).astype(jnp.bfloat16)
    b_low = (b - b_high.astype(jnp.float32)).astype(jnp.bfloat16)

    def product(x, y):
        return jnp.dot(x, y, preferred_element_type=jnp.float32)

    return product(a_high, b_high) + (product(a_high, b_low) + product(a_low, b_high))


def sweep(block):
    size = len(block)
    e = [[block[min(i, j)][max(i, j)] for j in range(size)] for i in range(size)]
    for k in range(size):
        inv = 1.0 / e[k][k]
        t = [e[k][j] * inv for j in range(size)]
        for i in range(size):
            for j in range(i, size):
                if i != k and j != k:
                    e[i][j] = e[i][j] - e[i][k] * t[j]
                    e[j][i] = e[i][j]
        for j in range(size):
            if j != k:
                e[k][j] = e[j][k] = t[j]
        e[k][k] = -inv
    return e


def panel_step(a, lane, sub):
    n = a.shape[0]
    cols = [jnp.broadcast_to(a[:, s : s + 1], (n, n)) for s in range(PANEL)]
    block = [[jnp.broadcast_to(cols[j][i : i + 1], (PANEL, n)) if i <= j else None for j in range(PANEL)] for i in range(PANEL)]
    negated = sweep(block)
    result = jnp.where(lane < PANEL, jnp.where(lane == sub, 1.0, 0.0), a)
    rows = [jnp.broadcast_to(result[t : t + 1], (PANEL, n)) for t in range(PANEL)]
    for s in range(PANEL):
        terms = [negated[s][t] * rows[t] for t in range(PANEL)]
        while len(terms) > 1:
            terms = [terms[i] + terms[i + 1] for i in range(0, len(terms), 2)]
        spread = jnp.concatenate([terms[0]] * (n // PANEL), axis=0)
        top = jnp.where(sub[:PANEL] == s, cols[s][:PANEL] - 1.0, cols[s][:PANEL])
        result = result + jnp.concatenate([top, cols[s][PANEL:]], axis=0) * spread
    return result


def inverse(a):
    n = a.shape[0]
    lane = lax.broadcasted_iota(jnp.int32, (n, n), 1)
    sub = lax.broadcasted_iota(jnp.int32, (n, n), 0)

    def body(_, mat):
        mat = panel_step(mat, lane, sub)
        return pltpu.roll(jnp.concatenate([mat[PANEL:], mat[:PANEL]], axis=0), n - PANEL, 1)

    return lax.fori_loop(0, n // PANEL, body, a)


def solve(corner, right):
    half = corner.shape[0] // 2
    cross, turned = corner[:half, half:], corner[half:, :half]
    first = inverse(corner[:half, :half])
    link, link_turned = dot(first, cross), dot(turned, first)
    second = inverse(corner[half:, half:] - dot(turned, link))
    low = dot(second, right[half:] - dot(link_turned, right[:half]))
    up = dot(first, right[:half]) - dot(link, low)
    return jnp.concatenate([up, low], axis=0)


def eliminate(dense, redundant):
    rr = dense[:redundant, :redundant]
    solved = solve((rr + rr.T) * 0.5, dense[:redundant, redundant:])
    return solved, dense[redundant:, redundant:] - dot(dense[redundant:, :redundant], solved)


def wide(ref, start, count):
    return jnp.concatenate([ref[start + i] for i in range(count)], axis=1)


def leaf_kernel(place, own, near, far2, far3, w_ref, schur_ref):
    z = place[1]
    inner = z & 1
    edge = own.shape[1]
    redundant = 4 * edge - w_ref.shape[1]
    pairs = [jnp.concatenate([own[z ^ m], near[z ^ m]], axis=1) for m in range(4)]
    corner = jnp.concatenate(pairs[:2], axis=0)
    side = jnp.concatenate(pairs[2:], axis=0)
    far = [jnp.concatenate([far2[i], far3[i]], axis=1) for i in (inner, 1 - inner)]
    far = jnp.concatenate(far, axis=0)
    bases = [wide(own, 4, 4), wide(near, 4, 4), wide(far2, 2, 4), wide(far3, 2, 4)]
    u = jnp.concatenate(bases, axis=0)
    ut = u.T
    left = jnp.concatenate([corner, side], axis=0)
    right = jnp.concatenate([side.T, far], axis=0)
    dense = dot3(dot3(ut, jnp.concatenate([left, right], axis=1)), u)
    solved, schur = eliminate(dense, redundant)
    schur_ref[...] = schur
    wt = ut[redundant:] - dot(solved.T, ut[:redundant])
    for m in range(4):
        w_ref[z ^ m] = wt[:, m * edge : (m + 1) * edge]


def pack_kernel(place, diag, bases, full, half, shard):
    edge = bases.shape[1]
    mine = place[1] >> 1
    other = 1 - mine
    for i in range(4):
        lanes = slice(i * edge, (i + 1) * edge)
        full[i] = diag[mine, lanes, :]
        full[4 + i] = bases[mine, :, lanes]
        half[2 + i] = bases[other, :, lanes]
    for i in range(2):
        half[i] = diag[other, pl.ds(pl.multiple_of((2 * mine + i) * edge, edge), edge), :]
    for c in range(bases.shape[0]):
        shard[c] = bases[c, :, bases.shape[2] - shard.shape[2] :]


def skeleton_kernel(place, own, near, far2, far3, out):
    for j, ref in enumerate((own, near, far2, far3)):
        out[j] = wide(ref, ref.shape[0] - 2, 2)


def split_kernel(place, near, v, first_mine, first_other, rest_mine, rest_other, turned):
    mine = place[1] >> 1
    count = first_mine.shape[0]
    turned[...] = v[...].T
    for which, first, rest in ((mine, first_mine, rest_mine), (1 - mine, first_other, rest_other)):
        for i in range(near.shape[1]):
            if i < count:
                first[i] = near[which, i]
            else:
                rest[i - count] = near[which, i]


def name_kernel(place, ids, low0, low1, high0, high1, mine_ref, other_ref):
    row, mine = place[0], place[1] >> 1
    clusters, slots = ids.shape
    for which, out in ((mine, mine_ref), (1 - mine, other_ref)):
        for k in range(1, slots):
            name = ids[which, k]
            apart = lax.div(name, clusters) ^ row
            spot = (apart >> 1) * clusters + lax.rem(name, clusters)
            inner = lax.rem(spot, low0.shape[0])
            late = spot >= low0.shape[0]
            low = jnp.where(late, low1[inner], low0[inner])
            high = jnp.where(late, high1[inner], high0[inner])
            out[k - 1] = jnp.where((apart & 1) > 0, high, low)


def coupling(w_ref, blocks, bases):
    w = jnp.concatenate([w_ref[b] for b in range(4)], axis=1)
    return dot3(w, dot3(jnp.concatenate(blocks, axis=1), jnp.concatenate(bases, axis=0)))


def tall(ref, start):
    return jnp.concatenate([ref[start + i] for i in range(4)], axis=0)


def deal(z, flipped, index, parts):
    quarter = parts[0].shape[1]
    for j, part in enumerate(parts):
        part[index] = flipped[index, pl.ds(pl.multiple_of((z ^ j) * quarter, quarter), quarter), :]


def near_first_kernel(place, count, w_ref, bases, n0, n1, n2, n3, schur, top, low, flipped, pair):
    result = coupling(w_ref, [tall(n, 0) for n in (n0, n1, n2, n3)], [bases[j] for j in range(4)])
    result = jnp.where(count[place[1] >> 1] > 0, result, 0.0)
    half = top.shape[0]
    top[...], low[...] = result[:half], result[half:]
    pair[0], pair[1] = schur[...], result
    flipped[...] = result.T


def owns(column):
    return ((column ^ (column >> 1)) & 1) == 1


def near_rest_kernel(place, count, w_ref, schur, first, *refs):
    z = place[1]
    blocks, named, parts = refs[:4], refs[4:8], refs[8:12]
    flipped, block_buffer, base_buffer, sems = refs[12:]
    total = named[0].shape[0]

    @pl.when(owns(z))
    def _():
        copies = []
        for k in range(total):
            for j in range(4):
                tile = pl.ds(4 * k, 4)
                copies.append(
                    pltpu.make_async_copy(blocks[j].at[tile], block_buffer.at[j, tile], sems.at[k, j, 0])
                )
                copies.append(
                    pltpu.make_async_copy(named[j].at[k], base_buffer.at[j, k], sems.at[k, j, 1])
                )
        for copy in copies:
            copy.start()
        flipped[0] = schur[...]
        flipped[1] = first[...]
        for i in range(2):
            deal(z, flipped, i, parts)
        for k in range(total):
            for copy in copies[8 * k : 8 * k + 8]:
                copy.wait()
            result = coupling(
                w_ref,
                [tall(block_buffer.at[j], 4 * k) for j in range(4)],
                [base_buffer[j, k] for j in range(4)],
            )
            flipped[k + 2] = jnp.where(count[z >> 1] > k + 1, result, 0.0).T
            deal(z, flipped, k + 2, parts)


def finish_kernel(place, *refs):
    row, z = place[0], place[1]
    parts, crown, (diag, near, final) = refs[:4], refs[4:8], refs[8:]
    owner = owns(z)
    swap = z >> 1
    for i in range(parts[0].shape[0]):
        here = jnp.where(owner, parts[0][i], parts[1][i])
        there = parts[2][i] + parts[3][i]
        for side, value in ((swap, here), (1 - swap, there)):
            if i == 0:
                diag[side] = value
            else:
                near[side, i - 1] = value
    arrived = crown[1][0] + (crown[2][0] + crown[3][0])
    final[0] = jnp.where(z == 3 * (row & 1), crown[0][0], arrived)


def parent_kernel(place, diag, near0, near1, pair, vt_ref, v_ref, p0, p1, p2, p3, flipped):
    row, z = place[0], place[1]
    size = diag.shape[0]

    @pl.when(z == 3 * (row & 1))
    def _():
        swap = (row & 1) > 0
        near = jnp.concatenate([near0[...], near1[...]], axis=0)

        def order(a, b):
            return jnp.where(swap, b, a), jnp.where(swap, a, b)

        diag_first, diag_second = order(diag[...], pair[0])
        near_first, near_second = order(near, pair[1])
        top = jnp.concatenate([diag_first, near_first], axis=1)
        low = jnp.concatenate([near_second, diag_second], axis=1)
        merged = jnp.concatenate([top, low], axis=0)
        dense = dot3(dot3(vt_ref[...], merged), v_ref[...])
        flipped[0] = eliminate(dense, size)[1].T
        deal(z, flipped, 0, (p0, p1, p2, p3))


def call(kernel, outs, scalars, arrays, us=2, scratch=(), left=0):
    vmem = pl.BlockSpec(memory_space=pltpu.VMEM)
    specs = [pl.BlockSpec(memory_space=pltpu.SMEM)] * len(scalars) + [vmem] * (len(arrays) - left)
    specs += [pl.BlockSpec(memory_space=pl.ANY)] * left
    shapes = [jax.ShapeDtypeStruct(shape, jnp.float32) for shape in outs]
    cost = pl.CostEstimate(flops=us * 10**9, bytes_accessed=us * 10**6, transcendentals=0)
    return pl.pallas_call(
        kernel,
        out_shape=shapes,
        in_specs=specs,
        out_specs=[vmem] * len(outs),
        scratch_shapes=[pltpu.VMEM(x, jnp.float32) if isinstance(x, tuple) else x for x in scratch],
        cost_estimate=cost,
    )(*scalars, *arrays)


def after(values, ready):
    return lax.optimization_barrier((values, ready))[0]


def levels(diag_blocks, near_blocks, cluster_bases, near_ids, near_count, parent_bases):
    clusters, edge, size = cluster_bases.shape
    slots = near_blocks.shape[1]
    skeleton = K
    n_row, n_col = lax.axis_size("row"), lax.axis_size("col")
    assert n_col == 2 * clusters == 4 and n_row & (n_row - 1) == 0
    quarter = skeleton // n_col
    row, column = lax.axis_index("row"), lax.axis_index("col")
    place = jnp.stack([row, column]).astype(jnp.int32)
    both = ("row", "col")
    owned = [(r, z) for r in range(n_row) for z in range(1, n_col - 1)]
    heads = [(r, (n_col - 1) * (r % 2)) for r in range(n_row)]

    def to_owner(x, j):
        return lax.ppermute(x, both, [(r * n_col + (z ^ j), r * n_col + z) for r, z in owned])

    def from_owner(x, j):
        return lax.ppermute(x, both, [(r * n_col + z, r * n_col + (z ^ j)) for r, z in owned])

    def from_sibling(x):
        return lax.ppermute(x, both, [((r ^ 1) * n_col + z, r * n_col + z) for r, z in owned])

    def from_neighbour(x):
        return lax.ppermute(x, both, [(r * n_col + (z ^ 1), r * n_col + z) for r, z in heads])

    def from_beside(x):
        return lax.ppermute(x, both, [((r ^ 1) * n_col + (z ^ 1), r * n_col + z) for r, z in heads])

    def from_head(x, j):
        return lax.ppermute(x, both, [(r * n_col + z, r * n_col + (z ^ j)) for r, z in heads])

    def across(x, bit):
        return lax.ppermute(x, "row", [(r, r ^ bit) for r in range(n_row)])

    def gather(x, y):
        got = [x]
        for j, payload in enumerate((x, y, y), 1):
            got.append(to_owner(payload, j))
        return got

    def scatter(parts, send):
        got = [parts[0]]
        for j in range(1, 4):
            got.append(send(parts[j], j))
        return got

    full, half, table = call(
        pack_kernel,
        [(8, edge, edge), (6, edge, edge), (clusters, edge, skeleton)],
        [place],
        [diag_blocks, cluster_bases],
    )
    leaf = gather(full, half)

    bits = [1 << t for t in range(1, n_row.bit_length() - 1)]
    pieces = [table]
    for bit in bits:
        pieces = [jnp.concatenate(pieces, axis=0) if len(pieces) > 1 else table]
        pieces.append(across(pieces[0], bit))

    near = near_blocks.reshape(clusters, slots * 4, edge, edge)
    rest_blocks = (slots - 1) * 4
    v = parent_bases[0]
    split = call(
        split_kernel,
        [(4, edge, edge)] * 2 + [(rest_blocks, edge, edge)] * 2 + [(size, size)],
        [place],
        [near, v],
    )
    swapped = []
    for piece in pieces:
        swapped.append(across(piece, 1))
    n_early = gather(*after((split[0], split[1]), leaf[1:]))
    n_rest = gather(*after((split[2], split[3]), leaf[1:]))
    (skeletons,) = call(skeleton_kernel, [(4, edge, skeleton)], [place], leaf)
    sibling = from_sibling(skeletons)

    w, schur = call(
        leaf_kernel, [(4, skeleton, edge), (skeleton, skeleton)], [place], leaf, 22
    )

    diag_got = from_neighbour(schur)
    top, low, first, pair = call(
        near_first_kernel,
        [(skeleton // 2, skeleton)] * 2 + [(skeleton, skeleton), (2, skeleton, skeleton)],
        [place, near_count],
        [w, sibling, *n_early, schur],
        4,
    )
    top_got = from_neighbour(top)
    low_got = from_neighbour(low)
    pair_got = from_beside(pair)
    chosen = call(
        name_kernel,
        [(slots - 1, edge, skeleton)] * 2,
        [place, near_ids],
        [*after(pieces, first), *swapped],
    )
    named = gather(*chosen)
    crown = call(
        parent_kernel,
        [(1, quarter, skeleton)] * 4,
        [place],
        [diag_got, top_got, low_got, pair_got, split[4], v],
        20,
        [(1, skeleton, skeleton)],
    )
    total = slots + 1
    results = call(
        near_rest_kernel,
        [(total, quarter, skeleton)] * 4,
        [place, near_count],
        [w, schur, first, *n_rest, *named],
        7,
        [
            (total, skeleton, skeleton),
            (4, rest_blocks, edge, edge),
            (4, slots - 1, edge, skeleton),
            pltpu.SemaphoreType.DMA((slots - 1, 4, 2)),
        ],
        8,
    )
    turned = call(
        finish_kernel,
        [(clusters, quarter, skeleton), (clusters, slots, quarter, skeleton), (1, quarter, skeleton)],
        [place],
        scatter(results, from_owner) + scatter(crown, from_head),
    )
    return tuple(jnp.swapaxes(x, -1, -2) for x in turned)


def solution(mesh):
    return jax.shard_map(
        levels,
        mesh=mesh,
        in_specs=(
            P("row", None, "col"),
            P("row", None, None, "col"),
            P("row", "col", None),
            P("row", None),
            P("row"),
            P("row", None, None),
        ),
        out_specs=(P("row", None, "col"), P("row", None, None, "col"), P("row", None, "col")),
        check_vma=False,
    )
```

```python
import jax
import jax.numpy as jnp
from jax import lax
from jax.experimental import pallas as pl
from jax.experimental.pallas import tpu as pltpu
from jax.sharding import PartitionSpec as P


K = 256
PANEL = 8


highest = lax.Precision.HIGHEST


def dot(a, b, left=1, right=0):
    dims = (((left,), (right,)), ((), ()))
    return lax.dot_general(a, b, dims, precision=highest, preferred_element_type=jnp.float32)


def dot3(a, b):
    a_high, b_high = a.astype(jnp.bfloat16), b.astype(jnp.bfloat16)
    a_low = (a - a_high.astype(jnp.float32)).astype(jnp.bfloat16)
    b_low = (b - b_high.astype(jnp.float32)).astype(jnp.bfloat16)

    def product(x, y):
        return jnp.dot(x, y, preferred_element_type=jnp.float32)

    return product(a_high, b_high) + (product(a_high, b_low) + product(a_low, b_high))


def sweep(block):
    size = len(block)
    e = [[block[min(i, j)][max(i, j)] for j in range(size)] for i in range(size)]
    for k in range(size):
        inv = 1.0 / e[k][k]
        t = [e[k][j] * inv for j in range(size)]
        for i in range(size):
            for j in range(i, size):
                if i != k and j != k:
                    e[i][j] = e[i][j] - e[i][k] * t[j]
                    e[j][i] = e[i][j]
        for j in range(size):
            if j != k:
                e[k][j] = e[j][k] = t[j]
        e[k][k] = -inv
    return e


def panel_step(a, lane, sub):
    n = a.shape[0]
    cols = [jnp.broadcast_to(a[:, s : s + 1], (n, n)) for s in range(PANEL)]
    block = [[jnp.broadcast_to(cols[j][i : i + 1], (PANEL, n)) if i <= j else None for j in range(PANEL)] for i in range(PANEL)]
    negated = sweep(block)
    result = jnp.where(lane < PANEL, jnp.where(lane == sub, 1.0, 0.0), a)
    rows = [jnp.broadcast_to(result[t : t + 1], (PANEL, n)) for t in range(PANEL)]
    for s in range(PANEL):
        terms = [negated[s][t] * rows[t] for t in range(PANEL)]
        while len(terms) > 1:
            terms = [terms[i] + terms[i + 1] for i in range(0, len(terms), 2)]
        spread = jnp.concatenate([terms[0]] * (n // PANEL), axis=0)
        top = jnp.where(sub[:PANEL] == s, cols[s][:PANEL] - 1.0, cols[s][:PANEL])
        result = result + jnp.concatenate([top, cols[s][PANEL:]], axis=0) * spread
    return result


def inverse(a):
    n = a.shape[0]
    lane = lax.broadcasted_iota(jnp.int32, (n, n), 1)
    sub = lax.broadcasted_iota(jnp.int32, (n, n), 0)

    def body(_, mat):
        mat = panel_step(mat, lane, sub)
        return pltpu.roll(jnp.concatenate([mat[PANEL:], mat[:PANEL]], axis=0), n - PANEL, 1)

    return lax.fori_loop(0, n // PANEL, body, a)


def solve(corner, right):
    half = corner.shape[0] // 2
    cross, turned = corner[:half, half:], corner[half:, :half]
    first = inverse(corner[:half, :half])
    link, link_turned = dot(first, cross), dot(turned, first)
    second = inverse(corner[half:, half:] - dot(turned, link))
    low = dot(second, right[half:] - dot(link_turned, right[:half]))
    up = dot(first, right[:half]) - dot(link, low)
    return jnp.concatenate([up, low], axis=0)


def eliminate(dense, redundant):
    rr = dense[:redundant, :redundant]
    solved = solve((rr + rr.T) * 0.5, dense[:redundant, redundant:])
    return solved, dense[redundant:, redundant:] - dot(dense[redundant:, :redundant], solved)


def wide(ref, start, count):
    return jnp.concatenate([ref[start + i] for i in range(count)], axis=1)


def leaf_kernel(place, own, near, far2, far3, w_ref, schur_ref):
    z = place[1]
    inner = z & 1
    edge = own.shape[1]
    redundant = 4 * edge - w_ref.shape[1]
    pairs = [jnp.concatenate([own[z ^ m], near[z ^ m]], axis=1) for m in range(4)]
    corner = jnp.concatenate(pairs[:2], axis=0)
    side = jnp.concatenate(pairs[2:], axis=0)
    far = [jnp.concatenate([far2[i], far3[i]], axis=1) for i in (inner, 1 - inner)]
    far = jnp.concatenate(far, axis=0)
    bases = [wide(own, 4, 4), wide(near, 4, 4), wide(far2, 2, 4), wide(far3, 2, 4)]
    u = jnp.concatenate(bases, axis=0)
    ut = u.T
    left = jnp.concatenate([corner, side], axis=0)
    right = jnp.concatenate([side.T, far], axis=0)
    dense = dot3(dot3(ut, jnp.concatenate([left, right], axis=1)), u)
    solved, schur = eliminate(dense, redundant)
    schur_ref[...] = schur
    wt = ut[redundant:] - dot(solved.T, ut[:redundant])
    for m in range(4):
        w_ref[z ^ m] = wt[:, m * edge : (m + 1) * edge]


def pack_kernel(place, diag, bases, full, half, shard):
    edge = bases.shape[1]
    mine = place[1] >> 1
    other = 1 - mine
    for i in range(4):
        lanes = slice(i * edge, (i + 1) * edge)
        full[i] = diag[mine, lanes, :]
        full[4 + i] = bases[mine, :, lanes]
        half[2 + i] = bases[other, :, lanes]
    for i in range(2):
        half[i] = diag[other, pl.ds(pl.multiple_of((2 * mine + i) * edge, edge), edge), :]
    for c in range(bases.shape[0]):
        shard[c] = bases[c, :, bases.shape[2] - shard.shape[2] :]


def skeleton_kernel(place, own, near, far2, far3, out):
    for j, ref in enumerate((own, near, far2, far3)):
        out[j] = wide(ref, ref.shape[0] - 2, 2)


def split_kernel(place, near, v, first_mine, first_other, rest_mine, rest_other, turned):
    mine = place[1] >> 1
    count = first_mine.shape[0]
    turned[...] = v[...].T
    for which, first, rest in ((mine, first_mine, rest_mine), (1 - mine, first_other, rest_other)):
        for i in range(near.shape[1]):
            if i < count:
                first[i] = near[which, i]
            else:
                rest[i - count] = near[which, i]


def name_kernel(place, ids, low0, low1, high0, high1, _, __, rest_mine, rest_other, found, sems):
    row, mine = place[0], place[1] >> 1
    clusters, slots = ids.shape
    edge, count = found.shape[2], found.shape[1]
    copies = []
    for side, (which, rest) in enumerate(((mine, rest_mine), (1 - mine, rest_other))):
        for k in range(1, slots):
            name = ids[which, k]
            apart = lax.div(name, clusters) ^ row
            spot = (apart >> 1) * clusters + lax.rem(name, clusters)
            inner = lax.rem(spot, low0.shape[0])
            late = spot >= low0.shape[0]
            low = jnp.where(late, low1[inner], low0[inner])
            high = jnp.where(late, high1[inner], high0[inner])
            base = jnp.where((apart & 1) > 0, high, low)
            for b in range(2):
                found[side, 2 * (k - 1) + b] = base[:, b * edge : (b + 1) * edge]
        copies.append(
            pltpu.make_async_copy(
                found.at[side], rest.at[pl.ds(rest.shape[0] - count, count)], sems.at[side]
            )
        )
    for copy in copies:
        copy.start()
    for copy in copies:
        copy.wait()


def coupling(w_ref, blocks, bases):
    w = jnp.concatenate([w_ref[b] for b in range(4)], axis=1)
    return dot3(w, dot3(jnp.concatenate(blocks, axis=1), jnp.concatenate(bases, axis=0)))


def tall(ref, start):
    return jnp.concatenate([ref[start + i] for i in range(4)], axis=0)


def deal(z, flipped, index, parts):
    quarter = parts[0].shape[1]
    for j, part in enumerate(parts):
        part[index] = flipped[index, pl.ds(pl.multiple_of((z ^ j) * quarter, quarter), quarter), :]


def near_first_kernel(place, count, w_ref, bases, n0, n1, n2, n3, schur, top, low, flipped, pair):
    result = coupling(w_ref, [tall(n, 0) for n in (n0, n1, n2, n3)], [bases[j] for j in range(4)])
    result = jnp.where(count[place[1] >> 1] > 0, result, 0.0)
    half = top.shape[0]
    top[...], low[...] = result[:half], result[half:]
    pair[0], pair[1] = schur[...], result
    flipped[...] = result.T


def owns(column):
    return ((column ^ (column >> 1)) & 1) == 1


def near_rest_kernel(place, count, w_ref, schur, first, *refs):
    z = place[1]
    blocks, parts = refs[:4], refs[4:8]
    flipped, block_buffer, base_buffer, sems = refs[8:]
    total = blocks[0].shape[0] // 6

    @pl.when(owns(z))
    def _():
        copies = []
        for k in range(total):
            for j in range(4):
                tile = pl.ds(4 * k, 4)
                copies.append(
                    pltpu.make_async_copy(blocks[j].at[tile], block_buffer.at[j, tile], sems.at[k, j, 0])
                )
                pair = pl.ds(2 * k, 2)
                base = blocks[j].at[pl.ds(4 * total + 2 * k, 2)]
                copies.append(
                    pltpu.make_async_copy(base, base_buffer.at[j, pair], sems.at[k, j, 1])
                )
        for copy in copies:
            copy.start()
        flipped[0] = schur[...]
        flipped[1] = first[...]
        for i in range(2):
            deal(z, flipped, i, parts)
        for k in range(total):
            for copy in copies[8 * k : 8 * k + 8]:
                copy.wait()
            result = coupling(
                w_ref,
                [tall(block_buffer.at[j], 4 * k) for j in range(4)],
                [wide(base_buffer.at[j], 2 * k, 2) for j in range(4)],
            )
            flipped[k + 2] = jnp.where(count[z >> 1] > k + 1, result, 0.0).T
            deal(z, flipped, k + 2, parts)


def finish_kernel(place, *refs):
    row, z = place[0], place[1]
    parts, crown, (diag, near, final) = refs[:4], refs[4:8], refs[8:]
    owner = owns(z)
    swap = z >> 1
    for i in range(parts[0].shape[0]):
        here = jnp.where(owner, parts[0][i], parts[1][i])
        there = parts[2][i] + parts[3][i]
        for side, value in ((swap, here), (1 - swap, there)):
            if i == 0:
                diag[side] = value
            else:
                near[side, i - 1] = value
    arrived = crown[1][0] + (crown[2][0] + crown[3][0])
    final[0] = jnp.where(z == 3 * (row & 1), crown[0][0], arrived)


def parent_kernel(place, diag, near0, near1, pair, vt_ref, v_ref, p0, p1, p2, p3, flipped):
    row, z = place[0], place[1]
    size = diag.shape[0]

    @pl.when(z == 3 * (row & 1))
    def _():
        swap = (row & 1) > 0
        near = jnp.concatenate([near0[...], near1[...]], axis=0)

        def order(a, b):
            return jnp.where(swap, b, a), jnp.where(swap, a, b)

        diag_first, diag_second = order(diag[...], pair[0])
        near_first, near_second = order(near, pair[1])
        top = jnp.concatenate([diag_first, near_first], axis=1)
        low = jnp.concatenate([near_second, diag_second], axis=1)
        merged = jnp.concatenate([top, low], axis=0)
        dense = dot3(dot3(vt_ref[...], merged), v_ref[...])
        flipped[0] = eliminate(dense, size)[1].T
        deal(z, flipped, 0, (p0, p1, p2, p3))


def call(kernel, outs, scalars, arrays, us=2, scratch=(), left=0):
    vmem = pl.BlockSpec(memory_space=pltpu.VMEM)
    specs = [pl.BlockSpec(memory_space=pltpu.SMEM)] * len(scalars) + [vmem] * (len(arrays) - left)
    specs += [pl.BlockSpec(memory_space=pl.ANY)] * left
    shapes = [jax.ShapeDtypeStruct(shape, jnp.float32) for shape in outs]
    cost = pl.CostEstimate(flops=us * 10**9, bytes_accessed=us * 10**6, transcendentals=0)
    return pl.pallas_call(
        kernel,
        out_shape=shapes,
        in_specs=specs,
        out_specs=[vmem] * len(outs),
        scratch_shapes=[pltpu.VMEM(x, jnp.float32) if isinstance(x, tuple) else x for x in scratch],
        cost_estimate=cost,
    )(*scalars, *arrays)


def after(values, ready):
    return lax.optimization_barrier((values, ready))[0]


def levels(diag_blocks, near_blocks, cluster_bases, near_ids, near_count, parent_bases):
    clusters, edge, size = cluster_bases.shape
    slots = near_blocks.shape[1]
    skeleton = K
    n_row, n_col = lax.axis_size("row"), lax.axis_size("col")
    assert n_col == 2 * clusters == 4 and n_row & (n_row - 1) == 0
    quarter = skeleton // n_col
    row, column = lax.axis_index("row"), lax.axis_index("col")
    place = jnp.stack([row, column]).astype(jnp.int32)
    both = ("row", "col")
    owned = [(r, z) for r in range(n_row) for z in range(1, n_col - 1)]
    heads = [(r, (n_col - 1) * (r % 2)) for r in range(n_row)]

    def to_owner(x, j):
        return lax.ppermute(x, both, [(r * n_col + (z ^ j), r * n_col + z) for r, z in owned])

    def from_owner(x, j):
        return lax.ppermute(x, both, [(r * n_col + z, r * n_col + (z ^ j)) for r, z in owned])

    def from_sibling(x):
        return lax.ppermute(x, both, [((r ^ 1) * n_col + z, r * n_col + z) for r, z in owned])

    def from_neighbour(x):
        return lax.ppermute(x, both, [(r * n_col + (z ^ 1), r * n_col + z) for r, z in heads])

    def from_beside(x):
        return lax.ppermute(x, both, [((r ^ 1) * n_col + (z ^ 1), r * n_col + z) for r, z in heads])

    def from_head(x, j):
        return lax.ppermute(x, both, [(r * n_col + z, r * n_col + (z ^ j)) for r, z in heads])

    def across(x, bit):
        return lax.ppermute(x, "row", [(r, r ^ bit) for r in range(n_row)])

    def gather(x, y):
        got = [x]
        for j, payload in enumerate((x, y, y), 1):
            got.append(to_owner(payload, j))
        return got

    def scatter(parts, send):
        got = [parts[0]]
        for j in range(1, 4):
            got.append(send(parts[j], j))
        return got

    full, half, table = call(
        pack_kernel,
        [(8, edge, edge), (6, edge, edge), (clusters, edge, skeleton)],
        [place],
        [diag_blocks, cluster_bases],
    )
    leaf = gather(full, half)

    bits = [1 << t for t in range(1, n_row.bit_length() - 1)]
    pieces = [table]
    for bit in bits:
        pieces = [jnp.concatenate(pieces, axis=0) if len(pieces) > 1 else table]
        pieces.append(across(pieces[0], bit))

    near = near_blocks.reshape(clusters, slots * 4, edge, edge)
    rest_blocks = (slots - 1) * 6
    v = parent_bases[0]
    split = call(
        split_kernel,
        [(4, edge, edge)] * 2 + [(rest_blocks, edge, edge)] * 2 + [(size, size)],
        [place],
        [near, v],
    )
    swapped = []
    for piece in pieces:
        swapped.append(across(piece, 1))
    n_early = gather(*after((split[0], split[1]), leaf[1:]))
    scalar, vmem = pl.BlockSpec(memory_space=pltpu.SMEM), pl.BlockSpec(memory_space=pltpu.VMEM)
    anywhere = pl.BlockSpec(memory_space=pl.ANY)
    rest = pl.pallas_call(
        name_kernel,
        out_shape=[jax.ShapeDtypeStruct((rest_blocks, edge, edge), jnp.float32)] * 2,
        in_specs=[scalar] * 2 + [vmem] * 4 + [anywhere] * 2,
        out_specs=[anywhere] * 2,
        scratch_shapes=[
            pltpu.VMEM((2, (slots - 1) * 2, edge, edge), jnp.float32),
            pltpu.SemaphoreType.DMA((2,)),
        ],
        input_output_aliases={6: 0, 7: 1},
    )(place, near_ids, *pieces, *swapped, split[2], split[3])
    n_rest = gather(*after(rest, leaf[1:]))
    (skeletons,) = call(skeleton_kernel, [(4, edge, skeleton)], [place], leaf)
    sibling = from_sibling(skeletons)

    w, schur = call(
        leaf_kernel, [(4, skeleton, edge), (skeleton, skeleton)], [place], leaf, 22
    )

    diag_got = from_neighbour(schur)
    top, low, first, pair = call(
        near_first_kernel,
        [(skeleton // 2, skeleton)] * 2 + [(skeleton, skeleton), (2, skeleton, skeleton)],
        [place, near_count],
        [w, sibling, *n_early, schur],
        4,
    )
    top_got = from_neighbour(top)
    low_got = from_neighbour(low)
    pair_got = from_beside(pair)
    crown = call(
        parent_kernel,
        [(1, quarter, skeleton)] * 4,
        [place],
        [diag_got, top_got, low_got, pair_got, split[4], v],
        20,
        [(1, skeleton, skeleton)],
    )
    total = slots + 1
    results = call(
        near_rest_kernel,
        [(total, quarter, skeleton)] * 4,
        [place, near_count],
        [w, schur, first, *n_rest],
        7,
        [
            (total, skeleton, skeleton),
            (4, (slots - 1) * 4, edge, edge),
            (4, (slots - 1) * 2, edge, edge),
            pltpu.SemaphoreType.DMA((slots - 1, 4, 2)),
        ],
        4,
    )
    turned = call(
        finish_kernel,
        [(clusters, quarter, skeleton), (clusters, slots, quarter, skeleton), (1, quarter, skeleton)],
        [place],
        scatter(results, from_owner) + scatter(crown, from_head),
    )
    return tuple(jnp.swapaxes(x, -1, -2) for x in turned)


def solution(mesh):
    return jax.shard_map(
        levels,
        mesh=mesh,
        in_specs=(
            P("row", None, "col"),
            P("row", None, None, "col"),
            P("row", "col", None),
            P("row", None),
            P("row"),
            P("row", None, None),
        ),
        out_specs=(P("row", None, "col"), P("row", None, None, "col"), P("row", None, "col")),
        check_vma=False,
    )
```

```python
import jax
import jax.numpy as jnp
from jax import lax
from jax.experimental import pallas as pl
from jax.experimental.pallas import tpu as pltpu
from jax.sharding import PartitionSpec as P


K = 256
PANEL = 8


highest = lax.Precision.HIGHEST


def dot(a, b, left=1, right=0):
    dims = (((left,), (right,)), ((), ()))
    return lax.dot_general(a, b, dims, precision=highest, preferred_element_type=jnp.float32)


def dot3(a, b):
    a_high, b_high = a.astype(jnp.bfloat16), b.astype(jnp.bfloat16)
    a_low = (a - a_high.astype(jnp.float32)).astype(jnp.bfloat16)
    b_low = (b - b_high.astype(jnp.float32)).astype(jnp.bfloat16)

    def product(x, y):
        return jnp.dot(x, y, preferred_element_type=jnp.float32)

    return product(a_high, b_high) + (product(a_high, b_low) + product(a_low, b_high))


def sweep(block):
    size = len(block)
    e = [[block[min(i, j)][max(i, j)] for j in range(size)] for i in range(size)]
    for k in range(size):
        inv = 1.0 / e[k][k]
        t = [e[k][j] * inv for j in range(size)]
        for i in range(size):
            for j in range(i, size):
                if i != k and j != k:
                    e[i][j] = e[i][j] - e[i][k] * t[j]
                    e[j][i] = e[i][j]
        for j in range(size):
            if j != k:
                e[k][j] = e[j][k] = t[j]
        e[k][k] = -inv
    return e


def panel_step(a, lane, sub):
    n = a.shape[0]
    cols = [jnp.broadcast_to(a[:, s : s + 1], (n, n)) for s in range(PANEL)]
    block = [[jnp.broadcast_to(cols[j][i : i + 1], (PANEL, n)) if i <= j else None for j in range(PANEL)] for i in range(PANEL)]
    negated = sweep(block)
    result = jnp.where(lane < PANEL, jnp.where(lane == sub, 1.0, 0.0), a)
    rows = [jnp.broadcast_to(result[t : t + 1], (PANEL, n)) for t in range(PANEL)]
    for s in range(PANEL):
        terms = [negated[s][t] * rows[t] for t in range(PANEL)]
        while len(terms) > 1:
            terms = [terms[i] + terms[i + 1] for i in range(0, len(terms), 2)]
        spread = jnp.concatenate([terms[0]] * (n // PANEL), axis=0)
        top = jnp.where(sub[:PANEL] == s, cols[s][:PANEL] - 1.0, cols[s][:PANEL])
        result = result + jnp.concatenate([top, cols[s][PANEL:]], axis=0) * spread
    return result


def inverse(a):
    n = a.shape[0]
    lane = lax.broadcasted_iota(jnp.int32, (n, n), 1)
    sub = lax.broadcasted_iota(jnp.int32, (n, n), 0)

    def body(_, mat):
        mat = panel_step(mat, lane, sub)
        return pltpu.roll(jnp.concatenate([mat[PANEL:], mat[:PANEL]], axis=0), n - PANEL, 1)

    return lax.fori_loop(0, n // PANEL, body, a)


def solve(corner, right):
    half = corner.shape[0] // 2
    cross, turned = corner[:half, half:], corner[half:, :half]
    first = inverse(corner[:half, :half])
    link, link_turned = dot(first, cross), dot(turned, first)
    second = inverse(corner[half:, half:] - dot(turned, link))
    low = dot(second, right[half:] - dot(link_turned, right[:half]))
    up = dot(first, right[:half]) - dot(link, low)
    return jnp.concatenate([up, low], axis=0)


def eliminate(dense, redundant):
    rr = dense[:redundant, :redundant]
    solved = solve((rr + rr.T) * 0.5, dense[:redundant, redundant:])
    return solved, dense[redundant:, redundant:] - dot3(dense[redundant:, :redundant], solved)


def wide(ref, start, count):
    return jnp.concatenate([ref[start + i] for i in range(count)], axis=1)


def leaf_kernel(place, own, near, far2, far3, w_ref, schur_ref):
    @pl.when(owns(place[1]))
    def _():
        z = place[1]
        inner = z & 1
        edge = own.shape[1]
        redundant = 4 * edge - w_ref.shape[1]
        pairs = [jnp.concatenate([own[z ^ m], near[z ^ m]], axis=1) for m in range(4)]
        corner = jnp.concatenate(pairs[:2], axis=0)
        side = jnp.concatenate(pairs[2:], axis=0)
        far = [jnp.concatenate([far2[i], far3[i]], axis=1) for i in (inner, 1 - inner)]
        far = jnp.concatenate(far, axis=0)
        bases = [wide(own, 4, 4), wide(near, 4, 4), wide(far2, 2, 4), wide(far3, 2, 4)]
        u = jnp.concatenate(bases, axis=0)
        ut = u.T
        left = jnp.concatenate([corner, side], axis=0)
        right = jnp.concatenate([side.T, far], axis=0)
        dense = dot3(dot3(ut, jnp.concatenate([left, right], axis=1)), u)
        solved, schur = eliminate(dense, redundant)
        schur_ref[...] = schur
        wt = ut[redundant:] - dot3(solved.T, ut[:redundant])
        for m in range(4):
            w_ref[z ^ m] = wt[:, m * edge : (m + 1) * edge]


def pack_kernel(place, diag, bases, full, half, shard):
    edge = bases.shape[1]
    mine = place[1] >> 1
    other = 1 - mine
    for i in range(4):
        lanes = slice(i * edge, (i + 1) * edge)
        full[i] = diag[mine, lanes, :]
        full[4 + i] = bases[mine, :, lanes]
        half[2 + i] = bases[other, :, lanes]
    for i in range(2):
        half[i] = diag[other, pl.ds(pl.multiple_of((2 * mine + i) * edge, edge), edge), :]
    for c in range(bases.shape[0]):
        shard[c] = bases[c, :, bases.shape[2] - shard.shape[2] :]


def skeleton_kernel(place, own, near, far2, far3, out):
    for j, ref in enumerate((own, near, far2, far3)):
        out[j] = wide(ref, ref.shape[0] - 2, 2)


def split_kernel(place, near, v, first_mine, first_other, rest_mine, rest_other, turned):
    mine = place[1] >> 1
    count = first_mine.shape[0]
    turned[...] = v[...].T
    for which, first, rest in ((mine, first_mine, rest_mine), (1 - mine, first_other, rest_other)):
        for i in range(near.shape[1]):
            if i < count:
                first[i] = near[which, i]
            else:
                rest[i - count] = near[which, i]


def name_kernel(place, ids, low0, low1, high0, high1, _, __, rest_mine, rest_other, found, sems):
    row, mine = place[0], place[1] >> 1
    clusters, slots = ids.shape
    edge, count = found.shape[2], found.shape[1]
    copies = []
    for side, (which, rest) in enumerate(((mine, rest_mine), (1 - mine, rest_other))):
        for k in range(1, slots):
            name = ids[which, k]
            apart = lax.div(name, clusters) ^ row
            spot = (apart >> 1) * clusters + lax.rem(name, clusters)
            inner = lax.rem(spot, low0.shape[0])
            late = spot >= low0.shape[0]
            low = jnp.where(late, low1[inner], low0[inner])
            high = jnp.where(late, high1[inner], high0[inner])
            base = jnp.where((apart & 1) > 0, high, low)
            for b in range(2):
                found[side, 2 * (k - 1) + b] = base[:, b * edge : (b + 1) * edge]
        copies.append(
            pltpu.make_async_copy(
                found.at[side], rest.at[pl.ds(rest.shape[0] - count, count)], sems.at[side]
            )
        )
    for copy in copies:
        copy.start()
    for copy in copies:
        copy.wait()


def coupling(w_ref, blocks, bases):
    w = jnp.concatenate([w_ref[b] for b in range(4)], axis=1)
    return dot3(w, dot3(jnp.concatenate(blocks, axis=1), jnp.concatenate(bases, axis=0)))


def tall(ref, start):
    return jnp.concatenate([ref[start + i] for i in range(4)], axis=0)


def deal(z, flipped, index, parts):
    quarter = parts[0].shape[1]
    for j, part in enumerate(parts):
        part[index] = flipped[index, pl.ds(pl.multiple_of((z ^ j) * quarter, quarter), quarter), :]


def near_first_kernel(place, count, w_ref, bases, n0, n1, n2, n3, schur, top, low, flipped, pair):
    @pl.when(owns(place[1]))
    def _():
        result = coupling(w_ref, [tall(n, 0) for n in (n0, n1, n2, n3)], [bases[j] for j in range(4)])
        result = jnp.where(count[place[1] >> 1] > 0, result, 0.0)
        half = top.shape[0]
        top[...], low[...] = result[:half], result[half:]
        pair[0], pair[1] = schur[...], result
        flipped[...] = result.T


def owns(column):
    return ((column ^ (column >> 1)) & 1) == 1


def near_rest_kernel(place, count, w_ref, schur, first, *refs):
    z = place[1]
    blocks, parts = refs[:4], refs[4:8]
    flipped, block_buffer, base_buffer, sems = refs[8:]
    total = blocks[0].shape[0] // 6

    @pl.when(owns(z))
    def _():
        copies = []
        for k in range(total):
            for j in range(4):
                tile = pl.ds(4 * k, 4)
                copies.append(
                    pltpu.make_async_copy(blocks[j].at[tile], block_buffer.at[j, tile], sems.at[k, j, 0])
                )
                pair = pl.ds(2 * k, 2)
                base = blocks[j].at[pl.ds(4 * total + 2 * k, 2)]
                copies.append(
                    pltpu.make_async_copy(base, base_buffer.at[j, pair], sems.at[k, j, 1])
                )
        for copy in copies:
            copy.start()
        flipped[0] = schur[...]
        flipped[1] = first[...]
        for i in range(2):
            deal(z, flipped, i, parts)
        for k in range(total):
            for copy in copies[8 * k : 8 * k + 8]:
                copy.wait()
            result = coupling(
                w_ref,
                [tall(block_buffer.at[j], 4 * k) for j in range(4)],
                [wide(base_buffer.at[j], 2 * k, 2) for j in range(4)],
            )
            flipped[k + 2] = jnp.where(count[z >> 1] > k + 1, result, 0.0).T
            deal(z, flipped, k + 2, parts)


def finish_kernel(place, *refs):
    row, z = place[0], place[1]
    parts, crown, (diag, near, final) = refs[:4], refs[4:8], refs[8:]
    owner = owns(z)
    swap = z >> 1
    for i in range(parts[0].shape[0]):
        here = jnp.where(owner, parts[0][i], parts[1][i])
        there = parts[2][i] + parts[3][i]
        for side, value in ((swap, here), (1 - swap, there)):
            if i == 0:
                diag[side] = value
            else:
                near[side, i - 1] = value
    arrived = crown[1][0] + (crown[2][0] + crown[3][0])
    final[0] = jnp.where(z == 3 * (row & 1), crown[0][0], arrived)


def parent_kernel(place, diag, near0, near1, pair, vt_ref, v_ref, p0, p1, p2, p3, flipped):
    row, z = place[0], place[1]
    size = diag.shape[0]

    @pl.when(z == 3 * (row & 1))
    def _():
        swap = (row & 1) > 0
        near = jnp.concatenate([near0[...], near1[...]], axis=0)

        def order(a, b):
            return jnp.where(swap, b, a), jnp.where(swap, a, b)

        diag_first, diag_second = order(diag[...], pair[0])
        near_first, near_second = order(near, pair[1])
        top = jnp.concatenate([diag_first, near_first], axis=1)
        low = jnp.concatenate([near_second, diag_second], axis=1)
        merged = jnp.concatenate([top, low], axis=0)
        dense = dot3(dot3(vt_ref[...], merged), v_ref[...])
        flipped[0] = eliminate(dense, size)[1].T
        deal(z, flipped, 0, (p0, p1, p2, p3))


def call(kernel, outs, scalars, arrays, us=2, scratch=(), left=0):
    vmem = pl.BlockSpec(memory_space=pltpu.VMEM)
    specs = [pl.BlockSpec(memory_space=pltpu.SMEM)] * len(scalars) + [vmem] * (len(arrays) - left)
    specs += [pl.BlockSpec(memory_space=pl.ANY)] * left
    shapes = [jax.ShapeDtypeStruct(shape, jnp.float32) for shape in outs]
    cost = pl.CostEstimate(flops=us * 10**9, bytes_accessed=us * 10**6, transcendentals=0)
    return pl.pallas_call(
        kernel,
        out_shape=shapes,
        in_specs=specs,
        out_specs=[vmem] * len(outs),
        scratch_shapes=[pltpu.VMEM(x, jnp.float32) if isinstance(x, tuple) else x for x in scratch],
        cost_estimate=cost,
    )(*scalars, *arrays)


def after(values, ready):
    return lax.optimization_barrier((values, ready))[0]


def levels(diag_blocks, near_blocks, cluster_bases, near_ids, near_count, parent_bases):
    clusters, edge, size = cluster_bases.shape
    slots = near_blocks.shape[1]
    skeleton = K
    n_row, n_col = lax.axis_size("row"), lax.axis_size("col")
    assert n_col == 2 * clusters == 4 and n_row & (n_row - 1) == 0
    quarter = skeleton // n_col
    row, column = lax.axis_index("row"), lax.axis_index("col")
    place = jnp.stack([row, column]).astype(jnp.int32)
    both = ("row", "col")
    owned = [(r, z) for r in range(n_row) for z in range(1, n_col - 1)]
    heads = [(r, (n_col - 1) * (r % 2)) for r in range(n_row)]

    def to_owner(x, j):
        return lax.ppermute(x, both, [(r * n_col + (z ^ j), r * n_col + z) for r, z in owned])

    def from_owner(x, j):
        return lax.ppermute(x, both, [(r * n_col + z, r * n_col + (z ^ j)) for r, z in owned])

    def from_sibling(x):
        return lax.ppermute(x, both, [((r ^ 1) * n_col + z, r * n_col + z) for r, z in owned])

    def from_neighbour(x):
        return lax.ppermute(x, both, [(r * n_col + (z ^ 1), r * n_col + z) for r, z in heads])

    def from_beside(x):
        return lax.ppermute(x, both, [((r ^ 1) * n_col + (z ^ 1), r * n_col + z) for r, z in heads])

    def from_head(x, j):
        return lax.ppermute(x, both, [(r * n_col + z, r * n_col + (z ^ j)) for r, z in heads])

    def across(x, bit):
        return lax.ppermute(x, "row", [(r, r ^ bit) for r in range(n_row)])

    def gather(x, y):
        got = [x]
        for j, payload in enumerate((x, y, y), 1):
            got.append(to_owner(payload, j))
        return got

    def scatter(parts, send):
        got = [parts[0]]
        for j in range(1, 4):
            got.append(send(parts[j], j))
        return got

    full, half, table = call(
        pack_kernel,
        [(8, edge, edge), (6, edge, edge), (clusters, edge, skeleton)],
        [place],
        [diag_blocks, cluster_bases],
    )
    leaf = gather(full, half)

    bits = [1 << t for t in range(1, n_row.bit_length() - 1)]
    pieces = [table]
    for bit in bits:
        pieces = [jnp.concatenate(pieces, axis=0) if len(pieces) > 1 else table]
        pieces.append(across(pieces[0], bit))

    near = near_blocks.reshape(clusters, slots * 4, edge, edge)
    rest_blocks = (slots - 1) * 6
    v = parent_bases[0]
    split = call(
        split_kernel,
        [(4, edge, edge)] * 2 + [(rest_blocks, edge, edge)] * 2 + [(size, size)],
        [place],
        [near, v],
    )
    swapped = []
    for piece in pieces:
        swapped.append(across(piece, 1))
    n_early = gather(*after((split[0], split[1]), leaf[1:]))
    scalar, vmem = pl.BlockSpec(memory_space=pltpu.SMEM), pl.BlockSpec(memory_space=pltpu.VMEM)
    anywhere = pl.BlockSpec(memory_space=pl.ANY)
    rest = pl.pallas_call(
        name_kernel,
        out_shape=[jax.ShapeDtypeStruct((rest_blocks, edge, edge), jnp.float32)] * 2,
        in_specs=[scalar] * 2 + [vmem] * 4 + [anywhere] * 2,
        out_specs=[anywhere] * 2,
        scratch_shapes=[
            pltpu.VMEM((2, (slots - 1) * 2, edge, edge), jnp.float32),
            pltpu.SemaphoreType.DMA((2,)),
        ],
        input_output_aliases={6: 0, 7: 1},
    )(place, near_ids, *pieces, *swapped, split[2], split[3])
    n_rest = gather(*after(rest, leaf[1:]))
    (skeletons,) = call(skeleton_kernel, [(4, edge, skeleton)], [place], leaf)
    sibling = from_sibling(skeletons)

    w, schur = call(
        leaf_kernel, [(4, skeleton, edge), (skeleton, skeleton)], [place], leaf, 22
    )

    diag_got = from_neighbour(schur)
    top, low, first, pair = call(
        near_first_kernel,
        [(skeleton // 2, skeleton)] * 2 + [(skeleton, skeleton), (2, skeleton, skeleton)],
        [place, near_count],
        [w, sibling, *n_early, schur],
        4,
    )
    top_got = from_neighbour(top)
    low_got = from_neighbour(low)
    pair_got = from_beside(pair)
    crown = call(
        parent_kernel,
        [(1, quarter, skeleton)] * 4,
        [place],
        [diag_got, top_got, low_got, pair_got, split[4], v],
        20,
        [(1, skeleton, skeleton)],
    )
    total = slots + 1
    results = call(
        near_rest_kernel,
        [(total, quarter, skeleton)] * 4,
        [place, near_count],
        [w, schur, first, *n_rest],
        7,
        [
            (total, skeleton, skeleton),
            (4, (slots - 1) * 4, edge, edge),
            (4, (slots - 1) * 2, edge, edge),
            pltpu.SemaphoreType.DMA((slots - 1, 4, 2)),
        ],
        4,
    )
    turned = call(
        finish_kernel,
        [(clusters, quarter, skeleton), (clusters, slots, quarter, skeleton), (1, quarter, skeleton)],
        [place],
        scatter(results, from_owner) + scatter(crown, from_head),
    )
    return tuple(jnp.swapaxes(x, -1, -2) for x in turned)


def solution(mesh):
    return jax.shard_map(
        levels,
        mesh=mesh,
        in_specs=(
            P("row", None, "col"),
            P("row", None, None, "col"),
            P("row", "col", None),
            P("row", None),
            P("row"),
            P("row", None, None),
        ),
        out_specs=(P("row", None, "col"), P("row", None, None, "col"), P("row", None, "col")),
        check_vma=False,
    )
```
